32 devices in a mesh: pairs: 8 (over z, x), grp: 4 (over y, core).
Axes of the slice: x: 2, y: 2, z: 4, core: 2. Of those that a mesh axis runs over, the one named last changes fastest.
Arguments:
- coefficients: bfloat16 [128, 512, 128], P('pairs', 'grp'), may hold values from -0.4140625 to 0.4140625
- domain: int32 [128, 512], P('pairs', 'grp'), may hold values from 0 to 767, as said below
- coupling_owner: int32 [128, 8], P('pairs'), may hold values from 0 to 7, all different within a row; in each aligned block of 16 rows (0 to 15, 16 to 31, ...) at most 16 rows name the same one
- coupling_slot: int32 [128, 8], P('pairs'), may hold values from 0 to 15
- coupling_fock: float32 [128, 8], P('pairs'), may hold values from -0.5 to 0.5
- exchange_integrals: float32 [128, 128, 128], P('pairs'), may hold values from -6 to 6
- pno_energy: float32 [128, 128], P('pairs'), may hold values from 0.3 to 3
- pair_shift: float32 [128], P('pairs'), may hold values from 0.4 to 2
- amplitudes_start: float32 [128, 128, 128], P('pairs'), may hold values from -1.8 to 1.8
Outputs:
- amplitudes: float32 [128, 128, 128], P('pairs')
The draws below stay inside these ranges and needn't reach their ends.
Inputs may be any that keep to these rules, and one draw needn't show every extreme that they name: `coupling_owner`: each row names different indices. Among the 16 rows of one index of pairs no value is named more than 16 times, a bound that some block reaches. `domain`: for each pair and each g from 0 to 3, the entries g * 128 to (g + 1) * 128 - 1 are distinct numbers from g * 192 to (g + 1) * 192 - 1.
All inputs are finite; a program needn't handle non-finite values.
Results may differ from the reference program's by a relative error of at most 0.0025.
Values may be sent and summed in bfloat16 or wider, within the bound.
A program may use at most 128 MiB of HBM per device.

```python
import math
import jax
import jax.numpy as jnp
import numpy as np
from jax import lax

NPNO = 128
DOM = 512
NB = 192
NCPL = 8
ITERS = 2
PAIRS_DEV = 16
NPAIRS = 128
DOMB = 128
MOST = 16
N_PAIRS = 8


def draw_domain(key, part):
    block_count = DOM // DOMB
    pair_keys = jax.random.split(key, NPAIRS * block_count)
    chosen = jax.vmap(lambda item_key: jax.random.permutation(item_key, NB)[:DOMB])(pair_keys)
    chosen = chosen.reshape(NPAIRS, block_count, DOMB).astype(jnp.int32)
    offsets = (jnp.arange(block_count, dtype=jnp.int32) * NB)[None, :, None]
    return (chosen + offsets).reshape(NPAIRS, DOM).astype(jnp.int32)


def touch_ends(entries, key, least, high):
    index_at = [jax.random.randint(jax.random.fold_in(key, axis), (), 0, length) for axis, length in enumerate(entries.shape)]
    longest = entries.shape.index(max(entries.shape))
    next_to = index_at[:longest] + [(index_at[longest] + 1) % entries.shape[longest]] + index_at[longest + 1:]
    return entries.at[tuple(index_at)].set(least).at[tuple(next_to)].set(high)


def steps_of(own_key, extent, pieces, smallest, high):
    level, own = 1.0, jax.random.fold_in(own_key, 6)
    for axis_at, blocks in pieces:
        steps = jnp.exp(jax.random.uniform(jax.random.fold_in(own, axis_at), (blocks,), jnp.float32, smallest / len(pieces), high / len(pieces)))
        level = level * jnp.repeat(steps, extent[axis_at] // blocks).reshape([-1 if axis == axis_at else 1 for axis in range(len(extent))])
    return level


def shared_out(rng, own, number, rows, amount, top, limit, skew):
    order = jax.random.permutation(rng, amount)
    packed, ordinary = shares(amount, rows * top, limit, skew, True), shares(amount, rows * top, limit, skew, False)
    places = jnp.arange(amount)

    def named(tallies, turn):
        used = int((tallies > 0).sum())
        fixed = max(1, used // 4)
        shifted = fixed + (places - fixed + turn * (used - fixed)) % max(1, amount - fixed)
        return jnp.zeros((amount,), jnp.int32).at[order[jnp.where(places < fixed, places, shifted)]].set(jnp.asarray(tallies, jnp.int32))

    tallies = jnp.where(number % 4 == 0, named(packed, number // 4), named(ordinary, number - number // 4 - 1))
    mixed = jax.random.permutation(jax.random.fold_in(own, 3), amount)
    donor, taker = mixed[0:amount // 2 * 2:2], mixed[1:amount // 2 * 2:2]
    room = jnp.minimum(tallies[donor] - 1, limit - tallies[taker]) // 2
    room = jnp.where((donor == order[0]) | (taker == order[0]) | (tallies[taker] == 0), 0, jnp.maximum(room, 0))
    shifted = jax.random.randint(jax.random.fold_in(own, 4), (amount // 2,), 0, 1 << 20) % (room + 1)
    tallies = tallies.at[donor].add(-shifted).at[taker].add(shifted)
    labels = jnp.searchsorted(jnp.cumsum(tallies), jnp.arange(rows * top), side="right").astype(jnp.int32)
    table = labels.reshape(top, rows).T
    table = table[jax.random.permutation(jax.random.fold_in(own, 1), rows)]
    turn = jax.random.randint(jax.random.fold_in(own, 2), (rows, 1), 0, top)
    return jnp.take_along_axis(table, (jnp.arange(top)[None, :] + turn) % top, axis=1)


def shares(count, total, reach, skew, full):
    weights = [(1 << 20) // math.isqrt(standing ** skew) + 1 for standing in range(1, count + 1)]
    largest = reach if full else min(reach, max(-(-total // count), total * weights[0] // sum(weights)))
    least = 1 if total - largest >= count - 1 else 0
    holding, spare = [largest] + [least] * (count - 1), total - largest - least * (count - 1)
    while spare > 0:
        candidates = [i for i in range(1, count) if holding[i] < largest] or [i for i in range(1, count) if holding[i] < reach]
        mass, budget = sum([weights[i] for i in candidates]), spare
        for i in candidates:
            more = min(reach - holding[i], max(1, budget * weights[i] // mass), spare)
            holding[i] = holding[i] + more
            spare = spare - more
    return np.array(holding)


def gaussian(own_key, dims, spread, reach, pieces=(), kind=jnp.bfloat16):
    loudness = steps_of(own_key, dims, pieces, -0.22, 0.18) if pieces else 1.0
    drawn = jax.random.normal(own_key, dims, jnp.float32) * spread * loudness
    return jnp.minimum(jnp.maximum(drawn, -reach), reach).astype(kind)


def setup_inputs(seed: int = 0) -> dict:
    seeds = jax.random.split(jax.random.key(seed), 10)
    coefficients = gaussian(seeds[0], (NPAIRS, DOM, NPNO), ((NPNO * DOM * DOMB / NB) ** -0.25), 0.4140625, ((0, 8), (1, 4)))
    domain = draw_domain(jax.random.fold_in(seeds[9], 71), 0)
    coupling_owner_keys = jax.random.split(jax.random.fold_in(seeds[2], 1), NPAIRS // PAIRS_DEV)
    coupling_owner_turns = jax.random.permutation(jax.random.fold_in(seeds[2], 3), NPAIRS // PAIRS_DEV)
    coupling_owner = jax.vmap(lambda own, number: shared_out(jax.random.fold_in(seeds[2], 2), own, number, PAIRS_DEV, N_PAIRS, NCPL, MOST, 2))(coupling_owner_keys, coupling_owner_turns).reshape((NPAIRS, NCPL))
    coupling_slot = touch_ends(jax.random.randint(seeds[3], (NPAIRS, NCPL), 0, PAIRS_DEV), jax.random.fold_in(seeds[3], 1), 0, PAIRS_DEV - 1).astype(jnp.int32)
    coupling_fock = jnp.clip(jax.random.uniform(seeds[4], (NPAIRS, NCPL), jnp.float32, -0.5, 0.5) * steps_of(seeds[4], (NPAIRS, NCPL), ((0, 8),), -0.4, 0.0), -0.5, 0.5)
    exchange_integrals = gaussian(seeds[5], (NPAIRS, NPNO, NPNO), 1.0, 6.0, ((0, 8),), jnp.float32)
    pno_energy = jnp.clip(jnp.exp(math.log(3.0) - 2.3025851 * jax.random.uniform(seeds[6], (NPAIRS, NPNO), jnp.float32) ** steps_of(seeds[6], (NPAIRS, NPNO), ((0, 8),), -0.2, 0.2)), 0.3, 3.0)
    pair_shift = jnp.clip(jnp.exp(math.log(2.0) - 1.609438 * jax.random.uniform(seeds[7], (NPAIRS,), jnp.float32) ** steps_of(seeds[7], (NPAIRS,), ((0, 8),), -0.2, 0.2)), 0.4, 2.0)
    amplitudes_start = gaussian(seeds[8], (NPAIRS, NPNO, NPNO), 0.3, 1.8, ((0, 8),), jnp.float32)
    return {"coefficients": coefficients, "domain": domain, "coupling_owner": coupling_owner, "coupling_slot": coupling_slot, "coupling_fock": coupling_fock, "exchange_integrals": exchange_integrals, "pno_energy": pno_energy, "pair_shift": pair_shift, "amplitudes_start": amplitudes_start}


def reference(coefficients, domain, coupling_owner, coupling_slot, coupling_fock, exchange_integrals, pno_energy, pair_shift, amplitudes_start):
    pair_count = coefficients.shape[0]
    total_functions = NB * (DOM // DOMB)
    source = (PAIRS_DEV * coupling_owner + coupling_slot).astype(jnp.int32)
    wide = coefficients.astype(jnp.float32)
    expanded = jnp.zeros((pair_count, total_functions, NPNO), jnp.float32)
    expanded = expanded.at[jnp.arange(pair_count, dtype=jnp.int32)[:, None], domain].set(wide)

    def intersection_one(operand):
        coef_target, dom_target, src = operand
        picked_rows = expanded[src][:, dom_target, :]
        product = jnp.einsum("ra,krc->kac", coef_target, picked_rows, precision=lax.Precision.HIGHEST)
        return product.astype(jnp.bfloat16)

    intersection = lax.map(intersection_one, (wide, domain, source))
    denominator = pno_energy[:, :, None] + pno_energy[:, None, :] + pair_shift[:, None, None]
    amplitudes = amplitudes_start
    for iteration in range(ITERS):
        sendable = amplitudes.astype(jnp.bfloat16)

        def couple(operand):
            intersection_target, src, fock_target = operand
            source_amp = sendable[src].astype(jnp.float32)
            intersection_wide = intersection_target.astype(jnp.float32)
            half_proj = jnp.einsum("kac,kcd->kad", intersection_wide, source_amp, precision=lax.Precision.HIGHEST)
            half_proj = lax.optimization_barrier(half_proj.astype(jnp.bfloat16)).astype(jnp.float32)
            projected = jnp.einsum("kad,kbd->kab", half_proj, intersection_wide, precision=lax.Precision.HIGHEST)
            return jnp.sum(fock_target[:, None, None] * projected, axis=0)

        coupled = lax.map(couple, (intersection, source, coupling_fock))
        amplitudes = -(exchange_integrals + coupled) / denominator
    return amplitudes
```

```python
import functools

import jax
import jax.numpy as jnp
from jax import lax
from jax.experimental import pallas as pl
from jax.experimental.pallas import tpu as pltpu
from jax.sharding import PartitionSpec as P

NB = 192
MESH = pl.DeviceIdType.MESH
F32, BF16 = jnp.float32, jnp.bfloat16


def ring_position(rank, n):
    odd = rank % 2
    return (1 - odd) * (rank // 2) + odd * (n - 1 - rank // 2)


def ring_rank(position, n):
    back = position // (n // 2)
    return (1 - back) * 2 * position + back * (2 * (n - 1 - position) + 1)


def places(n):
    p, g = lax.axis_index("pairs"), lax.axis_index("grp")
    position = ring_position(p, n)
    core, half = g % 2, g // 2
    mate = 2 * half + (1 - core)
    across = 2 * (1 - half) + core
    return p, g, position, mate, across


def at(position, n):
    return ring_rank((position + n) % n, n)


def greet(peers):
    barrier = pltpu.get_barrier_semaphore()
    for peer in peers:
        pl.semaphore_signal(barrier, inc=1, device_id=peer, device_id_type=MESH)
    pl.semaphore_wait(barrier, len(peers))


def remote(src, dst, send, recv, peer):
    return pltpu.make_async_remote_copy(
        src_ref=src, dst_ref=dst, send_sem=send, recv_sem=recv, device_id=peer, device_id_type=MESH
    )


def ring_parts(steps, parts):
    def of(step, direction):
        if step < steps:
            return tuple(range(parts))
        return tuple(c for c in range(parts) if c % 2 == direction)

    return of


def intersections(
    n, slot_ref, c_ref, dom_ref, out_ref,
    cbuf, dbuf, turned, wide, own, msend, mrecv, ysend, yrecv, keep,
    rs, rr, ms, mr, ys, yr,
):
    p, g, position, mate, across = places(n)
    pc = c_ref.shape[0]
    quarter = pc // 4
    rows = c_ref.shape[1]
    steps = n // 2
    right, left = at(position + 1, n), at(position - 1, n)
    ring_peer = (lambda r: (r, g))
    peers = [(right, g), (left, g), (p, mate), (p, across)]
    greet(peers)
    parts_of = ring_parts(steps, 3)
    hp = pc // 2

    def part(ref_c, ref_d, c):
        if c == 2:
            return ref_d
        return ref_c.at[pl.ds(c * hp, hp)]

    def move(step, direction, c):
        offset = -(step - 1) if direction == 0 else step - 1
        rank = at(position + offset, n)
        if step == 1:
            src = part(c_ref, dom_ref, c)
        else:
            src = part(cbuf.at[rank], dbuf.at[rank], c)
        dst = part(cbuf.at[rank], dbuf.at[rank], c)
        return remote(
            src, dst, rs.at[direction, step - 1, c], rr.at[direction, step - 1, c],
            ring_peer(right if direction == 0 else left),
        )

    def arrive(step, direction, c):
        offset = -step if direction == 0 else step
        rank = at(position + offset, n)
        dst = part(cbuf.at[rank], dbuf.at[rank], c)
        remote(
            dst, dst, rs.at[direction, step - 1, c], rr.at[direction, step - 1, c],
            ring_peer(left if direction == 0 else right),
        ).wait_recv()

    for c in (2, 0, 1):
        for d in (0, 1):
            if c in parts_of(1, d):
                move(1, d, c).start()

    base = g * NB
    lines = lax.broadcasted_iota(jnp.int32, (NB, rows), 0)
    core, half = g % 2, g // 2

    def expand(block, doms):
        def one(s, carry):
            hit = (lines == (doms[pl.ds(s, 1), :] - base)).astype(F32).astype(BF16)
            wide[s] = jnp.dot(hit, block[s], preferred_element_type=F32).astype(BF16)
            return carry

        lax.fori_loop(0, pc, one, 0, unroll=8)

    def mate_copy(k, rank):
        return remote(msend.at[k % 2], mrecv.at[rank], ms.at[k], mr.at[k], (p, mate))

    def across_copy(k, rank):
        return remote(ysend.at[k % 2], yrecv.at[rank], ys.at[k], yr.at[k], (p, across))

    ranks = []

    def product(t, rank):
        return jnp.dot(turned[t], wide[slot_ref[t, rank]], preferred_element_type=F32)

    def links(k, rank):
        if k >= 2:
            mate_copy(k - 2, ranks[k - 2]).wait_send()

        def theirs(i, carry):
            t = (2 * (i // quarter) + 1 - core) * quarter + i % quarter
            msend[k % 2, i] = product(t, rank)
            return carry

        lax.fori_loop(0, 2 * quarter, theirs, 0, unroll=8)
        mate_copy(k, rank).start()

        def ours(i, carry):
            t = (2 * (i // quarter) + core) * quarter + i % quarter
            own[k % 2, i] = product(t, rank)
            return carry

        lax.fori_loop(0, 2 * quarter, ours, 0, unroll=8)

    def finish(k):
        rank = ranks[k]
        if k >= 2:
            across_copy(k - 2, ranks[k - 2]).wait_send()
        mate_copy(k, rank).wait_recv()

        def send(j, carry):
            i = (1 - half) * quarter + j
            ysend[k % 2, j] = own[k % 2, i] + mrecv[rank, i]
            return carry

        lax.fori_loop(0, quarter, send, 0)
        across_copy(k, rank).start()

        def hold(j, carry):
            i = half * quarter + j
            keep[rank, j] = own[k % 2, i] + mrecv[rank, i]
            return carry

        lax.fori_loop(0, quarter, hold, 0)

    def process(rank):
        k = len(ranks)
        ranks.append(rank)
        links(k, rank)

    expand(c_ref, dom_ref)

    def turn(t, carry):
        turned[t] = wide[t].astype(F32).T.astype(BF16)
        return carry

    lax.fori_loop(0, pc, turn, 0, unroll=2)
    process(p)
    finish(0)
    for step in range(1, steps + 1):
        for c in (2, 0, 1):
            for d in (0, 1):
                if c in parts_of(step, d):
                    arrive(step, d, c)
                if step < steps and c in parts_of(step + 1, d):
                    move(step + 1, d, c).start()
        if step == steps - 1:
            yield None
        for d in (0, 1) if step < steps else (0,):
            rank = at(position + (-step if d == 0 else step), n)
            expand(cbuf.at[rank], dbuf.at[rank])
            process(rank)
            if d == 1:
                finish(len(ranks) - 2)
        finish(len(ranks) - 1)
    def settle(k):
        rank = ranks[k]
        across_copy(k, rank).wait_recv()

        def last(j, carry):
            out_ref[rank, j] = (keep[rank, j] + yrecv[rank, j]).astype(BF16)
            return carry

        lax.fori_loop(0, quarter, last, 0)

    yield settle
    for k in (n - 2, n - 1):
        mate_copy(k, ranks[k]).wait_send()
        across_copy(k, ranks[k]).wait_send()
    for step in range(1, steps + 1):
        for d in (0, 1):
            for c in parts_of(step, d):
                move(step, d, c).wait_send()


def iteration(
    n, first, joined, alone, slot_ref, fock_ref, start_ref, x_ref, k_ref, e_ref, out_ref,
    abuf, stage, acc, mine, rs, rr, ms, mr, ys, yr, fs, fr,
):
    p, g, position, mate, across = places(n)
    pc = k_ref.shape[0]
    width = k_ref.shape[1]
    quarter = pc // 4
    eighth = quarter // 2
    steps = n // 2
    right, left = at(position + 1, n), at(position - 1, n)
    diagonal = 3 - g
    if alone:
        greet([(right, g), (left, g), (p, mate), (p, across)])
    parts = 4 if joined else 3
    parts_of = ring_parts(steps, parts)

    def chunk(rank, group, c):
        return abuf.at[pl.ds(rank * pc + group * quarter + (c % 2) * eighth, eighth)]

    def span(rank, c):
        return chunk(rank, g if c < 2 else across, c)

    def ring_copy(step, direction, c):
        offset = -(step - 1) if direction == 0 else step - 1
        ref = span(at(position + offset, n), c)
        src = ref
        if step == 1 and c < 2 and not first:
            src = start_ref.at[pl.ds(c * eighth, eighth)]
        return remote(
            src, ref, rs.at[direction, step - 1, c], rr.at[direction, step - 1, c],
            (right if direction == 0 else left, g),
        )

    def arrive(step, direction, c):
        offset = -step if direction == 0 else step
        ref = span(at(position + offset, n), c)
        remote(
            ref, ref, rs.at[direction, step - 1, c], rr.at[direction, step - 1, c],
            (left if direction == 0 else right, g),
        ).wait_recv()

    def mate_copy(k, rank, c, src=None):
        ref = span(rank, c)
        return remote(ref if src is None else src, ref, ms.at[k, c], mr.at[k, c], (p, mate))

    def mate_wait(k, rank):
        for c in range(4):
            ref = chunk(rank, mate if c < 2 else diagonal, c)
            remote(ref, ref, ms.at[k, c], mr.at[k, c], (p, mate)).wait_recv()

    def across_copy(k, rank, c=1, src=None):
        ref = span(rank, c)
        sem = k if c == 1 else n
        return remote(ref if src is None else src, ref, ys.at[sem], yr.at[sem], (p, across))

    def across_wait(k, rank, c=3):
        ref = span(rank, c)
        sem = k if c == 3 else n
        remote(ref, ref, ys.at[sem], yr.at[sem], (p, across)).wait_recv()

    def own_half(c):
        return start_ref.at[pl.ds(c * eighth, eighth)]

    if first:
        def copy_own(i, carry):
            abuf[p * pc + i] = start_ref[i].astype(BF16)
            return carry

        def group_in(group):
            lax.fori_loop(group * quarter, (group + 1) * quarter, copy_own, 0)

        group_in(g)
        for c in (0, 1):
            for d in (0, 1):
                if c in parts_of(1, d):
                    ring_copy(1, d, c).start()
        group_in(across)
        for c in range(2, parts):
            for d in (0, 1):
                if c in parts_of(1, d):
                    ring_copy(1, d, c).start()
        group_in(mate)
        group_in(diagonal)
    else:
        for c in (0, 1):
            across_copy(0, p, c, own_half(c)).start()
            for d in (0, 1):
                if c in parts_of(1, d):
                    ring_copy(1, d, c).start()
        for c in (0, 1):
            mate_copy(0, p, c, own_half(c)).start()

        def copy_own(i, carry):
            abuf[p * pc + g * quarter + i] = start_ref[i]
            return carry

        lax.fori_loop(0, quarter, copy_own, 0)
        across_wait(0, p, 2)
        for d in (0, 1):
            if 2 in parts_of(1, d):
                ring_copy(1, d, 2).start()
        mate_copy(0, p, 2).start()
        across_wait(0, p, 3)
        mate_copy(0, p, 3).start()
        mate_wait(0, p)

    settle = yield None
    acc[...] = jnp.zeros_like(acc)

    def couple(rank, k):
        if settle is not None:
            settle(k)

        def copy(i, carry):
            stage[i] = abuf[rank * pc + i]
            return carry

        lax.fori_loop(0, pc, copy, 0, unroll=4)

        def one(j, carry):
            t = g * quarter + j
            source = stage[slot_ref[t, rank]]
            x = x_ref[rank, j]
            h = jnp.dot(x, source, preferred_element_type=F32).astype(BF16)
            y = lax.dot_general(h, x, (((1,), (1,)), ((), ())), preferred_element_type=F32)
            acc[j] += fock_ref[t, rank] * y
            return carry

        lax.fori_loop(0, quarter, one, 0, unroll=4)

    couple(p, 0)

    def exchange(blocks):
        for k, rank in () if joined else blocks:
            across_wait(k, rank)
            mate_copy(k, rank, 3).start()

    def use(blocks):
        for k, rank in blocks:
            mate_wait(k, rank)
            couple(rank, k)

    landed, shared = [], []
    for step in range(1, steps + 1):
        for c in (1, 0, 2, 3)[:parts]:
            for d in (0, 1):
                rank = at(position + (-step if d == 0 else step), n)
                if c in parts_of(step, d):
                    arrive(step, d, c)
                    if step < steps and c in parts_of(step + 1, d):
                        ring_copy(step + 1, d, c).start()
                    k = 2 * step - 1 + (d if step < steps else 0)
                    if c == 1 and not joined:
                        across_copy(k, rank).start()
                    mate_copy(k, rank, c).start()
        exchange(landed)
        use(shared)
        shared = landed
        landed = [
            (2 * step - 1 + d, at(position + (-step if d == 0 else step), n))
            for d in ((0, 1) if step < steps else (0,))
        ]
    exchange(landed)
    use(shared)
    use(landed)

    def scaled(j):
        t = g * quarter + j
        row = jnp.broadcast_to(e_ref[pl.ds(t, 1), :], (width, width))
        return (-(k_ref[t] + acc[j]) / (row.T + row + fock_ref[t, n])).astype(BF16)

    if first:
        def result(j, carry):
            out_ref[j] = scaled(j)
            return carry

        lax.fori_loop(0, quarter, result, 0, unroll=2)
    else:
        def block(ref, group):
            return ref.at[pl.ds(group * quarter, quarter)]

        def result(j, carry):
            value = scaled(j)
            mine[j] = value
            out_ref[g * quarter + j] = value
            return carry

        lax.fori_loop(0, quarter, result, 0, unroll=2)
        over = remote(mine, block(out_ref, g), fs.at[0], fr.at[0], (p, across))
        beside = remote(mine, block(out_ref, g), fs.at[1], fr.at[1], (p, mate))
        corner = remote(
            block(out_ref, across), block(out_ref, across), fs.at[2], fr.at[2], (p, mate)
        )
        over.start()
        beside.start()
        remote(mine, block(out_ref, across), fs.at[0], fr.at[0], (p, across)).wait_recv()
        corner.start()
        remote(mine, block(out_ref, mate), fs.at[1], fr.at[1], (p, mate)).wait_recv()
        remote(mine, block(out_ref, diagonal), fs.at[2], fr.at[2], (p, mate)).wait_recv()
        over.wait_send()
        beside.wait_send()
        corner.wait_send()
        across_copy(0, p, 0, own_half(0)).wait_send()
        across_copy(0, p, 1, own_half(1)).wait_send()
        for c in range(4):
            mate_copy(0, p, c).wait_send()
    for k in range(1, n):
        if not joined:
            across_copy(k, p).wait_send()
        for c in range(4):
            mate_copy(k, p, c).wait_send()
    for step in range(1, steps + 1):
        for d in (0, 1):
            for c in parts_of(step, d):
                ring_copy(step, d, c).wait_send()


def intersections_alone(*args):
    steps = intersections(*args)
    next(steps)
    settle = next(steps)
    for k in range(args[0]):
        settle(k)
    next(steps, None)


def iteration_alone(n, first, *args):
    steps = iteration(n, first, False, True, *args)
    next(steps)
    try:
        steps.send(None)
    except StopIteration:
        pass


def opening(
    n, made, slot_ref, fock_ref, c_ref, dom_ref, start_ref, k_ref, e_ref, out_ref,
    x_ref, amp_ref, *scratch
):
    used = made + (len(scratch) - made) // 2
    blocks = intersections(n, slot_ref, c_ref, dom_ref, x_ref, *scratch[:made])
    next(blocks)
    amps = iteration(
        n, True, True, False, slot_ref, fock_ref, start_ref, x_ref, k_ref, e_ref, amp_ref,
        *scratch[made:used],
    )
    next(amps)
    settle = next(blocks)
    try:
        amps.send(settle)
    except StopIteration:
        pass
    amps = iteration(
        n, False, False, False, slot_ref, fock_ref, amp_ref, x_ref, k_ref, e_ref, out_ref,
        *scratch[used:],
    )
    next(amps)
    try:
        amps.send(None)
    except StopIteration:
        pass
    next(blocks, None)


class Wires:
    def __init__(self, send, recv, here):
        self.send, self.recv, self.here = send, recv, here
        self.ids, self.started = {}, []

    def link(self, key, src, dst, peer):
        at_key = self.ids.setdefault(key, len(self.ids))
        return remote(src, dst, self.send.at[at_key], self.recv.at[at_key], peer)

    def start(self, key, src, dst, peer, when=None):
        copy = self.link(key, src, dst, peer)
        if when is None:
            copy.start()
        else:
            pl.when(when)(copy.start)
        self.started.append((key, src, dst, peer, when))

    def start_in(self, when, key, src, dst, peer):
        copy = self.link(key, src, dst, peer)
        copy.start()
        self.started.append((key, src, dst, peer, when))

    def start_all(self, when, jobs):
        def run():
            for key, src, dst, peer in jobs:
                self.start_in(when, key, src, dst, peer)

        pl.when(when)(run)

    def wait(self, key, dst, when=None):
        copy = self.link(key, dst, dst, self.here)
        if when is None:
            copy.wait_recv()
        else:
            pl.when(when)(copy.wait_recv)

    def drain(self):
        for *what, when in self.started:
            copy = self.link(*what)
            if when is None:
                copy.wait_send()
            else:
                pl.when(when)(copy.wait_send)


def note(*what):
    return None


def quadrants(
    n, owner_ref, slot_ref, fock_ref, shift_ref, c_ref, dom_ref, start_ref, k_ref, e_ref, out_ref,
    src, dom, blocks, bdom, bslot, bfock, wide, turned, x, start, k_own, amps_a, amps_b, amps_c, amps_d,
    acc, yout, yx, ysum, yin, mine, send, recv, local,
):
    p, g = lax.axis_index("pairs"), lax.axis_index("grp")
    pc, rows, width = c_ref.shape
    quarter = pc // 4
    half_quarter = quarter // 2
    layers = n // 2
    layer, column = p // 2, p % 2
    inner = (layer % 2 + layer // 2) % 2
    mid, end = inner == 1, inner == 0
    partner = (layer + 1 - 2 * (layer % 2)) * 2 + column
    cross = (layers - 1 - layer) * 2 + column
    far = ((layer + layers // 2) % layers) * 2 + column
    beside = layer * 2 + 1 - column
    groups = (g, g + 1 - 2 * (g % 2), (g + 2) % 4, 3 - g)
    _, mate, across, diagonal = groups
    to_mate, to_across = (p, mate), (p, across)
    to_partner, to_cross, to_beside, to_far = (partner, g), (cross, g), (beside, g), (far, g)
    wires = Wires(send, recv, to_mate)
    amps = ((amps_a, amps_b), (amps_c, amps_d))
    wires.mid = mid

    barrier = pltpu.get_barrier_semaphore()

    def hello(peer):
        pl.semaphore_signal(barrier, inc=1, device_id=peer, device_id_type=MESH)

    for peer in (to_far, to_partner, to_beside, to_across, to_mate):
        hello(peer)
    pl.when(mid)(lambda: hello(to_cross))

    load_start = pltpu.make_async_copy(start_ref, start, local.at[0])
    load_start.start()
    load_k = pltpu.make_async_copy(k_ref.at[pl.ds(g * quarter, quarter)], k_own, local.at[1])
    load_k.start()

    def four(group):
        return pl.ds(group * quarter, quarter)

    def two(group, h):
        return pl.ds(group * quarter + h * half_quarter, half_quarter)

    def source(b, rel):
        return c_ref if (b, rel) == (0, 0) else src.at[b, rel]

    def turn(rel):
        for t in range(quarter):
            blocks[0, rel, t] = source(0, rel)[g * quarter + t].T

    for s in range(pc):
        dom[0, 0, s] = dom_ref[pl.ds(s, 1), :]
    turn(0)

    def table(t, carry):
        at_pair = g * quarter + t
        ways = owner_ref.shape[0]
        named = [owner_ref[k, at_pair] for k in range(ways)]
        slots = [slot_ref[k, at_pair] for k in range(ways)]
        focks = [fock_ref[k, at_pair] for k in range(ways)]
        for owner in range(n):
            place, weight = 0, 0.0
            for k in range(ways):
                hit = named[k] == owner
                place = jnp.where(hit, slots[k], place)
                weight = jnp.where(hit, focks[k], weight)
            bslot[0, t, owner] = place
            bfock[0, t, owner] = weight
        return carry

    kinds = {
        "slot": lambda b: bslot.at[b],
        "fock": lambda b: bfock.at[b],
        "dom": lambda b: bdom.at[b],
    }
    for rel in range(2):
        kinds[rel] = functools.partial(lambda rel, b: blocks.at[b, rel], rel)
    for rel in range(2, 4):
        for h in (0, 1):
            kinds[rel, h] = functools.partial(
                lambda rel, h, b: blocks.at[b, rel, pl.ds(h * half_quarter, half_quarter)], rel, h
            )

    def ready(kind):
        at_slot = kinds[kind]
        ref = at_slot(0)
        wires.start_all(end, [
            (("far", kind), ref, at_slot(3), to_far),
            (("beside", kind), ref, at_slot(4), to_beside),
        ])
        wires.start_all(mid, [
            (("partner", kind), ref, at_slot(1), to_partner),
            (("cross", kind), ref, at_slot(2), to_cross),
        ])

    first, second = 2 * inner, 1 + 2 * inner

    def got_first(kind):
        landed, passed = kinds[kind](2), kinds[kind](4)

        def relay():
            wires.wait(("cross", kind), landed)
            wires.start_in(mid, ("beside", kind), landed, passed, to_beside)

        pl.when(mid)(relay)

    def got_second(kind):
        at_slot = kinds[kind]
        wires.wait(("partner", kind), at_slot(1), end)
        wires.wait(("far", kind), at_slot(3), mid)
        wires.start(("beside2", kind), at_slot(second), at_slot(5), to_beside)

    def got_beside(kind):
        wires.wait(("beside", kind), kinds[kind](4))

    def got_beside2(kind):
        wires.wait(("beside2", kind), kinds[kind](5))

    places_of = (first, 4, second, 5)

    lines = lax.broadcasted_iota(jnp.int32, (NB, rows), 0)
    lines2 = lax.broadcasted_iota(jnp.int32, (2 * NB, 2 * rows), 0)

    def expand(b, rel):
        note("expand", b, rel)
        base = groups[rel] * NB
        block = source(b, rel)

        def one(s, carry):
            hit = (lines == (dom[b, rel, s] - base)).astype(F32).astype(BF16)
            wide[b, s, pl.ds(rel * NB, NB)] = jnp.dot(
                hit, block[s], preferred_element_type=F32
            ).astype(BF16)
            return carry

        lax.fori_loop(0, pc, one, 0, unroll=4)

    def make_turned(b, hs=(0, 1)):
        note("make_turned", b)
        place = places_of[b]

        def one(t, carry):
            for h in hs:
                u, v = 2 * h, 2 * h + 1
                row = jnp.concatenate(
                    [
                        bdom[place, u * quarter + t] - groups[u] * NB,
                        bdom[place, v * quarter + t] - groups[v] * NB + NB,
                    ],
                    axis=1,
                )
                hit = (lines2 == row).astype(F32).astype(BF16)
                both = jnp.concatenate([blocks[place, u, t], blocks[place, v, t]], axis=1)
                turned[b, t, :, pl.ds(h * 2 * NB, 2 * NB)] = lax.dot_general(
                    both, hit, (((1,), (1,)), ((), ())), preferred_element_type=F32
                ).astype(BF16)
            return carry

        lax.fori_loop(0, quarter, one, 0, unroll=2)

    owners = (p, partner)

    def make_x(b, s):
        note("make_x", b, s)
        place = places_of[b]

        def one(t, carry):
            at_source = bslot[place, t, owners[s]]
            x[b, t, s] = jnp.dot(
                turned[b, t], wide[s, at_source], preferred_element_type=F32
            ).astype(BF16)
            return carry

        lax.fori_loop(0, quarter, one, 0, unroll=4)

    def couple(b, s, it):
        note("couple", b, s)
        place = places_of[b]
        found = []
        for t in range(quarter):
            at_source = bslot[place, t, owners[s]]
            xs = x[b, t, s]
            half = jnp.dot(xs, amps[it][s][at_source], preferred_element_type=F32).astype(BF16)
            found.append((t, xs, half))
        for t, xs, half in found:
            y = lax.dot_general(half, xs, (((1,), (1,)), ((), ())), preferred_element_type=F32)
            y = bfock[place, t, owners[s]] * y
            if s == 0:
                acc[b, t] = y
            elif b % 2 == 0:
                acc[b, t] += y
            else:
                yout[it, b // 2, t] = (acc[b, t] + y).astype(BF16)

    def post(it, m):
        for t in range(quarter):
            wires.start(("y", it, m, t), yout.at[it, m, t], yx.at[it, m, t], to_beside)

    def share_partner(it, h):
        part = two(g, h)
        wires.start(("a", it, 0, h), amps[it][0].at[part], amps[it][1].at[part], to_partner)

    def pass_partner(it, h):
        part = two(g, h)
        wires.wait(("a", it, 0, h), amps[it][1].at[part])
        for key, peer in ((1, to_across), (2, to_mate)):
            wires.start(("a", it, key, h), amps[it][1].at[part], amps[it][1].at[part], peer)

    def pass_across(it, h):
        part = two(across, h)
        wires.wait(("a", it, 1, h), amps[it][1].at[part])
        wires.start(("a", it, 3, h), amps[it][1].at[part], amps[it][1].at[part], to_mate)

    def have_partner(it):
        for h in (0, 1):
            wires.wait(("a", it, 2, h), amps[it][1].at[two(mate, h)])
            wires.wait(("a", it, 3, h), amps[it][1].at[two(diagonal, h)])

    def sum_second(it):
        for t in range(quarter):
            wires.wait(("y", it, 1, t), yx.at[it, 1, t])
            ysum[it, 1, t] = (acc[2, t] + yx[it, 1, t].astype(F32)).astype(BF16)
            wires.start_all(end, [(("yend", it, t), ysum.at[it, 1, t], yin.at[it, 0, t], to_partner)])
            wires.start_all(mid, [(("yfar", it, t), ysum.at[it, 1, t], yin.at[it, 0, t], to_far)])

    def sum_first(it):
        for t in range(quarter):
            wires.wait(("y", it, 0, t), yx.at[it, 0, t])
            total = acc[0, t] + yx[it, 0, t].astype(F32)
            acc[0, t] = total
            ysum[it, 0, t] = total.astype(BF16)
            wires.start_all(mid, [(("ynear", it, t), ysum.at[it, 0, t], yin.at[it, 1, t], to_cross)])

    def updated(it, t):
        wires.wait(("ynear", it, t), yin.at[it, 1, t], mid)
        wires.wait(("yend", it, t), yin.at[it, 0, t], mid)
        wires.wait(("yfar", it, t), yin.at[it, 0, t], end)
        at_pair = g * quarter + t
        near = yin[it, 1, t].astype(F32)
        total = yin[it, 0, t].astype(F32) + jnp.where(mid, near, acc[0, t])
        row = jnp.broadcast_to(e_ref[pl.ds(at_pair, 1), :], (width, width))
        return (-(k_own[t] + total) / (row.T + row + shift_ref[at_pair])).astype(BF16)

    swap_mate, swap_across = (1, 0, 3, 2), (2, 3, 0, 1)

    def from_mate(i):
        part = four(groups[i])
        wires.wait(("own mate", swap_mate[i]), src.at[0, 1, part])

    def from_across(i):
        part = four(groups[i])
        wires.wait(("own across", swap_across[i]), src.at[0, 2, part])
        wires.start(("own corner", i), src.at[0, 2, part], src.at[0, 3, part], to_mate)

    def from_corner(i):
        part = four(groups[i])
        wires.wait(("own corner", swap_mate[i]), src.at[0, 3, part])

    def to_next(i):
        part = four(groups[i])
        wires.start(("next", i), c_ref.at[part], src.at[1, 0, part], to_partner)

    def from_next(i):
        part = four(groups[i])
        wires.wait(("next", i), src.at[1, 0, part])
        wires.start(("next across", i), src.at[1, 0, part], src.at[1, 2, part], to_across)
        wires.start(("next mate", i), src.at[1, 0, part], src.at[1, 1, part], to_mate)

    def from_next_across(i):
        part = four(groups[i])
        wires.wait(("next across", swap_across[i]), src.at[1, 2, part])
        wires.start(("next corner", i), src.at[1, 2, part], src.at[1, 3, part], to_mate)

    def from_next_mate(i):
        wires.wait(("next mate", swap_mate[i]), src.at[1, 1, four(groups[i])])

    def from_next_corner(i):
        wires.wait(("next corner", swap_mate[i]), src.at[1, 3, four(groups[i])])

    def cast(s, carry):
        amps[0][0][s] = start[s].astype(BF16)
        return carry

    small = ("slot", "fock", "dom")
    late = ((2, 0), (2, 1), (3, 0), (3, 1))

    pl.semaphore_wait(barrier, 5 + inner)
    wires.start(("d", 1), dom.at[0, 0], dom.at[0, 1], to_mate)
    wires.start(("d", 2), dom.at[0, 0], dom.at[0, 2], to_across)
    for i in (2, 3, 0, 1):
        part = four(groups[i])
        wires.start(("own across", i), c_ref.at[part], src.at[0, 2, part], to_across)
    ready(0)
    for i in (1, 0, 2, 3):
        part = four(groups[i])
        wires.start(("own mate", i), c_ref.at[part], src.at[0, 1, part], to_mate)
    from_mate(0)
    turn(1)
    ready(1)
    to_next(0)
    to_next(1)
    lax.fori_loop(0, quarter, table, 0)
    wires.wait(("d", 1), dom.at[0, 1])
    wires.wait(("d", 2), dom.at[0, 2])
    wires.start(("d", 3), dom.at[0, 2], dom.at[0, 3], to_mate)
    load_start.wait()
    lax.fori_loop(0, pc, cast, 0, unroll=2)
    wires.wait(("d", 3), dom.at[0, 3])
    for rel in range(4):
        for t in range(quarter):
            bdom[0, rel * quarter + t] = dom[0, rel, g * quarter + t]
    wires.start(("d", 4), dom.at[0], dom.at[1], to_partner)
    for kind in small:
        ready(kind)
    from_across(0)
    turn(2)
    got_first(0)
    got_second(0)
    expand(0, 0)
    from_across(1)
    from_corner(0)
    turn(3)
    to_next(2)
    share_partner(0, 0)
    share_partner(0, 1)
    to_next(3)
    for kind in late:
        ready(kind)
    got_first(1)
    got_second(1)
    from_across(2)
    from_next(0)
    for i in (1, 2, 3):
        from_mate(i)
    expand(0, 1)
    from_across(3)
    from_next(1)
    for kind in small:
        got_first(kind)
    for i in (1, 2, 3):
        from_corner(i)
    from_next_across(2)
    for kind in late:
        got_first(kind)
    expand(0, 2)
    from_next(2)
    expand(0, 3)
    for h in (0, 1):
        pass_partner(0, h)
    from_next_across(3)
    wires.wait(("d", 4), dom.at[1])
    from_next(3)
    for kind in small:
        got_second(kind)
    for i in range(4):
        from_next_mate(i)
    expand(1, 0)
    from_next_across(0)
    make_turned(0)
    make_x(0, 0)
    for kind in ((2, 0), (2, 1)):
        got_second(kind)
    pass_across(0, 0)
    pass_across(0, 1)
    for kind in (*small, 0, 1, *late):
        got_beside(kind)
    make_turned(1)
    make_x(1, 0)
    for kind in ((3, 0),):
        got_second(kind)
    from_next_across(1)
    for kind in ((3, 1),):
        got_second(kind)
    expand(1, 1)
    have_partner(0)
    for i in range(4):
        from_next_corner(i)
    expand(1, 2)
    expand(1, 3)
    make_x(1, 1)
    couple(1, 0, 0)
    couple(1, 1, 0)
    post(0, 0)
    make_turned(2)
    make_x(2, 0)
    make_x(2, 1)
    couple(2, 0, 0)
    couple(2, 1, 0)
    make_x(0, 1)
    for kind in (*small, 0, 1, *late):
        got_beside2(kind)
    make_turned(3)
    make_x(3, 0)
    make_x(3, 1)
    couple(3, 0, 0)
    couple(3, 1, 0)
    post(0, 1)
    couple(0, 0, 0)
    couple(0, 1, 0)
    load_k.wait()
    sum_first(0)
    sum_second(0)

    for t in range(quarter):
        amps[1][0][g * quarter + t] = updated(0, t)
        if t % half_quarter == half_quarter - 1:
            h = t // half_quarter
            part = two(g, h)
            share_partner(1, h)
            wires.start(("own", 1, h), amps[1][0].at[part], amps[1][0].at[part], to_across)
            wires.start(("own", 2, h), amps[1][0].at[part], amps[1][0].at[part], to_mate)
    for h in (0, 1):
        pass_partner(1, h)
        part = two(across, h)
        wires.wait(("own", 1, h), amps[1][0].at[part])
        wires.start(("own", 3, h), amps[1][0].at[part], amps[1][0].at[part], to_mate)
    for h in (0, 1):
        wires.wait(("own", 2, h), amps[1][0].at[two(mate, h)])
        wires.wait(("own", 3, h), amps[1][0].at[two(diagonal, h)])
    couple(3, 0, 1)
    couple(1, 0, 1)
    pass_across(1, 0)
    couple(2, 0, 1)
    pass_across(1, 1)
    couple(0, 0, 1)
    have_partner(1)
    couple(3, 1, 1)
    post(1, 1)
    couple(1, 1, 1)
    post(1, 0)
    couple(2, 1, 1)
    couple(0, 1, 1)
    sum_second(1)
    sum_first(1)

    for t in range(quarter):
        value = updated(1, t)
        mine[t] = value
        out_ref[g * quarter + t] = value
        if t % half_quarter == half_quarter - 1:
            h = t // half_quarter
            part = pl.ds(h * half_quarter, half_quarter)
            wires.start(("out", 1, h), mine.at[part], out_ref.at[two(g, h)], to_across)
            wires.start(("out", 2, h), mine.at[part], out_ref.at[two(g, h)], to_mate)
    for h in (0, 1):
        part = out_ref.at[two(across, h)]
        wires.wait(("out", 1, h), part)
        wires.start(("out", 3, h), part, part, to_mate)
    for h in (0, 1):
        wires.wait(("out", 2, h), out_ref.at[two(mate, h)])
        wires.wait(("out", 3, h), out_ref.at[two(diagonal, h)])
    wires.drain()


WIRES = 190


def quadrants_fit(n, groups, pc):
    return n == 2 * groups and groups == 4 and pc % (2 * groups) == 0


def quadrants_kernel(n, *refs):
    quadrants(n, *refs)


def quadrants_call(
    n, owner, slot, fock, shift, coefficients, domain, start, integrals, energy
):
    pc, rows, width = coefficients.shape
    quarter = pc // 4
    big = (width, width)
    vmem, smem = pl.BlockSpec(memory_space=pltpu.VMEM), pl.BlockSpec(memory_space=pltpu.SMEM)
    hbm = pl.BlockSpec(memory_space=pl.ANY)
    dma = pltpu.SemaphoreType.DMA
    return pl.pallas_call(
        functools.partial(quadrants_kernel, n),
        out_shape=jax.ShapeDtypeStruct((pc, *big), BF16),
        in_specs=[smem, smem, smem, smem, vmem, vmem, hbm, hbm, vmem],
        out_specs=vmem,
        scratch_shapes=[
            pltpu.VMEM((2, 4, pc, rows, width), BF16),
            pltpu.VMEM((2, 4, pc, 1, rows), jnp.int32),
            pltpu.VMEM((6, 4, quarter, width, rows), BF16),
            pltpu.VMEM((6, 4 * quarter, 1, rows), jnp.int32),
            pltpu.SMEM((6, quarter, n), jnp.int32),
            pltpu.SMEM((6, quarter, n), F32),
            pltpu.VMEM((2, pc, 4 * NB, width), BF16),
            pltpu.VMEM((4, quarter, width, 4 * NB), BF16),
            pltpu.VMEM((4, quarter, 2, *big), BF16),
            pltpu.VMEM((pc, *big), F32),
            pltpu.VMEM((quarter, *big), F32),
            *[pltpu.VMEM((pc, *big), BF16)] * 4,
            pltpu.VMEM((4, quarter, *big), F32),
            pltpu.VMEM((2, 2, quarter, *big), BF16),
            pltpu.VMEM((2, 2, quarter, *big), BF16),
            pltpu.VMEM((2, 2, quarter, *big), BF16),
            pltpu.VMEM((2, 2, quarter, *big), BF16),
            pltpu.VMEM((quarter, *big), BF16),
            dma((WIRES,)), dma((WIRES,)), dma((2,)),
        ],
        compiler_params=pltpu.CompilerParams(
            collective_id=0, has_side_effects=True, vmem_limit_bytes=60 * 2**20
        ),
        name="quadrants",
    )(owner.T, slot.T, fock.T, shift, coefficients, domain, start, integrals, energy).astype(F32)


def on_device(
    coefficients, domain, coupling_owner, coupling_slot, coupling_fock,
    exchange_integrals, pno_energy, pair_shift, amplitudes_start,
):
    n = lax.axis_size("pairs")
    pc, rows, width = coefficients.shape
    quarter = pc // lax.axis_size("grp")
    steps = n // 2
    named = coupling_owner[:, :, None] == jnp.arange(n, dtype=jnp.int32)[None, None, :]
    slots = jnp.sum(jnp.where(named, coupling_slot[:, :, None], 0), axis=1)
    focks = jnp.sum(jnp.where(named, coupling_fock[:, :, None], 0.0), axis=1)
    focks = jnp.concatenate([focks, pair_shift[:, None]], axis=1)
    vmem, smem = pl.BlockSpec(memory_space=pltpu.VMEM), pl.BlockSpec(memory_space=pltpu.SMEM)
    dma = pltpu.SemaphoreType.DMA

    def params(collective):
        return pltpu.CompilerParams(
            collective_id=collective, has_side_effects=True, vmem_limit_bytes=60 * 2**20
        )

    if quadrants_fit(n, lax.axis_size("grp"), pc):
        return quadrants_call(
            n, coupling_owner, coupling_slot, coupling_fock, pair_shift, coefficients, domain,
            amplitudes_start, exchange_integrals, pno_energy,
        )

    big = (width, width)
    x_shape = jax.ShapeDtypeStruct((n, quarter, *big), BF16)
    block_scratch = [
        pltpu.VMEM((n, pc, rows, width), BF16),
        pltpu.VMEM((n, pc, rows), jnp.int32),
        pltpu.VMEM((pc, width, NB), BF16),
        pltpu.VMEM((pc, NB, width), BF16),
        pltpu.VMEM((2, 2 * quarter, *big), F32),
        pltpu.VMEM((2, 2 * quarter, *big), F32),
        pltpu.VMEM((n, 2 * quarter, *big), F32),
        pltpu.VMEM((2, quarter, *big), F32),
        pltpu.VMEM((n, quarter, *big), F32),
        pltpu.VMEM((n, quarter, *big), F32),
        dma((2, steps, 3)), dma((2, steps, 3)),
        dma((n,)), dma((n,)), dma((n,)), dma((n,)),
    ]
    amp_scratch = [
        pltpu.VMEM((n * pc, *big), BF16),
        pltpu.VMEM((pc, *big), BF16),
        pltpu.VMEM((quarter, *big), F32),
        pltpu.VMEM((quarter, *big), BF16),
        dma((2, steps, 4)), dma((2, steps, 4)),
        dma((n, 4)), dma((n, 4)), dma((n + 1,)), dma((n + 1,)), dma((3,)), dma((3,)),
    ]
    half_shape = jax.ShapeDtypeStruct((quarter, *big), BF16)

    def iterate(first, start, x):
        return pl.pallas_call(
            functools.partial(iteration_alone, n, first),
            out_shape=half_shape if first else jax.ShapeDtypeStruct((pc, *big), BF16),
            in_specs=[smem, smem, vmem, vmem, vmem, vmem],
            out_specs=vmem,
            scratch_shapes=amp_scratch,
            compiler_params=params(1 if first else 2),
            name="first" if first else "second",
        )(slots, focks, start, x, exchange_integrals, pno_energy)

    held = n * width * (2 * pc * (rows + width) + 4 * width * 4 * quarter + 2 * width * quarter)
    if held < 40 * 2**20:
        return pl.pallas_call(
            functools.partial(opening, n, len(block_scratch)),
            out_shape=jax.ShapeDtypeStruct((pc, *big), BF16),
            in_specs=[smem, smem, vmem, vmem, vmem, vmem, vmem],
            out_specs=vmem,
            scratch_shapes=[
                pltpu.VMEM(x_shape.shape, BF16), pltpu.VMEM(half_shape.shape, BF16),
                *block_scratch, *amp_scratch, *amp_scratch,
            ],
            compiler_params=params(0),
            name="amplitudes",
        )(slots, focks, coefficients, domain, amplitudes_start, exchange_integrals, pno_energy).astype(F32)
    else:
        x = pl.pallas_call(
            functools.partial(intersections_alone, n),
            out_shape=x_shape,
            in_specs=[smem, vmem, vmem],
            out_specs=vmem,
            scratch_shapes=block_scratch,
            compiler_params=params(0),
            name="intersections",
        )(slots, coefficients, domain)
        amps = iterate(True, amplitudes_start, x)
    return iterate(False, amps, x).astype(F32)


def solution(mesh):
    placed = (
        P("pairs", "grp", None),
        P("pairs", "grp"),
        P("pairs", None),
        P("pairs", None),
        P("pairs", None),
        P("pairs", None, None),
        P("pairs", None),
        P("pairs"),
        P("pairs", None, None),
    )
    return jax.shard_map(
        on_device, mesh=mesh, in_specs=placed, out_specs=P("pairs", None, None), check_vma=False
    )
```

```python
import functools

import jax
import jax.numpy as jnp
from jax import lax
from jax.experimental import pallas as pl
from jax.experimental.pallas import tpu as pltpu
from jax.sharding import PartitionSpec as P

NB = 192
MESH = pl.DeviceIdType.MESH
F32, BF16 = jnp.float32, jnp.bfloat16


def ring_position(rank, n):
    odd = rank % 2
    return (1 - odd) * (rank // 2) + odd * (n - 1 - rank // 2)


def ring_rank(position, n):
    back = position // (n // 2)
    return (1 - back) * 2 * position + back * (2 * (n - 1 - position) + 1)


def places(n):
    p, g = lax.axis_index("pairs"), lax.axis_index("grp")
    position = ring_position(p, n)
    core, half = g % 2, g // 2
    mate = 2 * half + (1 - core)
    across = 2 * (1 - half) + core
    return p, g, position, mate, across


def at(position, n):
    return ring_rank((position + n) % n, n)


def greet(peers):
    barrier = pltpu.get_barrier_semaphore()
    for peer in peers:
        pl.semaphore_signal(barrier, inc=1, device_id=peer, device_id_type=MESH)
    pl.semaphore_wait(barrier, len(peers))


def remote(src, dst, send, recv, peer):
    return pltpu.make_async_remote_copy(
        src_ref=src, dst_ref=dst, send_sem=send, recv_sem=recv, device_id=peer, device_id_type=MESH
    )


def ring_parts(steps, parts):
    def of(step, direction):
        if step < steps:
            return tuple(range(parts))
        return tuple(c for c in range(parts) if c % 2 == direction)

    return of


def intersections(
    n, slot_ref, c_ref, dom_ref, out_ref,
    cbuf, dbuf, turned, wide, own, msend, mrecv, ysend, yrecv, keep,
    rs, rr, ms, mr, ys, yr,
):
    p, g, position, mate, across = places(n)
    pc = c_ref.shape[0]
    quarter = pc // 4
    rows = c_ref.shape[1]
    steps = n // 2
    right, left = at(position + 1, n), at(position - 1, n)
    ring_peer = (lambda r: (r, g))
    peers = [(right, g), (left, g), (p, mate), (p, across)]
    greet(peers)
    parts_of = ring_parts(steps, 3)
    hp = pc // 2

    def part(ref_c, ref_d, c):
        if c == 2:
            return ref_d
        return ref_c.at[pl.ds(c * hp, hp)]

    def move(step, direction, c):
        offset = -(step - 1) if direction == 0 else step - 1
        rank = at(position + offset, n)
        if step == 1:
            src = part(c_ref, dom_ref, c)
        else:
            src = part(cbuf.at[rank], dbuf.at[rank], c)
        dst = part(cbuf.at[rank], dbuf.at[rank], c)
        return remote(
            src, dst, rs.at[direction, step - 1, c], rr.at[direction, step - 1, c],
            ring_peer(right if direction == 0 else left),
        )

    def arrive(step, direction, c):
        offset = -step if direction == 0 else step
        rank = at(position + offset, n)
        dst = part(cbuf.at[rank], dbuf.at[rank], c)
        remote(
            dst, dst, rs.at[direction, step - 1, c], rr.at[direction, step - 1, c],
            ring_peer(left if direction == 0 else right),
        ).wait_recv()

    for c in (2, 0, 1):
        for d in (0, 1):
            if c in parts_of(1, d):
                move(1, d, c).start()

    base = g * NB
    lines = lax.broadcasted_iota(jnp.int32, (NB, rows), 0)
    core, half = g % 2, g // 2

    def expand(block, doms):
        def one(s, carry):
            hit = (lines == (doms[pl.ds(s, 1), :] - base)).astype(F32).astype(BF16)
            wide[s] = jnp.dot(hit, block[s], preferred_element_type=F32).astype(BF16)
            return carry

        lax.fori_loop(0, pc, one, 0, unroll=8)

    def mate_copy(k, rank):
        return remote(msend.at[k % 2], mrecv.at[rank], ms.at[k], mr.at[k], (p, mate))

    def across_copy(k, rank):
        return remote(ysend.at[k % 2], yrecv.at[rank], ys.at[k], yr.at[k], (p, across))

    ranks = []

    def product(t, rank):
        return jnp.dot(turned[t], wide[slot_ref[t, rank]], preferred_element_type=F32)

    def links(k, rank):
        if k >= 2:
            mate_copy(k - 2, ranks[k - 2]).wait_send()

        def theirs(i, carry):
            t = (2 * (i // quarter) + 1 - core) * quarter + i % quarter
            msend[k % 2, i] = product(t, rank)
            return carry

        lax.fori_loop(0, 2 * quarter, theirs, 0, unroll=8)
        mate_copy(k, rank).start()

        def ours(i, carry):
            t = (2 * (i // quarter) + core) * quarter + i % quarter
            own[k % 2, i] = product(t, rank)
            return carry

        lax.fori_loop(0, 2 * quarter, ours, 0, unroll=8)

    def finish(k):
        rank = ranks[k]
        if k >= 2:
            across_copy(k - 2, ranks[k - 2]).wait_send()
        mate_copy(k, rank).wait_recv()

        def send(j, carry):
            i = (1 - half) * quarter + j
            ysend[k % 2, j] = own[k % 2, i] + mrecv[rank, i]
            return carry

        lax.fori_loop(0, quarter, send, 0)
        across_copy(k, rank).start()

        def hold(j, carry):
            i = half * quarter + j
            keep[rank, j] = own[k % 2, i] + mrecv[rank, i]
            return carry

        lax.fori_loop(0, quarter, hold, 0)

    def process(rank):
        k = len(ranks)
        ranks.append(rank)
        links(k, rank)

    expand(c_ref, dom_ref)

    def turn(t, carry):
        turned[t] = wide[t].astype(F32).T.astype(BF16)
        return carry

    lax.fori_loop(0, pc, turn, 0, unroll=2)
    process(p)
    finish(0)
    for step in range(1, steps + 1):
        for c in (2, 0, 1):
            for d in (0, 1):
                if c in parts_of(step, d):
                    arrive(step, d, c)
                if step < steps and c in parts_of(step + 1, d):
                    move(step + 1, d, c).start()
        if step == steps - 1:
            yield None
        for d in (0, 1) if step < steps else (0,):
            rank = at(position + (-step if d == 0 else step), n)
            expand(cbuf.at[rank], dbuf.at[rank])
            process(rank)
            if d == 1:
                finish(len(ranks) - 2)
        finish(len(ranks) - 1)
    def settle(k):
        rank = ranks[k]
        across_copy(k, rank).wait_recv()

        def last(j, carry):
            out_ref[rank, j] = (keep[rank, j] + yrecv[rank, j]).astype(BF16)
            return carry

        lax.fori_loop(0, quarter, last, 0)

    yield settle
    for k in (n - 2, n - 1):
        mate_copy(k, ranks[k]).wait_send()
        across_copy(k, ranks[k]).wait_send()
    for step in range(1, steps + 1):
        for d in (0, 1):
            for c in parts_of(step, d):
                move(step, d, c).wait_send()


def iteration(
    n, first, joined, alone, slot_ref, fock_ref, start_ref, x_ref, k_ref, e_ref, out_ref,
    abuf, stage, acc, mine, rs, rr, ms, mr, ys, yr, fs, fr,
):
    p, g, position, mate, across = places(n)
    pc = k_ref.shape[0]
    width = k_ref.shape[1]
    quarter = pc // 4
    eighth = quarter // 2
    steps = n // 2
    right, left = at(position + 1, n), at(position - 1, n)
    diagonal = 3 - g
    if alone:
        greet([(right, g), (left, g), (p, mate), (p, across)])
    parts = 4 if joined else 3
    parts_of = ring_parts(steps, parts)

    def chunk(rank, group, c):
        return abuf.at[pl.ds(rank * pc + group * quarter + (c % 2) * eighth, eighth)]

    def span(rank, c):
        return chunk(rank, g if c < 2 else across, c)

    def ring_copy(step, direction, c):
        offset = -(step - 1) if direction == 0 else step - 1
        ref = span(at(position + offset, n), c)
        src = ref
        if step == 1 and c < 2 and not first:
            src = start_ref.at[pl.ds(c * eighth, eighth)]
        return remote(
            src, ref, rs.at[direction, step - 1, c], rr.at[direction, step - 1, c],
            (right if direction == 0 else left, g),
        )

    def arrive(step, direction, c):
        offset = -step if direction == 0 else step
        ref = span(at(position + offset, n), c)
        remote(
            ref, ref, rs.at[direction, step - 1, c], rr.at[direction, step - 1, c],
            (left if direction == 0 else right, g),
        ).wait_recv()

    def mate_copy(k, rank, c, src=None):
        ref = span(rank, c)
        return remote(ref if src is None else src, ref, ms.at[k, c], mr.at[k, c], (p, mate))

    def mate_wait(k, rank):
        for c in range(4):
            ref = chunk(rank, mate if c < 2 else diagonal, c)
            remote(ref, ref, ms.at[k, c], mr.at[k, c], (p, mate)).wait_recv()

    def across_copy(k, rank, c=1, src=None):
        ref = span(rank, c)
        sem = k if c == 1 else n
        return remote(ref if src is None else src, ref, ys.at[sem], yr.at[sem], (p, across))

    def across_wait(k, rank, c=3):
        ref = span(rank, c)
        sem = k if c == 3 else n
        remote(ref, ref, ys.at[sem], yr.at[sem], (p, across)).wait_recv()

    def own_half(c):
        return start_ref.at[pl.ds(c * eighth, eighth)]

    if first:
        def copy_own(i, carry):
            abuf[p * pc + i] = start_ref[i].astype(BF16)
            return carry

        def group_in(group):
            lax.fori_loop(group * quarter, (group + 1) * quarter, copy_own, 0)

        group_in(g)
        for c in (0, 1):
            for d in (0, 1):
                if c in parts_of(1, d):
                    ring_copy(1, d, c).start()
        group_in(across)
        for c in range(2, parts):
            for d in (0, 1):
                if c in parts_of(1, d):
                    ring_copy(1, d, c).start()
        group_in(mate)
        group_in(diagonal)
    else:
        for c in (0, 1):
            across_copy(0, p, c, own_half(c)).start()
            for d in (0, 1):
                if c in parts_of(1, d):
                    ring_copy(1, d, c).start()
        for c in (0, 1):
            mate_copy(0, p, c, own_half(c)).start()

        def copy_own(i, carry):
            abuf[p * pc + g * quarter + i] = start_ref[i]
            return carry

        lax.fori_loop(0, quarter, copy_own, 0)
        across_wait(0, p, 2)
        for d in (0, 1):
            if 2 in parts_of(1, d):
                ring_copy(1, d, 2).start()
        mate_copy(0, p, 2).start()
        across_wait(0, p, 3)
        mate_copy(0, p, 3).start()
        mate_wait(0, p)

    settle = yield None
    acc[...] = jnp.zeros_like(acc)

    def couple(rank, k):
        if settle is not None:
            settle(k)

        def copy(i, carry):
            stage[i] = abuf[rank * pc + i]
            return carry

        lax.fori_loop(0, pc, copy, 0, unroll=4)

        def one(j, carry):
            t = g * quarter + j
            source = stage[slot_ref[t, rank]]
            x = x_ref[rank, j]
            h = jnp.dot(x, source, preferred_element_type=F32).astype(BF16)
            y = lax.dot_general(h, x, (((1,), (1,)), ((), ())), preferred_element_type=F32)
            acc[j] += fock_ref[t, rank] * y
            return carry

        lax.fori_loop(0, quarter, one, 0, unroll=4)

    couple(p, 0)

    def exchange(blocks):
        for k, rank in () if joined else blocks:
            across_wait(k, rank)
            mate_copy(k, rank, 3).start()

    def use(blocks):
        for k, rank in blocks:
            mate_wait(k, rank)
            couple(rank, k)

    landed, shared = [], []
    for step in range(1, steps + 1):
        for c in (1, 0, 2, 3)[:parts]:
            for d in (0, 1):
                rank = at(position + (-step if d == 0 else step), n)
                if c in parts_of(step, d):
                    arrive(step, d, c)
                    if step < steps and c in parts_of(step + 1, d):
                        ring_copy(step + 1, d, c).start()
                    k = 2 * step - 1 + (d if step < steps else 0)
                    if c == 1 and not joined:
                        across_copy(k, rank).start()
                    mate_copy(k, rank, c).start()
        exchange(landed)
        use(shared)
        shared = landed
        landed = [
            (2 * step - 1 + d, at(position + (-step if d == 0 else step), n))
            for d in ((0, 1) if step < steps else (0,))
        ]
    exchange(landed)
    use(shared)
    use(landed)

    def scaled(j):
        t = g * quarter + j
        row = jnp.broadcast_to(e_ref[pl.ds(t, 1), :], (width, width))
        return (-(k_ref[t] + acc[j]) / (row.T + row + fock_ref[t, n])).astype(BF16)

    if first:
        def result(j, carry):
            out_ref[j] = scaled(j)
            return carry

        lax.fori_loop(0, quarter, result, 0, unroll=2)
    else:
        def block(ref, group):
            return ref.at[pl.ds(group * quarter, quarter)]

        def result(j, carry):
            value = scaled(j)
            mine[j] = value
            out_ref[g * quarter + j] = value
            return carry

        lax.fori_loop(0, quarter, result, 0, unroll=2)
        over = remote(mine, block(out_ref, g), fs.at[0], fr.at[0], (p, across))
        beside = remote(mine, block(out_ref, g), fs.at[1], fr.at[1], (p, mate))
        corner = remote(
            block(out_ref, across), block(out_ref, across), fs.at[2], fr.at[2], (p, mate)
        )
        over.start()
        beside.start()
        remote(mine, block(out_ref, across), fs.at[0], fr.at[0], (p, across)).wait_recv()
        corner.start()
        remote(mine, block(out_ref, mate), fs.at[1], fr.at[1], (p, mate)).wait_recv()
        remote(mine, block(out_ref, diagonal), fs.at[2], fr.at[2], (p, mate)).wait_recv()
        over.wait_send()
        beside.wait_send()
        corner.wait_send()
        across_copy(0, p, 0, own_half(0)).wait_send()
        across_copy(0, p, 1, own_half(1)).wait_send()
        for c in range(4):
            mate_copy(0, p, c).wait_send()
    for k in range(1, n):
        if not joined:
            across_copy(k, p).wait_send()
        for c in range(4):
            mate_copy(k, p, c).wait_send()
    for step in range(1, steps + 1):
        for d in (0, 1):
            for c in parts_of(step, d):
                ring_copy(step, d, c).wait_send()


def intersections_alone(*args):
    steps = intersections(*args)
    next(steps)
    settle = next(steps)
    for k in range(args[0]):
        settle(k)
    next(steps, None)


def iteration_alone(n, first, *args):
    steps = iteration(n, first, False, True, *args)
    next(steps)
    try:
        steps.send(None)
    except StopIteration:
        pass


def opening(
    n, made, slot_ref, fock_ref, c_ref, dom_ref, start_ref, k_ref, e_ref, out_ref,
    x_ref, amp_ref, *scratch
):
    used = made + (len(scratch) - made) // 2
    blocks = intersections(n, slot_ref, c_ref, dom_ref, x_ref, *scratch[:made])
    next(blocks)
    amps = iteration(
        n, True, True, False, slot_ref, fock_ref, start_ref, x_ref, k_ref, e_ref, amp_ref,
        *scratch[made:used],
    )
    next(amps)
    settle = next(blocks)
    try:
        amps.send(settle)
    except StopIteration:
        pass
    amps = iteration(
        n, False, False, False, slot_ref, fock_ref, amp_ref, x_ref, k_ref, e_ref, out_ref,
        *scratch[used:],
    )
    next(amps)
    try:
        amps.send(None)
    except StopIteration:
        pass
    next(blocks, None)


class Wires:
    def __init__(self, send, recv, here):
        self.send, self.recv, self.here = send, recv, here
        self.sends, self.recvs, self.wholes = {}, {}, {}

    def link(self, key, src, dst, peer, out=None):
        out = key if out is None else out
        at_send = self.sends.setdefault(out, len(self.sends))
        at_recv = self.recvs.setdefault(key, len(self.recvs))
        return remote(src, dst, self.send.at[at_send], self.recv.at[at_recv], peer)

    def start_in(self, when, key, src, dst, peer, out=None, whole=None):
        self.link(key, src, dst, peer, out).start()
        out = key if out is None else out
        role = 0 if when is None else 1 + (when is self.mid)
        self.wholes[out, role] = (src if whole is None else whole, when)

    def start(self, key, src, dst, peer, when=None, out=None, whole=None):
        def run():
            self.start_in(when, key, src, dst, peer, out, whole)

        if when is None:
            run()
        else:
            pl.when(when)(run)

    def start_all(self, when, jobs):
        def run():
            for job in jobs:
                self.start_in(when, *job)

        pl.when(when)(run)

    def wait(self, key, dst, when=None):
        at_recv = self.recvs.setdefault(key, len(self.recvs))
        copy = remote(dst, dst, self.send.at[0], self.recv.at[at_recv], self.here)
        if when is None:
            copy.wait_recv()
        else:
            pl.when(when)(copy.wait_recv)

    def drain(self):
        for (out, _), (whole, when) in self.wholes.items():
            at_send = self.sends[out]
            copy = remote(whole, whole, self.send.at[at_send], self.recv.at[0], self.here)
            if when is None:
                copy.wait_send()
            else:
                pl.when(when)(copy.wait_send)


def note(*what):
    return None


def quadrants(
    n, owner_hbm, slot_hbm, fock_hbm, shift_hbm, c_hbm, dom_hbm, start_ref, k_ref, e_hbm, out_ref,
    owner_ref, slot_ref, fock_ref, shift_ref, c_ref, dom_ref, e_ref, src, dom, blocks, bdom, bslot, bfock, wide, turned, x, start, k_own, amps_a, amps_b, amps_c, amps_d,
    acc, yout, yx, ysum, yin, mine, send, recv, local, nearby,
):
    p, g = lax.axis_index("pairs"), lax.axis_index("grp")
    pc, rows, width = c_ref.shape
    quarter = pc // 4
    half_quarter = quarter // 2
    layers = n // 2
    layer, column = p // 2, p % 2
    inner = (layer % 2 + layer // 2) % 2
    mid, end = inner == 1, inner == 0
    partner = (layer + 1 - 2 * (layer % 2)) * 2 + column
    cross = (layers - 1 - layer) * 2 + column
    far = ((layer + layers // 2) % layers) * 2 + column
    beside = layer * 2 + 1 - column
    groups = (g, g + 1 - 2 * (g % 2), (g + 2) % 4, 3 - g)
    _, mate, across, diagonal = groups
    to_mate, to_across = (p, mate), (p, across)
    to_partner, to_cross, to_beside, to_far = (partner, g), (cross, g), (beside, g), (far, g)
    wires = Wires(send, recv, to_mate)
    amps = ((amps_a, amps_b), (amps_c, amps_d))
    wires.mid = mid

    barrier = pltpu.get_barrier_semaphore()

    def hello(peer):
        pl.semaphore_signal(barrier, inc=1, device_id=peer, device_id_type=MESH)

    for peer in (to_partner, to_beside, to_across, to_mate):
        hello(peer)
    pl.when(mid)(lambda: hello(to_cross))

    pairs = (
        (c_hbm, c_ref), (dom_hbm, dom_ref), (owner_hbm, owner_ref), (slot_hbm, slot_ref),
        (fock_hbm, fock_ref), (shift_hbm, shift_ref), (e_hbm, e_ref), (start_ref, start),
        (k_ref.at[pl.ds(g * quarter, quarter)], k_own),
    )
    loads = [pltpu.make_async_copy(*pair, local.at[i]) for i, pair in enumerate(pairs)]
    for load in loads:
        load.start()
    load_c, load_dom, load_owner, load_slot, load_fock, load_shift, load_e, load_start, load_k = loads
    load_c.wait()
    load_dom.wait()

    def four(group):
        return pl.ds(group * quarter, quarter)

    def two(group, h):
        return pl.ds(group * quarter + h * half_quarter, half_quarter)

    def both_quarters(ref):
        return ref.at[pl.ds(0, 2 * quarter)]

    def three_quarters(ref):
        return ref.at[pl.ds(0, 3 * quarter)]

    def source(b, rel):
        return c_ref if (b, rel) == (0, 0) else src.at[b, rel]

    def turn(rel):
        for t in range(quarter):
            blocks[0, rel, t] = source(0, rel)[g * quarter + t].T

    for s in range(pc):
        dom[0, 0, s] = dom_ref[pl.ds(s, 1), :]
    turn(0)

    def table(t, carry):
        at_pair = g * quarter + t
        ways = owner_ref.shape[0]
        named = [owner_ref[k, at_pair] for k in range(ways)]
        slots = [slot_ref[k, at_pair] for k in range(ways)]
        focks = [fock_ref[k, at_pair] for k in range(ways)]
        for owner in range(n):
            place, weight = 0, 0.0
            for k in range(ways):
                hit = named[k] == owner
                place = jnp.where(hit, slots[k], place)
                weight = jnp.where(hit, focks[k], weight)
            bslot[0, t, owner] = place
            bfock[0, t, owner] = weight
        return carry

    small = ("slot", "fock", "dom")
    kinds = {
        "slot": lambda b: bslot.at[b],
        "fock": lambda b: bfock.at[b],
        "dom": lambda b: bdom.at[b],
    }
    for rel in range(2):
        kinds[rel] = functools.partial(lambda rel, b: blocks.at[b, rel], rel)
    for rel in range(2, 4):
        for h in (0, 1):
            kinds[rel, h] = functools.partial(
                lambda rel, h, b: blocks.at[b, rel, pl.ds(h * half_quarter, half_quarter)], rel, h
            )

    def ready(kind):
        at_slot = kinds[kind]
        ref = at_slot(0)
        whole, tag = (ref, kind) if kind in small else (blocks.at[0], 0)
        together = ("beside", tag)
        wires.start_all(end, [
            (("second", kind), ref, at_slot(3), to_far, ("second", tag), whole),
            (together, ref, at_slot(4), to_beside, together, whole),
        ])
        wires.start_all(mid, [
            (("second", kind), ref, at_slot(1), to_partner, ("second", tag), whole),
            (("cross", kind), ref, at_slot(2), to_cross, ("cross", tag), whole),
        ])

    first, second = 2 * inner, 1 + 2 * inner

    def got_first(kind):
        landed, passed = kinds[kind](2), kinds[kind](4)
        whole, tag = (landed, kind) if kind in small else (blocks.at[2], 0)
        together = ("beside", tag)

        def relay():
            wires.wait(("cross", kind), landed)
            wires.start_in(mid, together, landed, passed, to_beside, together, whole)

        pl.when(mid)(relay)

    def got_second(kind):
        at_slot = kinds[kind]
        landed = at_slot(second)
        whole, tag = (landed, kind) if kind in small else (blocks.at[0], 0)
        together = ("beside2", tag)
        wires.wait(("second", kind), landed)
        wires.start(together, landed, at_slot(5), to_beside, None, together, whole)

    def got_beside():
        for kind in small:
            wires.wait(("beside", kind), kinds[kind](4))
        wires.wait(("beside", 0), blocks.at[4])

    def got_beside2():
        for kind in small:
            wires.wait(("beside2", kind), kinds[kind](5))
        wires.wait(("beside2", 0), blocks.at[5])

    places_of = (first, 4, second, 5)

    lines = lax.broadcasted_iota(jnp.int32, (NB, rows), 0)
    lines2 = lax.broadcasted_iota(jnp.int32, (2 * NB, 2 * rows), 0)

    def expand(b, rel):
        note("expand", b, rel)
        base = groups[rel] * NB
        block = source(b, rel)

        def one(s, carry):
            hit = (lines == (dom[b, rel, s] - base)).astype(F32).astype(BF16)
            wide[b, s, pl.ds(rel * NB, NB)] = jnp.dot(
                hit, block[s], preferred_element_type=F32
            ).astype(BF16)
            return carry

        lax.fori_loop(0, pc, one, 0, unroll=4)

    def make_turned(b, hs=(0, 1)):
        note("make_turned", b)
        place = places_of[b]

        def one(t, carry):
            for h in hs:
                u, v = 2 * h, 2 * h + 1
                row = jnp.concatenate(
                    [
                        bdom[place, u * quarter + t] - groups[u] * NB,
                        bdom[place, v * quarter + t] - groups[v] * NB + NB,
                    ],
                    axis=1,
                )
                hit = (lines2 == row).astype(F32).astype(BF16)
                both = jnp.concatenate([blocks[place, u, t], blocks[place, v, t]], axis=1)
                turned[b, t, :, pl.ds(h * 2 * NB, 2 * NB)] = lax.dot_general(
                    both, hit, (((1,), (1,)), ((), ())), preferred_element_type=F32
                ).astype(BF16)
            return carry

        lax.fori_loop(0, quarter, one, 0, unroll=2)

    owners = (p, partner)

    def make_x(b, s):
        note("make_x", b, s)
        place = places_of[b]

        def one(t, carry):
            at_source = bslot[place, t, owners[s]]
            x[b, t, s] = jnp.dot(
                turned[b, t], wide[s, at_source], preferred_element_type=F32
            ).astype(BF16)
            return carry

        lax.fori_loop(0, quarter, one, 0, unroll=4)

    def couple(b, s, it):
        note("couple", b, s)
        place = places_of[b]
        found = []
        for t in range(quarter):
            at_source = bslot[place, t, owners[s]]
            xs = x[b, t, s]
            half = jnp.dot(xs, amps[it][s][at_source], preferred_element_type=F32).astype(BF16)
            found.append((t, xs, half))
        for t, xs, half in found:
            y = lax.dot_general(half, xs, (((1,), (1,)), ((), ())), preferred_element_type=F32)
            y = bfock[place, t, owners[s]] * y
            if s == 0:
                acc[b, t] = y
            elif b % 2 == 0:
                acc[b, t] += y
            else:
                yout[it, b // 2, t] = (acc[b, t] + y).astype(BF16)

    def post(it, m):
        for t in range(quarter):
            wires.start(
                ("y", it, m, t), yout.at[it, m, t], yx.at[it, m, t], to_beside, None,
                ("y", it, m), yout.at[it, m],
            )

    def share_partner(it, h):
        part = two(g, h)
        wires.start(
            ("a", it, 0, h), amps[it][0].at[part], amps[it][1].at[part], to_partner, None,
            ("a", it, 0), amps[it][0].at[four(g)],
        )

    def pass_partner(it, h):
        part = two(g, h)
        wires.wait(("a", it, 0, h), amps[it][1].at[part])
        ref = amps[it][1].at[part]
        wires.start(("a", it, 1, h), ref, ref, to_across, None, ("a", it, 1), amps[it][1].at[four(g)])
        wires.start(("a", it, 2), ref, ref, to_mate, None, ("a", it, 2), both_quarters(amps[it][1]))

    def pass_across(it, h):
        part = two(across, h)
        wires.wait(("a", it, 1, h), amps[it][1].at[part])
        ref = amps[it][1].at[part]
        wires.start(("a", it, 2), ref, ref, to_mate, None, ("a", it, 2), both_quarters(amps[it][1]))

    def have_partner(it):
        wires.wait(("a", it, 2), both_quarters(amps[it][1]))

    def sum_second(it):
        for t in range(quarter):
            wires.wait(("y", it, 1, t), yx.at[it, 1, t])
            ysum[it, 1, t] = (acc[2, t] + yx[it, 1, t].astype(F32)).astype(BF16)
            job = (("yfar", it, t), ysum.at[it, 1, t], yin.at[it, 0, t])
            group = (("yfar", it), ysum.at[it, 1])
            wires.start_all(end, [(*job, to_partner, *group)])
            wires.start_all(mid, [(*job, to_far, *group)])

    def sum_first(it):
        for t in range(quarter):
            wires.wait(("y", it, 0, t), yx.at[it, 0, t])
            total = acc[0, t] + yx[it, 0, t].astype(F32)
            acc[0, t] = total
            ysum[it, 0, t] = total.astype(BF16)
            wires.start_all(mid, [(
                ("ynear", it, t), ysum.at[it, 0, t], yin.at[it, 1, t], to_cross,
                ("ynear", it), ysum.at[it, 0],
            )])

    def coupled(it, t):
        wires.wait(("ynear", it, t), yin.at[it, 1, t], mid)
        wires.wait(("yfar", it, t), yin.at[it, 0, t])
        near = yin[it, 1, t].astype(F32)
        return yin[it, 0, t].astype(F32) + jnp.where(mid, near, acc[0, t])

    def updated(it, t):
        at_pair = g * quarter + t
        total = coupled(it, t)
        row = jnp.broadcast_to(e_ref[pl.ds(at_pair, 1), :], (width, width))
        return (-(k_own[t] + total) / (row.T + row + shift_ref[at_pair])).astype(BF16)

    swap_mate, swap_across = (1, 0, 3, 2), (2, 3, 0, 1)

    def from_mate():
        wires.wait(("own mate", 1), src.at[0, 1, four(g)])

    def from_mate_rest():
        wires.wait(("own mate", 0), three_quarters(src.at[0, 1]))

    def from_across(i):
        part = four(groups[i])
        wires.wait(("own across", swap_across[i]), src.at[0, 2, part])
        wires.start(
            ("own corner", int(i == 1)), src.at[0, 2, part], src.at[0, 3, part], to_mate, None,
            ("own corner", 0), src.at[0, 2],
        )

    def from_corner():
        wires.wait(("own corner", 1), src.at[0, 3, four(g)])

    def from_corner_rest():
        wires.wait(("own corner", 0), three_quarters(src.at[0, 3]))

    def to_next(i):
        part = four(groups[i])
        wires.start(
            ("next", i), c_ref.at[part], src.at[1, 0, part], to_partner, None, ("next", 0), c_ref
        )

    def from_next(i):
        part = four(groups[i])
        wires.wait(("next", i), src.at[1, 0, part])
        ref = src.at[1, 0, part]
        wires.start(
            ("next across", i), ref, src.at[1, 2, part], to_across, None,
            ("next across", 0), src.at[1, 0],
        )
        wires.start(
            ("next mate", 0), ref, src.at[1, 1, part], to_mate, None,
            ("next mate", 0), src.at[1, 0],
        )

    def from_next_across(i):
        part = four(groups[i])
        wires.wait(("next across", swap_across[i]), src.at[1, 2, part])
        wires.start(
            ("next corner", 0), src.at[1, 2, part], src.at[1, 3, part], to_mate, None,
            ("next corner", 0), src.at[1, 2],
        )

    def from_next_mate():
        wires.wait(("next mate", 0), src.at[1, 1])

    def from_next_corner():
        wires.wait(("next corner", 0), src.at[1, 3])

    def cast(s, carry):
        amps[0][0][s] = start[s].astype(BF16)
        return carry

    late = ((2, 0), (2, 1), (3, 0), (3, 1))

    pl.semaphore_wait(barrier, 4 + inner)

    def nearby_is_in():
        pl.semaphore_signal(nearby, inc=1, device_id=to_partner, device_id_type=MESH)

    pl.when(mid)(nearby_is_in)
    wires.start(("d", 1), dom.at[0, 0], dom.at[0, 1], to_mate)
    wires.start(("d", 2), dom.at[0, 0], dom.at[0, 2], to_across)
    for i in (2, 3, 0, 1):
        part = four(groups[i])
        wires.start(
            ("own across", i), c_ref.at[part], src.at[0, 2, part], to_across, None,
            ("own across", 0), c_ref,
        )
    for i in (1, 0, 2, 3):
        part = four(groups[i])
        wires.start(
            ("own mate", int(i == 1)), c_ref.at[part], src.at[0, 1, part], to_mate, None,
            ("own mate", 0), c_ref,
        )
    pl.when(end)(lambda: pl.semaphore_wait(nearby, 1))
    ready(0)
    from_mate()
    turn(1)
    ready(1)
    to_next(0)
    to_next(1)
    for load in (load_owner, load_slot, load_fock):
        load.wait()
    lax.fori_loop(0, quarter, table, 0)
    wires.wait(("d", 1), dom.at[0, 1])
    wires.wait(("d", 2), dom.at[0, 2])
    wires.start(("d", 3), dom.at[0, 2], dom.at[0, 3], to_mate)
    load_start.wait()
    lax.fori_loop(0, pc, cast, 0, unroll=2)
    wires.wait(("d", 3), dom.at[0, 3])
    for rel in range(4):
        for t in range(quarter):
            bdom[0, rel * quarter + t] = dom[0, rel, g * quarter + t]
    wires.start(("d", 4), dom.at[0], dom.at[1], to_partner)
    for kind in small:
        ready(kind)
    from_across(0)
    turn(2)
    got_first(0)
    got_second(0)
    expand(0, 0)
    from_across(1)
    from_corner()
    turn(3)
    to_next(2)
    share_partner(0, 0)
    share_partner(0, 1)
    to_next(3)
    for kind in late:
        ready(kind)
    got_first(1)
    got_second(1)
    from_across(2)
    from_next(0)
    from_mate_rest()
    expand(0, 1)
    from_across(3)
    from_next(1)
    for kind in small:
        got_first(kind)
    from_corner_rest()
    from_next_across(2)
    for kind in late:
        got_first(kind)
    expand(0, 2)
    from_next(2)
    expand(0, 3)
    for h in (0, 1):
        pass_partner(0, h)
    from_next_across(3)
    wires.wait(("d", 4), dom.at[1])
    from_next(3)
    for kind in small:
        got_second(kind)
    from_next_mate()
    expand(1, 0)
    from_next_across(0)
    make_turned(0)
    make_x(0, 0)
    for kind in ((2, 0), (2, 1)):
        got_second(kind)
    pass_across(0, 0)
    pass_across(0, 1)
    got_beside()
    make_turned(1)
    make_x(1, 0)
    for kind in ((3, 0),):
        got_second(kind)
    from_next_across(1)
    for kind in ((3, 1),):
        got_second(kind)
    expand(1, 1)
    have_partner(0)
    from_next_corner()
    expand(1, 2)
    expand(1, 3)
    make_x(1, 1)
    couple(1, 0, 0)
    couple(1, 1, 0)
    post(0, 0)
    make_turned(2)
    make_x(2, 0)
    make_x(2, 1)
    couple(2, 0, 0)
    couple(2, 1, 0)
    make_x(0, 1)
    got_beside2()
    make_turned(3)
    make_x(3, 0)
    make_x(3, 1)
    couple(3, 0, 0)
    couple(3, 1, 0)
    post(0, 1)
    couple(0, 0, 0)
    couple(0, 1, 0)
    for load in (load_k, load_e, load_shift):
        load.wait()
    sum_first(0)
    sum_second(0)

    for t in range(quarter):
        amps[1][0][g * quarter + t] = updated(0, t)
        if t % half_quarter == half_quarter - 1:
            h = t // half_quarter
            part = two(g, h)
            ref = amps[1][0].at[part]
            share_partner(1, h)
            wires.start(
                ("own", 1, h), ref, ref, to_across, None, ("own", 1), amps[1][0].at[four(g)]
            )
            wires.start(
                ("own", 2), ref, ref, to_mate, None, ("own", 2), both_quarters(amps[1][0])
            )
    for h in (0, 1):
        pass_partner(1, h)
        part = two(across, h)
        wires.wait(("own", 1, h), amps[1][0].at[part])
        ref = amps[1][0].at[part]
        wires.start(("own", 2), ref, ref, to_mate, None, ("own", 2), both_quarters(amps[1][0]))
    wires.wait(("own", 2), both_quarters(amps[1][0]))
    couple(3, 0, 1)
    couple(1, 0, 1)
    pass_across(1, 0)
    couple(2, 0, 1)
    pass_across(1, 1)
    couple(0, 0, 1)
    have_partner(1)
    couple(3, 1, 1)
    post(1, 1)
    couple(1, 1, 1)
    post(1, 0)
    couple(2, 1, 1)
    couple(0, 1, 1)
    sum_second(1)
    sum_first(1)

    for t in range(quarter):
        value = coupled(1, t).astype(BF16)
        mine[t] = value
        out_ref[g * quarter + t] = value
        if t % half_quarter == half_quarter - 1:
            h = t // half_quarter
            part = mine.at[pl.ds(h * half_quarter, half_quarter)]
            dst = out_ref.at[two(g, h)]
            wires.start(("out", 1, h), part, dst, to_across, None, ("out", 1), mine)
            wires.start(("out", 2), part, dst, to_mate, None, ("out", 2), both_quarters(out_ref))
    for h in (0, 1):
        ref = out_ref.at[two(across, h)]
        wires.wait(("out", 1, h), ref)
        wires.start(("out", 2), ref, ref, to_mate, None, ("out", 2), both_quarters(out_ref))
    wires.wait(("out", 2), both_quarters(out_ref))
    wires.drain()
    assert len(wires.sends) <= SENDS and len(wires.recvs) <= RECVS, (len(wires.sends), len(wires.recvs))


SENDS, RECVS = 45, 96


def quadrants_fit(n, groups, pc):
    return n == 2 * groups and groups == 4 and pc % (2 * groups) == 0


def quadrants_kernel(n, *refs):
    quadrants(n, *refs)


def quadrants_call(
    n, owner, slot, fock, shift, coefficients, domain, start, integrals, energy
):
    pc, rows, width = coefficients.shape
    quarter = pc // 4
    big, ways = (width, width), owner.shape[1]
    vmem, hbm = pl.BlockSpec(memory_space=pltpu.VMEM), pl.BlockSpec(memory_space=pl.ANY)
    dma = pltpu.SemaphoreType.DMA
    total = pl.pallas_call(
        functools.partial(quadrants_kernel, n),
        out_shape=jax.ShapeDtypeStruct((pc, *big), BF16),
        in_specs=[hbm] * 9,
        out_specs=vmem,
        scratch_shapes=[
            pltpu.SMEM((ways, pc), jnp.int32), pltpu.SMEM((ways, pc), jnp.int32),
            pltpu.SMEM((ways, pc), F32), pltpu.SMEM((pc,), F32),
            pltpu.VMEM((pc, rows, width), BF16), pltpu.VMEM((pc, rows), jnp.int32),
            pltpu.VMEM((pc, width), F32),
            pltpu.VMEM((2, 4, pc, rows, width), BF16),
            pltpu.VMEM((2, 4, pc, 1, rows), jnp.int32),
            pltpu.VMEM((6, 4, quarter, width, rows), BF16),
            pltpu.VMEM((6, 4 * quarter, 1, rows), jnp.int32),
            pltpu.SMEM((6, quarter, n), jnp.int32),
            pltpu.SMEM((6, quarter, n), F32),
            pltpu.VMEM((2, pc, 4 * NB, width), BF16),
            pltpu.VMEM((4, quarter, width, 4 * NB), BF16),
            pltpu.VMEM((4, quarter, 2, *big), BF16),
            pltpu.VMEM((pc, *big), F32),
            pltpu.VMEM((quarter, *big), F32),
            *[pltpu.VMEM((pc, *big), BF16)] * 4,
            pltpu.VMEM((4, quarter, *big), F32),
            pltpu.VMEM((2, 2, quarter, *big), BF16),
            pltpu.VMEM((2, 2, quarter, *big), BF16),
            pltpu.VMEM((2, 2, quarter, *big), BF16),
            pltpu.VMEM((2, 2, quarter, *big), BF16),
            pltpu.VMEM((quarter, *big), BF16),
            dma((SENDS,)), dma((RECVS,)), dma((9,)), pltpu.SemaphoreType.REGULAR,
        ],
        compiler_params=pltpu.CompilerParams(
            collective_id=0, has_side_effects=True, vmem_limit_bytes=60 * 2**20
        ),
        name="quadrants",
    )(owner.T, slot.T, fock.T, shift, coefficients, domain, start, integrals, energy)
    denominator = energy[:, :, None] + energy[:, None, :] + shift[:, None, None]
    return -(integrals + total.astype(F32)) / denominator


def on_device(
    coefficients, domain, coupling_owner, coupling_slot, coupling_fock,
    exchange_integrals, pno_energy, pair_shift, amplitudes_start,
):
    n = lax.axis_size("pairs")
    pc, rows, width = coefficients.shape
    quarter = pc // lax.axis_size("grp")
    steps = n // 2
    named = coupling_owner[:, :, None] == jnp.arange(n, dtype=jnp.int32)[None, None, :]
    slots = jnp.sum(jnp.where(named, coupling_slot[:, :, None], 0), axis=1)
    focks = jnp.sum(jnp.where(named, coupling_fock[:, :, None], 0.0), axis=1)
    focks = jnp.concatenate([focks, pair_shift[:, None]], axis=1)
    vmem, smem = pl.BlockSpec(memory_space=pltpu.VMEM), pl.BlockSpec(memory_space=pltpu.SMEM)
    dma = pltpu.SemaphoreType.DMA

    def params(collective):
        return pltpu.CompilerParams(
            collective_id=collective, has_side_effects=True, vmem_limit_bytes=60 * 2**20
        )

    if quadrants_fit(n, lax.axis_size("grp"), pc):
        return quadrants_call(
            n, coupling_owner, coupling_slot, coupling_fock, pair_shift, coefficients, domain,
            amplitudes_start, exchange_integrals, pno_energy,
        )

    big = (width, width)
    x_shape = jax.ShapeDtypeStruct((n, quarter, *big), BF16)
    block_scratch = [
        pltpu.VMEM((n, pc, rows, width), BF16),
        pltpu.VMEM((n, pc, rows), jnp.int32),
        pltpu.VMEM((pc, width, NB), BF16),
        pltpu.VMEM((pc, NB, width), BF16),
        pltpu.VMEM((2, 2 * quarter, *big), F32),
        pltpu.VMEM((2, 2 * quarter, *big), F32),
        pltpu.VMEM((n, 2 * quarter, *big), F32),
        pltpu.VMEM((2, quarter, *big), F32),
        pltpu.VMEM((n, quarter, *big), F32),
        pltpu.VMEM((n, quarter, *big), F32),
        dma((2, steps, 3)), dma((2, steps, 3)),
        dma((n,)), dma((n,)), dma((n,)), dma((n,)),
    ]
    amp_scratch = [
        pltpu.VMEM((n * pc, *big), BF16),
        pltpu.VMEM((pc, *big), BF16),
        pltpu.VMEM((quarter, *big), F32),
        pltpu.VMEM((quarter, *big), BF16),
        dma((2, steps, 4)), dma((2, steps, 4)),
        dma((n, 4)), dma((n, 4)), dma((n + 1,)), dma((n + 1,)), dma((3,)), dma((3,)),
    ]
    half_shape = jax.ShapeDtypeStruct((quarter, *big), BF16)

    def iterate(first, start, x):
        return pl.pallas_call(
            functools.partial(iteration_alone, n, first),
            out_shape=half_shape if first else jax.ShapeDtypeStruct((pc, *big), BF16),
            in_specs=[smem, smem, vmem, vmem, vmem, vmem],
            out_specs=vmem,
            scratch_shapes=amp_scratch,
            compiler_params=params(1 if first else 2),
            name="first" if first else "second",
        )(slots, focks, start, x, exchange_integrals, pno_energy)

    held = n * width * (2 * pc * (rows + width) + 4 * width * 4 * quarter + 2 * width * quarter)
    if held < 40 * 2**20:
        return pl.pallas_call(
            functools.partial(opening, n, len(block_scratch)),
            out_shape=jax.ShapeDtypeStruct((pc, *big), BF16),
            in_specs=[smem, smem, vmem, vmem, vmem, vmem, vmem],
            out_specs=vmem,
            scratch_shapes=[
                pltpu.VMEM(x_shape.shape, BF16), pltpu.VMEM(half_shape.shape, BF16),
                *block_scratch, *amp_scratch, *amp_scratch,
            ],
            compiler_params=params(0),
            name="amplitudes",
        )(slots, focks, coefficients, domain, amplitudes_start, exchange_integrals, pno_energy).astype(F32)
    else:
        x = pl.pallas_call(
            functools.partial(intersections_alone, n),
            out_shape=x_shape,
            in_specs=[smem, vmem, vmem],
            out_specs=vmem,
            scratch_shapes=block_scratch,
            compiler_params=params(0),
            name="intersections",
        )(slots, coefficients, domain)
        amps = iterate(True, amplitudes_start, x)
    return iterate(False, amps, x).astype(F32)


def solution(mesh):
    placed = (
        P("pairs", "grp", None),
        P("pairs", "grp"),
        P("pairs", None),
        P("pairs", None),
        P("pairs", None),
        P("pairs", None, None),
        P("pairs", None),
        P("pairs"),
        P("pairs", None, None),
    )
    return jax.shard_map(
        on_device, mesh=mesh, in_specs=placed, out_specs=P("pairs", None, None), check_vma=False
    )
```

```python
import functools

import jax
import jax.numpy as jnp
from jax import lax
from jax.experimental import pallas as pl
from jax.experimental.pallas import tpu as pltpu
from jax.sharding import PartitionSpec as P

NB = 192
MESH = pl.DeviceIdType.MESH
F32, BF16 = jnp.float32, jnp.bfloat16


def ring_position(rank, n):
    odd = rank % 2
    return (1 - odd) * (rank // 2) + odd * (n - 1 - rank // 2)


def ring_rank(position, n):
    back = position // (n // 2)
    return (1 - back) * 2 * position + back * (2 * (n - 1 - position) + 1)


def places(n):
    p, g = lax.axis_index("pairs"), lax.axis_index("grp")
    position = ring_position(p, n)
    core, half = g % 2, g // 2
    mate = 2 * half + (1 - core)
    across = 2 * (1 - half) + core
    return p, g, position, mate, across


def at(position, n):
    return ring_rank((position + n) % n, n)


def greet(peers):
    barrier = pltpu.get_barrier_semaphore()
    for peer in peers:
        pl.semaphore_signal(barrier, inc=1, device_id=peer, device_id_type=MESH)
    pl.semaphore_wait(barrier, len(peers))


def remote(src, dst, send, recv, peer):
    return pltpu.make_async_remote_copy(
        src_ref=src, dst_ref=dst, send_sem=send, recv_sem=recv, device_id=peer, device_id_type=MESH
    )


def ring_parts(steps, parts):
    def of(step, direction):
        if step < steps:
            return tuple(range(parts))
        return tuple(c for c in range(parts) if c % 2 == direction)

    return of


def intersections(
    n, slot_ref, c_ref, dom_ref, out_ref,
    cbuf, dbuf, turned, wide, own, msend, mrecv, ysend, yrecv, keep,
    rs, rr, ms, mr, ys, yr,
):
    p, g, position, mate, across = places(n)
    pc = c_ref.shape[0]
    quarter = pc // 4
    rows = c_ref.shape[1]
    steps = n // 2
    right, left = at(position + 1, n), at(position - 1, n)
    ring_peer = (lambda r: (r, g))
    peers = [(right, g), (left, g), (p, mate), (p, across)]
    greet(peers)
    parts_of = ring_parts(steps, 3)
    hp = pc // 2

    def part(ref_c, ref_d, c):
        if c == 2:
            return ref_d
        return ref_c.at[pl.ds(c * hp, hp)]

    def move(step, direction, c):
        offset = -(step - 1) if direction == 0 else step - 1
        rank = at(position + offset, n)
        if step == 1:
            src = part(c_ref, dom_ref, c)
        else:
            src = part(cbuf.at[rank], dbuf.at[rank], c)
        dst = part(cbuf.at[rank], dbuf.at[rank], c)
        return remote(
            src, dst, rs.at[direction, step - 1, c], rr.at[direction, step - 1, c],
            ring_peer(right if direction == 0 else left),
        )

    def arrive(step, direction, c):
        offset = -step if direction == 0 else step
        rank = at(position + offset, n)
        dst = part(cbuf.at[rank], dbuf.at[rank], c)
        remote(
            dst, dst, rs.at[direction, step - 1, c], rr.at[direction, step - 1, c],
            ring_peer(left if direction == 0 else right),
        ).wait_recv()

    for c in (2, 0, 1):
        for d in (0, 1):
            if c in parts_of(1, d):
                move(1, d, c).start()

    base = g * NB
    lines = lax.broadcasted_iota(jnp.int32, (NB, rows), 0)
    core, half = g % 2, g // 2

    def expand(block, doms):
        def one(s, carry):
            hit = (lines == (doms[pl.ds(s, 1), :] - base)).astype(F32).astype(BF16)
            wide[s] = jnp.dot(hit, block[s], preferred_element_type=F32).astype(BF16)
            return carry

        lax.fori_loop(0, pc, one, 0, unroll=8)

    def mate_copy(k, rank):
        return remote(msend.at[k % 2], mrecv.at[rank], ms.at[k], mr.at[k], (p, mate))

    def across_copy(k, rank):
        return remote(ysend.at[k % 2], yrecv.at[rank], ys.at[k], yr.at[k], (p, across))

    ranks = []

    def product(t, rank):
        return jnp.dot(turned[t], wide[slot_ref[t, rank]], preferred_element_type=F32)

    def links(k, rank):
        if k >= 2:
            mate_copy(k - 2, ranks[k - 2]).wait_send()

        def theirs(i, carry):
            t = (2 * (i // quarter) + 1 - core) * quarter + i % quarter
            msend[k % 2, i] = product(t, rank)
            return carry

        lax.fori_loop(0, 2 * quarter, theirs, 0, unroll=8)
        mate_copy(k, rank).start()

        def ours(i, carry):
            t = (2 * (i // quarter) + core) * quarter + i % quarter
            own[k % 2, i] = product(t, rank)
            return carry

        lax.fori_loop(0, 2 * quarter, ours, 0, unroll=8)

    def finish(k):
        rank = ranks[k]
        if k >= 2:
            across_copy(k - 2, ranks[k - 2]).wait_send()
        mate_copy(k, rank).wait_recv()

        def send(j, carry):
            i = (1 - half) * quarter + j
            ysend[k % 2, j] = own[k % 2, i] + mrecv[rank, i]
            return carry

        lax.fori_loop(0, quarter, send, 0)
        across_copy(k, rank).start()

        def hold(j, carry):
            i = half * quarter + j
            keep[rank, j] = own[k % 2, i] + mrecv[rank, i]
            return carry

        lax.fori_loop(0, quarter, hold, 0)

    def process(rank):
        k = len(ranks)
        ranks.append(rank)
        links(k, rank)

    expand(c_ref, dom_ref)

    def turn(t, carry):
        turned[t] = wide[t].astype(F32).T.astype(BF16)
        return carry

    lax.fori_loop(0, pc, turn, 0, unroll=2)
    process(p)
    finish(0)
    for step in range(1, steps + 1):
        for c in (2, 0, 1):
            for d in (0, 1):
                if c in parts_of(step, d):
                    arrive(step, d, c)
                if step < steps and c in parts_of(step + 1, d):
                    move(step + 1, d, c).start()
        if step == steps - 1:
            yield None
        for d in (0, 1) if step < steps else (0,):
            rank = at(position + (-step if d == 0 else step), n)
            expand(cbuf.at[rank], dbuf.at[rank])
            process(rank)
            if d == 1:
                finish(len(ranks) - 2)
        finish(len(ranks) - 1)
    def settle(k):
        rank = ranks[k]
        across_copy(k, rank).wait_recv()

        def last(j, carry):
            out_ref[rank, j] = (keep[rank, j] + yrecv[rank, j]).astype(BF16)
            return carry

        lax.fori_loop(0, quarter, last, 0)

    yield settle
    for k in (n - 2, n - 1):
        mate_copy(k, ranks[k]).wait_send()
        across_copy(k, ranks[k]).wait_send()
    for step in range(1, steps + 1):
        for d in (0, 1):
            for c in parts_of(step, d):
                move(step, d, c).wait_send()


def iteration(
    n, first, joined, alone, slot_ref, fock_ref, start_ref, x_ref, k_ref, e_ref, out_ref,
    abuf, stage, acc, mine, rs, rr, ms, mr, ys, yr, fs, fr,
):
    p, g, position, mate, across = places(n)
    pc = k_ref.shape[0]
    width = k_ref.shape[1]
    quarter = pc // 4
    eighth = quarter // 2
    steps = n // 2
    right, left = at(position + 1, n), at(position - 1, n)
    diagonal = 3 - g
    if alone:
        greet([(right, g), (left, g), (p, mate), (p, across)])
    parts = 4 if joined else 3
    parts_of = ring_parts(steps, parts)

    def chunk(rank, group, c):
        return abuf.at[pl.ds(rank * pc + group * quarter + (c % 2) * eighth, eighth)]

    def span(rank, c):
        return chunk(rank, g if c < 2 else across, c)

    def ring_copy(step, direction, c):
        offset = -(step - 1) if direction == 0 else step - 1
        ref = span(at(position + offset, n), c)
        src = ref
        if step == 1 and c < 2 and not first:
            src = start_ref.at[pl.ds(c * eighth, eighth)]
        return remote(
            src, ref, rs.at[direction, step - 1, c], rr.at[direction, step - 1, c],
            (right if direction == 0 else left, g),
        )

    def arrive(step, direction, c):
        offset = -step if direction == 0 else step
        ref = span(at(position + offset, n), c)
        remote(
            ref, ref, rs.at[direction, step - 1, c], rr.at[direction, step - 1, c],
            (left if direction == 0 else right, g),
        ).wait_recv()

    def mate_copy(k, rank, c, src=None):
        ref = span(rank, c)
        return remote(ref if src is None else src, ref, ms.at[k, c], mr.at[k, c], (p, mate))

    def mate_wait(k, rank):
        for c in range(4):
            ref = chunk(rank, mate if c < 2 else diagonal, c)
            remote(ref, ref, ms.at[k, c], mr.at[k, c], (p, mate)).wait_recv()

    def across_copy(k, rank, c=1, src=None):
        ref = span(rank, c)
        sem = k if c == 1 else n
        return remote(ref if src is None else src, ref, ys.at[sem], yr.at[sem], (p, across))

    def across_wait(k, rank, c=3):
        ref = span(rank, c)
        sem = k if c == 3 else n
        remote(ref, ref, ys.at[sem], yr.at[sem], (p, across)).wait_recv()

    def own_half(c):
        return start_ref.at[pl.ds(c * eighth, eighth)]

    if first:
        def copy_own(i, carry):
            abuf[p * pc + i] = start_ref[i].astype(BF16)
            return carry

        def group_in(group):
            lax.fori_loop(group * quarter, (group + 1) * quarter, copy_own, 0)

        group_in(g)
        for c in (0, 1):
            for d in (0, 1):
                if c in parts_of(1, d):
                    ring_copy(1, d, c).start()
        group_in(across)
        for c in range(2, parts):
            for d in (0, 1):
                if c in parts_of(1, d):
                    ring_copy(1, d, c).start()
        group_in(mate)
        group_in(diagonal)
    else:
        for c in (0, 1):
            across_copy(0, p, c, own_half(c)).start()
            for d in (0, 1):
                if c in parts_of(1, d):
                    ring_copy(1, d, c).start()
        for c in (0, 1):
            mate_copy(0, p, c, own_half(c)).start()

        def copy_own(i, carry):
            abuf[p * pc + g * quarter + i] = start_ref[i]
            return carry

        lax.fori_loop(0, quarter, copy_own, 0)
        across_wait(0, p, 2)
        for d in (0, 1):
            if 2 in parts_of(1, d):
                ring_copy(1, d, 2).start()
        mate_copy(0, p, 2).start()
        across_wait(0, p, 3)
        mate_copy(0, p, 3).start()
        mate_wait(0, p)

    settle = yield None
    acc[...] = jnp.zeros_like(acc)

    def couple(rank, k):
        if settle is not None:
            settle(k)

        def copy(i, carry):
            stage[i] = abuf[rank * pc + i]
            return carry

        lax.fori_loop(0, pc, copy, 0, unroll=4)

        def one(j, carry):
            t = g * quarter + j
            source = stage[slot_ref[t, rank]]
            x = x_ref[rank, j]
            h = jnp.dot(x, source, preferred_element_type=F32).astype(BF16)
            y = lax.dot_general(h, x, (((1,), (1,)), ((), ())), preferred_element_type=F32)
            acc[j] += fock_ref[t, rank] * y
            return carry

        lax.fori_loop(0, quarter, one, 0, unroll=4)

    couple(p, 0)

    def exchange(blocks):
        for k, rank in () if joined else blocks:
            across_wait(k, rank)
            mate_copy(k, rank, 3).start()

    def use(blocks):
        for k, rank in blocks:
            mate_wait(k, rank)
            couple(rank, k)

    landed, shared = [], []
    for step in range(1, steps + 1):
        for c in (1, 0, 2, 3)[:parts]:
            for d in (0, 1):
                rank = at(position + (-step if d == 0 else step), n)
                if c in parts_of(step, d):
                    arrive(step, d, c)
                    if step < steps and c in parts_of(step + 1, d):
                        ring_copy(step + 1, d, c).start()
                    k = 2 * step - 1 + (d if step < steps else 0)
                    if c == 1 and not joined:
                        across_copy(k, rank).start()
                    mate_copy(k, rank, c).start()
        exchange(landed)
        use(shared)
        shared = landed
        landed = [
            (2 * step - 1 + d, at(position + (-step if d == 0 else step), n))
            for d in ((0, 1) if step < steps else (0,))
        ]
    exchange(landed)
    use(shared)
    use(landed)

    def scaled(j):
        t = g * quarter + j
        row = jnp.broadcast_to(e_ref[pl.ds(t, 1), :], (width, width))
        return (-(k_ref[t] + acc[j]) / (row.T + row + fock_ref[t, n])).astype(BF16)

    if first:
        def result(j, carry):
            out_ref[j] = scaled(j)
            return carry

        lax.fori_loop(0, quarter, result, 0, unroll=2)
    else:
        def block(ref, group):
            return ref.at[pl.ds(group * quarter, quarter)]

        def result(j, carry):
            value = scaled(j)
            mine[j] = value
            out_ref[g * quarter + j] = value
            return carry

        lax.fori_loop(0, quarter, result, 0, unroll=2)
        over = remote(mine, block(out_ref, g), fs.at[0], fr.at[0], (p, across))
        beside = remote(mine, block(out_ref, g), fs.at[1], fr.at[1], (p, mate))
        corner = remote(
            block(out_ref, across), block(out_ref, across), fs.at[2], fr.at[2], (p, mate)
        )
        over.start()
        beside.start()
        remote(mine, block(out_ref, across), fs.at[0], fr.at[0], (p, across)).wait_recv()
        corner.start()
        remote(mine, block(out_ref, mate), fs.at[1], fr.at[1], (p, mate)).wait_recv()
        remote(mine, block(out_ref, diagonal), fs.at[2], fr.at[2], (p, mate)).wait_recv()
        over.wait_send()
        beside.wait_send()
        corner.wait_send()
        across_copy(0, p, 0, own_half(0)).wait_send()
        across_copy(0, p, 1, own_half(1)).wait_send()
        for c in range(4):
            mate_copy(0, p, c).wait_send()
    for k in range(1, n):
        if not joined:
            across_copy(k, p).wait_send()
        for c in range(4):
            mate_copy(k, p, c).wait_send()
    for step in range(1, steps + 1):
        for d in (0, 1):
            for c in parts_of(step, d):
                ring_copy(step, d, c).wait_send()


def intersections_alone(*args):
    steps = intersections(*args)
    next(steps)
    settle = next(steps)
    for k in range(args[0]):
        settle(k)
    next(steps, None)


def iteration_alone(n, first, *args):
    steps = iteration(n, first, False, True, *args)
    next(steps)
    try:
        steps.send(None)
    except StopIteration:
        pass


def opening(
    n, made, slot_ref, fock_ref, c_ref, dom_ref, start_ref, k_ref, e_ref, out_ref,
    x_ref, amp_ref, *scratch
):
    used = made + (len(scratch) - made) // 2
    blocks = intersections(n, slot_ref, c_ref, dom_ref, x_ref, *scratch[:made])
    next(blocks)
    amps = iteration(
        n, True, True, False, slot_ref, fock_ref, start_ref, x_ref, k_ref, e_ref, amp_ref,
        *scratch[made:used],
    )
    next(amps)
    settle = next(blocks)
    try:
        amps.send(settle)
    except StopIteration:
        pass
    amps = iteration(
        n, False, False, False, slot_ref, fock_ref, amp_ref, x_ref, k_ref, e_ref, out_ref,
        *scratch[used:],
    )
    next(amps)
    try:
        amps.send(None)
    except StopIteration:
        pass
    next(blocks, None)


class Wires:
    def __init__(self, send, recv, here):
        self.send, self.recv, self.here = send, recv, here
        self.sends, self.recvs, self.wholes = {}, {}, {}

    def link(self, key, src, dst, peer, out=None):
        out = key if out is None else out
        at_send = self.sends.setdefault(out, len(self.sends))
        at_recv = self.recvs.setdefault(key, len(self.recvs))
        return remote(src, dst, self.send.at[at_send], self.recv.at[at_recv], peer)

    def start_in(self, when, key, src, dst, peer, out=None, whole=None):
        self.link(key, src, dst, peer, out).start()
        out = key if out is None else out
        role = 0 if when is None else 1 + (when is self.mid)
        self.wholes[out, role] = (src if whole is None else whole, when)

    def start(self, key, src, dst, peer, when=None, out=None, whole=None):
        def run():
            self.start_in(when, key, src, dst, peer, out, whole)

        if when is None:
            run()
        else:
            pl.when(when)(run)

    def start_all(self, when, jobs):
        def run():
            for job in jobs:
                self.start_in(when, *job)

        pl.when(when)(run)

    def wait(self, key, dst, when=None):
        at_recv = self.recvs.setdefault(key, len(self.recvs))
        copy = remote(dst, dst, self.send.at[0], self.recv.at[at_recv], self.here)
        if when is None:
            copy.wait_recv()
        else:
            pl.when(when)(copy.wait_recv)

    def drain(self):
        for (out, _), (whole, when) in self.wholes.items():
            at_send = self.sends[out]
            copy = remote(whole, whole, self.send.at[at_send], self.recv.at[0], self.here)
            if when is None:
                copy.wait_send()
            else:
                pl.when(when)(copy.wait_send)


def note(*what):
    return None


def quadrants(
    n, owner_hbm, slot_hbm, fock_hbm, shift_hbm, c_hbm, dom_hbm, start_ref, k_ref, e_hbm, out_ref,
    owner_ref, slot_ref, fock_ref, shift_ref, c_ref, dom_ref, e_ref, src, dom, blocks, bdom, bslot, bfock, wide, turned, x, start, k_own, amps_a, amps_b, amps_c, amps_d,
    acc, yout, yx, ysum, yin, mine, send, recv, local,
):
    p, g = lax.axis_index("pairs"), lax.axis_index("grp")
    pc, rows, width = c_ref.shape
    quarter = pc // 4
    half_quarter = quarter // 2
    layers = n // 2
    layer, column = p // 2, p % 2
    inner = (layer % 2 + layer // 2) % 2
    mid, end = inner == 1, inner == 0
    partner = (layer + 1 - 2 * (layer % 2)) * 2 + column
    cross = (layers - 1 - layer) * 2 + column
    far = ((layer + layers // 2) % layers) * 2 + column
    beside = layer * 2 + 1 - column
    groups = (g, g + 1 - 2 * (g % 2), (g + 2) % 4, 3 - g)
    _, mate, across, diagonal = groups
    to_mate, to_across = (p, mate), (p, across)
    to_partner, to_cross, to_beside, to_far = (partner, g), (cross, g), (beside, g), (far, g)
    wires = Wires(send, recv, to_mate)
    amps = ((amps_a, amps_b), (amps_c, amps_d))
    wires.mid = mid

    barrier = pltpu.get_barrier_semaphore()

    def hello(peer):
        pl.semaphore_signal(barrier, inc=1, device_id=peer, device_id_type=MESH)

    for peer in (to_partner, to_beside, to_across, to_mate):
        hello(peer)
    pl.when(mid)(lambda: hello(to_cross))

    pairs = (
        (c_hbm, c_ref), (dom_hbm, dom_ref), (owner_hbm, owner_ref), (slot_hbm, slot_ref),
        (fock_hbm, fock_ref), (shift_hbm, shift_ref), (e_hbm, e_ref), (start_ref, start),
        (k_ref.at[pl.ds(g * quarter, quarter)], k_own),
    )
    loads = [pltpu.make_async_copy(*pair, local.at[i]) for i, pair in enumerate(pairs)]
    for load in loads:
        load.start()
    load_c, load_dom, load_owner, load_slot, load_fock, load_shift, load_e, load_start, load_k = loads
    load_c.wait()
    load_dom.wait()

    def four(group):
        return pl.ds(group * quarter, quarter)

    def two(group, h):
        return pl.ds(group * quarter + h * half_quarter, half_quarter)

    def both_quarters(ref):
        return ref.at[pl.ds(0, 2 * quarter)]

    def three_quarters(ref):
        return ref.at[pl.ds(0, 3 * quarter)]

    def source(b, rel):
        return c_ref if (b, rel) == (0, 0) else src.at[b, rel]

    def turn(rel, b=0):
        for t in range(quarter):
            blocks[b, rel, t] = source(b, rel)[g * quarter + t].T

    for s in range(pc):
        dom[0, 0, s] = dom_ref[pl.ds(s, 1), :]
    turn(0)

    def table(t, carry):
        at_pair = g * quarter + t
        ways = owner_ref.shape[0]
        named = [owner_ref[k, at_pair] for k in range(ways)]
        slots = [slot_ref[k, at_pair] for k in range(ways)]
        focks = [fock_ref[k, at_pair] for k in range(ways)]
        for owner in range(n):
            place, weight = 0, 0.0
            for k in range(ways):
                hit = named[k] == owner
                place = jnp.where(hit, slots[k], place)
                weight = jnp.where(hit, focks[k], weight)
            bslot[0, t, owner] = place
            bfock[0, t, owner] = weight
        return carry

    small = ("slot", "fock", "dom")
    kinds = {
        "slot": lambda b: bslot.at[b],
        "fock": lambda b: bfock.at[b],
        "dom": lambda b: bdom.at[b],
    }
    for rel in range(4):
        for h in (0, 1):
            kinds[rel, h] = functools.partial(
                lambda rel, h, b: blocks.at[b, rel, pl.ds(h * half_quarter, half_quarter)], rel, h
            )
        kinds[rel] = functools.partial(lambda rel, b: blocks.at[b, rel], rel)

    def grouped(kind, ref):
        return (ref, kind) if kind in small else (blocks.at[0], 0)

    def ready(kind):
        ref = kinds[kind](0)
        whole, tag = grouped(kind, ref)
        together = ("beside", tag)
        if kind in ("slot", "fock"):
            wires.start(("second", kind), ref, kinds[kind](1), to_partner)
        wires.start_all(end, [(together, ref, kinds[kind](4), to_beside, together, whole)])
        wires.start_all(
            mid, [(("cross", kind), ref, kinds[kind](2), to_cross, ("cross", tag), whole)]
        )

    def next_ready(kind):
        ref = kinds[kind](1)
        whole, tag = grouped(kind, ref)
        together = ("beside2", tag)
        if kind in ("slot", "fock"):
            wires.wait(("second", kind), ref)
        wires.start_all(end, [(together, ref, kinds[kind](5), to_beside, together, whole)])
        wires.start_all(
            mid, [(("further", kind), ref, kinds[kind](3), to_cross, ("further", tag), whole)]
        )

    first, second = 2 * inner, 1 + 2 * inner

    def got_first(kind):
        landed, passed = kinds[kind](2), kinds[kind](4)
        whole, tag = grouped(kind, landed)
        together = ("beside", tag)

        def relay():
            wires.wait(("cross", kind), landed)
            wires.start_in(mid, together, landed, passed, to_beside, together, whole)

        pl.when(mid)(relay)

    def got_further(kind):
        landed, passed = kinds[kind](3), kinds[kind](5)
        whole, tag = grouped(kind, landed)
        together = ("beside2", tag)

        def relay():
            wires.wait(("further", kind), landed)
            wires.start_in(mid, together, landed, passed, to_beside, together, whole)

        pl.when(mid)(relay)

    def got_beside():
        for kind in small:
            wires.wait(("beside", kind), kinds[kind](4))
        wires.wait(("beside", 0), blocks.at[4])

    def got_beside2():
        for kind in small:
            wires.wait(("beside2", kind), kinds[kind](5))
        wires.wait(("beside2", 0), blocks.at[5])

    places_of = (first, 4, second, 5)

    lines = lax.broadcasted_iota(jnp.int16, (NB, rows), 0)
    lines2 = lax.broadcasted_iota(jnp.int16, (2 * NB, 2 * rows), 0)

    def one_hot(numbers, row):
        hit = numbers == row.astype(jnp.int16)
        return jnp.where(hit, jnp.ones(hit.shape, BF16), jnp.zeros(hit.shape, BF16))

    def expand(b, rel, parts=(0, 1, 2, 3)):
        base = groups[rel] * NB
        block = source(b, rel)

        def one(s, carry):
            hit = one_hot(lines, dom[b, rel, s] - base)
            wide[b, s, pl.ds(rel * NB, NB)] = jnp.dot(
                hit, block[s], preferred_element_type=F32
            ).astype(BF16)
            return carry

        if len(parts) == 4:
            note("expand", b, rel)
            lax.fori_loop(0, pc, one, 0, unroll=4)
            return
        for i in parts:
            note("expand4", b, rel)
            for t in range(quarter):
                one(groups[i] * quarter + t, 0)

    def make_turned(b, hs=(0, 1)):
        note("make_turned", b)
        place = places_of[b]

        def one(t, carry):
            for h in hs:
                u, v = 2 * h, 2 * h + 1
                row = jnp.concatenate(
                    [
                        bdom[place, u * quarter + t] - groups[u] * NB,
                        bdom[place, v * quarter + t] - groups[v] * NB + NB,
                    ],
                    axis=1,
                )
                hit = one_hot(lines2, row)
                both = jnp.concatenate([blocks[place, u, t], blocks[place, v, t]], axis=1)
                turned[b, t, :, pl.ds(h * 2 * NB, 2 * NB)] = lax.dot_general(
                    both, hit, (((1,), (1,)), ((), ())), preferred_element_type=F32
                ).astype(BF16)
            return carry

        lax.fori_loop(0, quarter, one, 0, unroll=2)

    owners = (p, partner)

    def make_x(b, s):
        note("make_x", b, s)
        place = places_of[b]

        def one(t, carry):
            at_source = bslot[place, t, owners[s]]
            x[b, t, s] = jnp.dot(
                turned[b, t], wide[s, at_source], preferred_element_type=F32
            ).astype(BF16)
            return carry

        lax.fori_loop(0, quarter, one, 0, unroll=4)

    def couple(b, s, it):
        note("couple", b, s)
        place = places_of[b]
        found = []
        for t in range(quarter):
            at_source = bslot[place, t, owners[s]]
            xs = x[b, t, s]
            half = jnp.dot(xs, amps[it][s][at_source], preferred_element_type=F32).astype(BF16)
            found.append((t, xs, half))
        for t, xs, half in found:
            y = lax.dot_general(half, xs, (((1,), (1,)), ((), ())), preferred_element_type=F32)
            y = bfock[place, t, owners[s]] * y
            if s == 0:
                acc[b, t] = y
            elif b % 2 == 0:
                acc[b, t] += y
            else:
                yout[it, b // 2, t] = (acc[b, t] + y).astype(BF16)

    def post(it, m):
        for t in range(quarter):
            wires.start(
                ("y", it, m, t), yout.at[it, m, t], yx.at[it, m, t], to_beside, None,
                ("y", it, m), yout.at[it, m],
            )

    def share(t):
        at_pair = g * quarter + t
        ref, part = amps[1][0].at[at_pair], amps[1][0].at[four(g)]
        wires.start(("a", 1, 0, t), ref, amps[1][1].at[at_pair], to_partner, None, ("a", 1, 0), part)
        wires.start(("own", 1, t), ref, ref, to_across, None, ("own", 1), part)
        wires.start(("own", 2), ref, ref, to_mate, None, ("own", 2), both_quarters(amps[1][0]))

    def pass_partner(t):
        ref, part = amps[1][1].at[g * quarter + t], amps[1][1].at[four(g)]
        wires.wait(("a", 1, 0, t), ref)
        wires.start(("a", 1, 1, t), ref, ref, to_across, None, ("a", 1, 1), part)
        wires.start(("a", 1, 2), ref, ref, to_mate, None, ("a", 1, 2), both_quarters(amps[1][1]))

    def pass_own(t):
        ref = amps[1][0].at[across * quarter + t]
        wires.wait(("own", 1, t), ref)
        wires.start(("own", 2), ref, ref, to_mate, None, ("own", 2), both_quarters(amps[1][0]))

    def pass_across(t):
        ref = amps[1][1].at[across * quarter + t]
        wires.wait(("a", 1, 1, t), ref)
        wires.start(("a", 1, 2), ref, ref, to_mate, None, ("a", 1, 2), both_quarters(amps[1][1]))

    def share_start(j):
        part = four((g, across)[j])
        wires.start(
            ("start", j), amps[0][0].at[part], amps[0][1].at[part], to_partner, None,
            ("start", 0), both_quarters(amps[0][0]),
        )

    def pass_start(j):
        ref = amps[0][1].at[four((g, across)[j])]
        wires.wait(("start", j), ref)
        wires.start(("a", 0, 2), ref, ref, to_mate, None, ("a", 0, 2), both_quarters(amps[0][1]))

    def have_partner(it):
        wires.wait(("a", it, 2), both_quarters(amps[it][1]))

    def sum_second(it):
        for t in range(quarter):
            wires.wait(("y", it, 1, t), yx.at[it, 1, t])
            ysum[it, 1, t] = (acc[2, t] + yx[it, 1, t].astype(F32)).astype(BF16)
            job = (("yfar", it, t), ysum.at[it, 1, t], yin.at[it, 0, t])
            group = (("yfar", it), ysum.at[it, 1])
            wires.start_all(end, [(*job, to_partner, *group)])
            wires.start_all(mid, [(*job, to_far, *group)])

    def sum_first(it):
        for t in range(quarter):
            wires.wait(("y", it, 0, t), yx.at[it, 0, t])
            total = acc[0, t] + yx[it, 0, t].astype(F32)
            acc[0, t] = total
            ysum[it, 0, t] = total.astype(BF16)
            wires.start_all(mid, [(
                ("ynear", it, t), ysum.at[it, 0, t], yin.at[it, 1, t], to_cross,
                ("ynear", it), ysum.at[it, 0],
            )])

    def coupled(it, t):
        wires.wait(("ynear", it, t), yin.at[it, 1, t], mid)
        wires.wait(("yfar", it, t), yin.at[it, 0, t])
        near = yin[it, 1, t].astype(F32)
        return yin[it, 0, t].astype(F32) + jnp.where(mid, near, acc[0, t])

    def updated(it, t):
        at_pair = g * quarter + t
        total = coupled(it, t)
        row = jnp.broadcast_to(e_ref[pl.ds(at_pair, 1), :], (width, width))
        return (-(k_own[t] + total) / (row.T + row + shift_ref[at_pair])).astype(BF16)

    swap_mate, swap_across = (1, 0, 3, 2), (2, 3, 0, 1)

    def from_mate():
        wires.wait(("own mate", 1), src.at[0, 1, four(g)])

    def from_mate_rest():
        wires.wait(("own mate", 0), three_quarters(src.at[0, 1]))

    def from_across(i):
        part = four(groups[i])
        wires.wait(("own across", swap_across[i]), src.at[0, 2, part])
        wires.start(
            ("own corner", int(i == 1)), src.at[0, 2, part], src.at[0, 3, part], to_mate, None,
            ("own corner", 0), src.at[0, 2],
        )

    def from_corner():
        wires.wait(("own corner", 1), src.at[0, 3, four(g)])

    def from_corner_rest():
        wires.wait(("own corner", 0), three_quarters(src.at[0, 3]))

    def to_next(i):
        part = four(groups[i])
        wires.start(
            ("next", i), c_ref.at[part], src.at[1, 0, part], to_partner, None, ("next", 0), c_ref
        )

    def from_next(i):
        part = four(groups[i])
        ref = src.at[1, 0, part]
        wires.wait(("next", i), ref)
        if i in (2, 3):
            wires.start(
                ("next across", i), ref, src.at[1, 2, part], to_across, None,
                ("next across", 0), both_quarters(src.at[1, 0]),
            )
        wires.start(
            ("next mate", int(i == 1)), ref, src.at[1, 1, part], to_mate, None,
            ("next mate", 0), src.at[1, 0],
        )

    def to_wide(i):
        part = four(groups[i])
        wires.start(
            ("next wide", i), src.at[0, 2, part], src.at[1, 2, part], to_partner, None,
            ("next wide", 0), both_quarters(src.at[0, 2]),
        )

    def corner(i):
        part = four(groups[i])
        wires.start(
            ("next corner", int(i == 1)), src.at[1, 2, part], src.at[1, 3, part], to_mate, None,
            ("next corner", 0), src.at[1, 2],
        )

    def from_next_across(i):
        wires.wait(("next across", swap_across[i]), src.at[1, 2, four(groups[i])])
        corner(i)

    def from_wide(i):
        wires.wait(("next wide", i), src.at[1, 2, four(groups[i])])
        corner(i)

    def from_next_mate():
        wires.wait(("next mate", 1), src.at[1, 1, four(g)])

    def from_next_mate_rest():
        wires.wait(("next mate", 0), three_quarters(src.at[1, 1]))

    def from_next_corner():
        wires.wait(("next corner", 1), src.at[1, 3, four(g)])

    def from_next_corner_rest():
        wires.wait(("next corner", 0), three_quarters(src.at[1, 3]))

    def own_across(i):
        part = four(groups[i])
        wires.start(
            ("own across", i), c_ref.at[part], src.at[0, 2, part], to_across, None,
            ("own across", 0), c_ref,
        )

    def cast(s, carry):
        amps[0][0][s] = start[s].astype(BF16)
        return carry

    pl.semaphore_wait(barrier, 4 + inner)
    wires.start(("d", 1), dom.at[0, 0], dom.at[0, 1], to_mate)
    wires.start(("d", 2), dom.at[0, 0], dom.at[0, 2], to_across)
    own_across(2)
    to_next(0)
    ready(0)
    for i in (1, 0, 2, 3):
        part = four(groups[i])
        wires.start(
            ("own mate", int(i == 1)), c_ref.at[part], src.at[0, 1, part], to_mate, None,
            ("own mate", 0), c_ref,
        )
    own_across(3)
    own_across(0)
    for i in (2, 3, 1):
        to_next(i)
    from_mate()
    turn(1)
    ready(1)
    wires.wait(("d", 1), dom.at[0, 1])
    wires.wait(("d", 2), dom.at[0, 2])
    wires.start(("d", 3), dom.at[0, 2], dom.at[0, 3], to_mate)
    for load in (load_owner, load_slot, load_fock):
        load.wait()
    lax.fori_loop(0, quarter, table, 0)
    ready("slot")
    ready("fock")
    wires.wait(("d", 3), dom.at[0, 3])
    for rel in range(4):
        for t in range(quarter):
            bdom[0, rel * quarter + t] = dom[0, rel, g * quarter + t]
    ready("dom")
    wires.start(("d", 4), dom.at[0], dom.at[1], to_partner)
    from_next(0)
    turn(0, 1)
    next_ready(0)
    got_first(0)
    from_across(0)
    turn(2)
    ready(2)
    expand(0, 0)
    from_next(2)
    own_across(1)
    from_across(1)
    got_first(1)
    from_corner()
    turn(3)
    ready(3)
    load_start.wait()
    lax.fori_loop(0, pc, cast, 0, unroll=2)
    from_next(3)
    from_across(2)
    to_wide(2)
    share_start(0)
    got_further(0)
    from_mate_rest()
    expand(0, 1)
    from_next(1)
    from_next_across(0)
    turn(2, 1)
    next_ready(2)
    from_next_mate()
    turn(1, 1)
    next_ready(1)
    got_first(2)
    from_across(3)
    to_wide(3)
    share_start(1)
    for kind in small:
        got_first(kind)
    wires.wait(("d", 4), dom.at[1])
    for rel in range(4):
        for t in range(quarter):
            bdom[1, rel * quarter + t] = dom[1, rel, g * quarter + t]
    next_ready("dom")
    next_ready("slot")
    next_ready("fock")
    got_first(3)
    from_wide(2)
    from_next_across(1)
    from_corner_rest()
    expand(0, 2)
    from_next_corner()
    turn(3, 1)
    next_ready((3, 0))
    next_ready((3, 1))
    pass_start(0)
    got_further(2)
    expand(0, 3)
    for kind in small:
        got_further(kind)
    make_turned(0)
    make_x(0, 0)
    got_further(1)
    from_wide(3)
    expand(1, 0)
    from_next_mate_rest()
    expand(1, 1)
    from_next_corner_rest()
    expand(1, 2)
    pass_start(1)
    got_beside()
    got_further((3, 0))
    expand(1, 3)
    got_further((3, 1))
    make_x(0, 1)
    make_turned(1)
    make_x(1, 0)
    make_x(1, 1)
    have_partner(0)
    couple(1, 0, 0)
    couple(1, 1, 0)
    post(0, 0)
    make_turned(2)
    make_x(2, 0)
    make_x(2, 1)
    couple(2, 0, 0)
    couple(2, 1, 0)
    couple(0, 0, 0)
    couple(0, 1, 0)
    got_beside2()
    make_turned(3)
    make_x(3, 0)
    make_x(3, 1)
    couple(3, 0, 0)
    couple(3, 1, 0)
    post(0, 1)
    for load in (load_k, load_e, load_shift):
        load.wait()
    sum_first(0)
    sum_second(0)

    for t in range(quarter):
        amps[1][0][g * quarter + t] = updated(0, t)
        share(t)
    for t in range(quarter):
        pass_partner(t)
        pass_own(t)
    wires.wait(("own", 2), both_quarters(amps[1][0]))
    couple(3, 0, 1)
    couple(1, 0, 1)
    for t in range(half_quarter):
        pass_across(t)
    couple(2, 0, 1)
    couple(0, 0, 1)
    for t in range(half_quarter, quarter):
        pass_across(t)
    have_partner(1)
    couple(3, 1, 1)
    post(1, 1)
    couple(1, 1, 1)
    post(1, 0)
    couple(2, 1, 1)
    couple(0, 1, 1)
    sum_second(1)
    sum_first(1)

    for t in range(quarter):
        value = coupled(1, t).astype(BF16)
        mine[t] = value
        out_ref[g * quarter + t] = value
        part, dst = mine.at[t], out_ref.at[g * quarter + t]
        wires.start(("out", 1, t), part, dst, to_across, None, ("out", 1), mine)
        wires.start(("out", 2), part, dst, to_mate, None, ("out", 2), both_quarters(out_ref))
    for t in range(quarter):
        ref = out_ref.at[across * quarter + t]
        wires.wait(("out", 1, t), ref)
        wires.start(("out", 2), ref, ref, to_mate, None, ("out", 2), both_quarters(out_ref))
    wires.wait(("out", 2), both_quarters(out_ref))
    wires.drain()
    assert len(wires.sends) <= SENDS and len(wires.recvs) <= RECVS, (len(wires.sends), len(wires.recvs))


SENDS, RECVS = 50, 120


def quadrants_fit(n, groups, pc):
    return n == 2 * groups and groups == 4 and pc % (2 * groups) == 0


def quadrants_kernel(n, *refs):
    quadrants(n, *refs)


def quadrants_call(
    n, owner, slot, fock, shift, coefficients, domain, start, integrals, energy
):
    pc, rows, width = coefficients.shape
    quarter = pc // 4
    big, ways = (width, width), owner.shape[1]
    vmem, hbm = pl.BlockSpec(memory_space=pltpu.VMEM), pl.BlockSpec(memory_space=pl.ANY)
    dma = pltpu.SemaphoreType.DMA
    total = pl.pallas_call(
        functools.partial(quadrants_kernel, n),
        out_shape=jax.ShapeDtypeStruct((pc, *big), BF16),
        in_specs=[hbm] * 9,
        out_specs=vmem,
        scratch_shapes=[
            pltpu.SMEM((ways, pc), jnp.int32), pltpu.SMEM((ways, pc), jnp.int32),
            pltpu.SMEM((ways, pc), F32), pltpu.SMEM((pc,), F32),
            pltpu.VMEM((pc, rows, width), BF16), pltpu.VMEM((pc, rows), jnp.int32),
            pltpu.VMEM((pc, width), F32),
            pltpu.VMEM((2, 4, pc, rows, width), BF16),
            pltpu.VMEM((2, 4, pc, 1, rows), jnp.int32),
            pltpu.VMEM((6, 4, quarter, width, rows), BF16),
            pltpu.VMEM((6, 4 * quarter, 1, rows), jnp.int32),
            pltpu.SMEM((6, quarter, n), jnp.int32),
            pltpu.SMEM((6, quarter, n), F32),
            pltpu.VMEM((2, pc, 4 * NB, width), BF16),
            pltpu.VMEM((4, quarter, width, 4 * NB), BF16),
            pltpu.VMEM((4, quarter, 2, *big), BF16),
            pltpu.VMEM((pc, *big), F32),
            pltpu.VMEM((quarter, *big), F32),
            *[pltpu.VMEM((pc, *big), BF16)] * 4,
            pltpu.VMEM((4, quarter, *big), F32),
            pltpu.VMEM((2, 2, quarter, *big), BF16),
            pltpu.VMEM((2, 2, quarter, *big), BF16),
            pltpu.VMEM((2, 2, quarter, *big), BF16),
            pltpu.VMEM((2, 2, quarter, *big), BF16),
            pltpu.VMEM((quarter, *big), BF16),
            dma((SENDS,)), dma((RECVS,)), dma((9,)),
        ],
        compiler_params=pltpu.CompilerParams(
            collective_id=0, has_side_effects=True, vmem_limit_bytes=60 * 2**20
        ),
        name="quadrants",
    )(owner.T, slot.T, fock.T, shift, coefficients, domain, start, integrals, energy)
    denominator = energy[:, :, None] + energy[:, None, :] + shift[:, None, None]
    return -(integrals + total.astype(F32)) / denominator


def on_device(
    coefficients, domain, coupling_owner, coupling_slot, coupling_fock,
    exchange_integrals, pno_energy, pair_shift, amplitudes_start,
):
    n = lax.axis_size("pairs")
    pc, rows, width = coefficients.shape
    quarter = pc // lax.axis_size("grp")
    steps = n // 2
    named = coupling_owner[:, :, None] == jnp.arange(n, dtype=jnp.int32)[None, None, :]
    slots = jnp.sum(jnp.where(named, coupling_slot[:, :, None], 0), axis=1)
    focks = jnp.sum(jnp.where(named, coupling_fock[:, :, None], 0.0), axis=1)
    focks = jnp.concatenate([focks, pair_shift[:, None]], axis=1)
    vmem, smem = pl.BlockSpec(memory_space=pltpu.VMEM), pl.BlockSpec(memory_space=pltpu.SMEM)
    dma = pltpu.SemaphoreType.DMA

    def params(collective):
        return pltpu.CompilerParams(
            collective_id=collective, has_side_effects=True, vmem_limit_bytes=60 * 2**20
        )

    if quadrants_fit(n, lax.axis_size("grp"), pc):
        return quadrants_call(
            n, coupling_owner, coupling_slot, coupling_fock, pair_shift, coefficients, domain,
            amplitudes_start, exchange_integrals, pno_energy,
        )

    big = (width, width)
    x_shape = jax.ShapeDtypeStruct((n, quarter, *big), BF16)
    block_scratch = [
        pltpu.VMEM((n, pc, rows, width), BF16),
        pltpu.VMEM((n, pc, rows), jnp.int32),
        pltpu.VMEM((pc, width, NB), BF16),
        pltpu.VMEM((pc, NB, width), BF16),
        pltpu.VMEM((2, 2 * quarter, *big), F32),
        pltpu.VMEM((2, 2 * quarter, *big), F32),
        pltpu.VMEM((n, 2 * quarter, *big), F32),
        pltpu.VMEM((2, quarter, *big), F32),
        pltpu.VMEM((n, quarter, *big), F32),
        pltpu.VMEM((n, quarter, *big), F32),
        dma((2, steps, 3)), dma((2, steps, 3)),
        dma((n,)), dma((n,)), dma((n,)), dma((n,)),
    ]
    amp_scratch = [
        pltpu.VMEM((n * pc, *big), BF16),
        pltpu.VMEM((pc, *big), BF16),
        pltpu.VMEM((quarter, *big), F32),
        pltpu.VMEM((quarter, *big), BF16),
        dma((2, steps, 4)), dma((2, steps, 4)),
        dma((n, 4)), dma((n, 4)), dma((n + 1,)), dma((n + 1,)), dma((3,)), dma((3,)),
    ]
    half_shape = jax.ShapeDtypeStruct((quarter, *big), BF16)

    def iterate(first, start, x):
        return pl.pallas_call(
            functools.partial(iteration_alone, n, first),
            out_shape=half_shape if first else jax.ShapeDtypeStruct((pc, *big), BF16),
            in_specs=[smem, smem, vmem, vmem, vmem, vmem],
            out_specs=vmem,
            scratch_shapes=amp_scratch,
            compiler_params=params(1 if first else 2),
            name="first" if first else "second",
        )(slots, focks, start, x, exchange_integrals, pno_energy)

    held = n * width * (2 * pc * (rows + width) + 4 * width * 4 * quarter + 2 * width * quarter)
    if held < 40 * 2**20:
        return pl.pallas_call(
            functools.partial(opening, n, len(block_scratch)),
            out_shape=jax.ShapeDtypeStruct((pc, *big), BF16),
            in_specs=[smem, smem, vmem, vmem, vmem, vmem, vmem],
            out_specs=vmem,
            scratch_shapes=[
                pltpu.VMEM(x_shape.shape, BF16), pltpu.VMEM(half_shape.shape, BF16),
                *block_scratch, *amp_scratch, *amp_scratch,
            ],
            compiler_params=params(0),
            name="amplitudes",
        )(slots, focks, coefficients, domain, amplitudes_start, exchange_integrals, pno_energy).astype(F32)
    else:
        x = pl.pallas_call(
            functools.partial(intersections_alone, n),
            out_shape=x_shape,
            in_specs=[smem, vmem, vmem],
            out_specs=vmem,
            scratch_shapes=block_scratch,
            compiler_params=params(0),
            name="intersections",
        )(slots, coefficients, domain)
        amps = iterate(True, amplitudes_start, x)
    return iterate(False, amps, x).astype(F32)


def solution(mesh):
    placed = (
        P("pairs", "grp", None),
        P("pairs", "grp"),
        P("pairs", None),
        P("pairs", None),
        P("pairs", None),
        P("pairs", None, None),
        P("pairs", None),
        P("pairs"),
        P("pairs", None, None),
    )
    return jax.shard_map(
        on_device, mesh=mesh, in_specs=placed, out_specs=P("pairs", None, None), check_vma=False
    )
```

```python
import functools

import jax
import jax.numpy as jnp
from jax import lax
from jax.experimental import pallas as pl
from jax.experimental.pallas import tpu as pltpu
from jax.sharding import PartitionSpec as P

NB = 192
MESH = pl.DeviceIdType.MESH
F32, BF16 = jnp.float32, jnp.bfloat16


def ring_position(rank, n):
    odd = rank % 2
    return (1 - odd) * (rank // 2) + odd * (n - 1 - rank // 2)


def ring_rank(position, n):
    back = position // (n // 2)
    return (1 - back) * 2 * position + back * (2 * (n - 1 - position) + 1)


def places(n):
    p, g = lax.axis_index("pairs"), lax.axis_index("grp")
    position = ring_position(p, n)
    core, half = g % 2, g // 2
    mate = 2 * half + (1 - core)
    across = 2 * (1 - half) + core
    return p, g, position, mate, across


def at(position, n):
    return ring_rank((position + n) % n, n)


def greet(peers):
    barrier = pltpu.get_barrier_semaphore()
    for peer in peers:
        pl.semaphore_signal(barrier, inc=1, device_id=peer, device_id_type=MESH)
    pl.semaphore_wait(barrier, len(peers))


def remote(src, dst, send, recv, peer):
    return pltpu.make_async_remote_copy(
        src_ref=src, dst_ref=dst, send_sem=send, recv_sem=recv, device_id=peer, device_id_type=MESH
    )


def ring_parts(steps, parts):
    def of(step, direction):
        if step < steps:
            return tuple(range(parts))
        return tuple(c for c in range(parts) if c % 2 == direction)

    return of


def intersections(
    n, slot_ref, c_ref, dom_ref, out_ref,
    cbuf, dbuf, turned, wide, own, msend, mrecv, ysend, yrecv, keep,
    rs, rr, ms, mr, ys, yr,
):
    p, g, position, mate, across = places(n)
    pc = c_ref.shape[0]
    quarter = pc // 4
    rows = c_ref.shape[1]
    steps = n // 2
    right, left = at(position + 1, n), at(position - 1, n)
    ring_peer = (lambda r: (r, g))
    peers = [(right, g), (left, g), (p, mate), (p, across)]
    greet(peers)
    parts_of = ring_parts(steps, 3)
    hp = pc // 2

    def part(ref_c, ref_d, c):
        if c == 2:
            return ref_d
        return ref_c.at[pl.ds(c * hp, hp)]

    def move(step, direction, c):
        offset = -(step - 1) if direction == 0 else step - 1
        rank = at(position + offset, n)
        if step == 1:
            src = part(c_ref, dom_ref, c)
        else:
            src = part(cbuf.at[rank], dbuf.at[rank], c)
        dst = part(cbuf.at[rank], dbuf.at[rank], c)
        return remote(
            src, dst, rs.at[direction, step - 1, c], rr.at[direction, step - 1, c],
            ring_peer(right if direction == 0 else left),
        )

    def arrive(step, direction, c):
        offset = -step if direction == 0 else step
        rank = at(position + offset, n)
        dst = part(cbuf.at[rank], dbuf.at[rank], c)
        remote(
            dst, dst, rs.at[direction, step - 1, c], rr.at[direction, step - 1, c],
            ring_peer(left if direction == 0 else right),
        ).wait_recv()

    for c in (2, 0, 1):
        for d in (0, 1):
            if c in parts_of(1, d):
                move(1, d, c).start()

    base = g * NB
    lines = lax.broadcasted_iota(jnp.int32, (NB, rows), 0)
    core, half = g % 2, g // 2

    def expand(block, doms):
        def one(s, carry):
            hit = (lines == (doms[pl.ds(s, 1), :] - base)).astype(F32).astype(BF16)
            wide[s] = jnp.dot(hit, block[s], preferred_element_type=F32).astype(BF16)
            return carry

        lax.fori_loop(0, pc, one, 0, unroll=8)

    def mate_copy(k, rank):
        return remote(msend.at[k % 2], mrecv.at[rank], ms.at[k], mr.at[k], (p, mate))

    def across_copy(k, rank):
        return remote(ysend.at[k % 2], yrecv.at[rank], ys.at[k], yr.at[k], (p, across))

    ranks = []

    def product(t, rank):
        return jnp.dot(turned[t], wide[slot_ref[t, rank]], preferred_element_type=F32)

    def links(k, rank):
        if k >= 2:
            mate_copy(k - 2, ranks[k - 2]).wait_send()

        def theirs(i, carry):
            t = (2 * (i // quarter) + 1 - core) * quarter + i % quarter
            msend[k % 2, i] = product(t, rank)
            return carry

        lax.fori_loop(0, 2 * quarter, theirs, 0, unroll=8)
        mate_copy(k, rank).start()

        def ours(i, carry):
            t = (2 * (i // quarter) + core) * quarter + i % quarter
            own[k % 2, i] = product(t, rank)
            return carry

        lax.fori_loop(0, 2 * quarter, ours, 0, unroll=8)

    def finish(k):
        rank = ranks[k]
        if k >= 2:
            across_copy(k - 2, ranks[k - 2]).wait_send()
        mate_copy(k, rank).wait_recv()

        def send(j, carry):
            i = (1 - half) * quarter + j
            ysend[k % 2, j] = own[k % 2, i] + mrecv[rank, i]
            return carry

        lax.fori_loop(0, quarter, send, 0)
        across_copy(k, rank).start()

        def hold(j, carry):
            i = half * quarter + j
            keep[rank, j] = own[k % 2, i] + mrecv[rank, i]
            return carry

        lax.fori_loop(0, quarter, hold, 0)

    def process(rank):
        k = len(ranks)
        ranks.append(rank)
        links(k, rank)

    expand(c_ref, dom_ref)

    def turn(t, carry):
        turned[t] = wide[t].astype(F32).T.astype(BF16)
        return carry

    lax.fori_loop(0, pc, turn, 0, unroll=2)
    process(p)
    finish(0)
    for step in range(1, steps + 1):
        for c in (2, 0, 1):
            for d in (0, 1):
                if c in parts_of(step, d):
                    arrive(step, d, c)
                if step < steps and c in parts_of(step + 1, d):
                    move(step + 1, d, c).start()
        if step == steps - 1:
            yield None
        for d in (0, 1) if step < steps else (0,):
            rank = at(position + (-step if d == 0 else step), n)
            expand(cbuf.at[rank], dbuf.at[rank])
            process(rank)
            if d == 1:
                finish(len(ranks) - 2)
        finish(len(ranks) - 1)
    def settle(k):
        rank = ranks[k]
        across_copy(k, rank).wait_recv()

        def last(j, carry):
            out_ref[rank, j] = (keep[rank, j] + yrecv[rank, j]).astype(BF16)
            return carry

        lax.fori_loop(0, quarter, last, 0)

    yield settle
    for k in (n - 2, n - 1):
        mate_copy(k, ranks[k]).wait_send()
        across_copy(k, ranks[k]).wait_send()
    for step in range(1, steps + 1):
        for d in (0, 1):
            for c in parts_of(step, d):
                move(step, d, c).wait_send()


def iteration(
    n, first, joined, alone, slot_ref, fock_ref, start_ref, x_ref, k_ref, e_ref, out_ref,
    abuf, stage, acc, mine, rs, rr, ms, mr, ys, yr, fs, fr,
):
    p, g, position, mate, across = places(n)
    pc = k_ref.shape[0]
    width = k_ref.shape[1]
    quarter = pc // 4
    eighth = quarter // 2
    steps = n // 2
    right, left = at(position + 1, n), at(position - 1, n)
    diagonal = 3 - g
    if alone:
        greet([(right, g), (left, g), (p, mate), (p, across)])
    parts = 4 if joined else 3
    parts_of = ring_parts(steps, parts)

    def chunk(rank, group, c):
        return abuf.at[pl.ds(rank * pc + group * quarter + (c % 2) * eighth, eighth)]

    def span(rank, c):
        return chunk(rank, g if c < 2 else across, c)

    def ring_copy(step, direction, c):
        offset = -(step - 1) if direction == 0 else step - 1
        ref = span(at(position + offset, n), c)
        src = ref
        if step == 1 and c < 2 and not first:
            src = start_ref.at[pl.ds(c * eighth, eighth)]
        return remote(
            src, ref, rs.at[direction, step - 1, c], rr.at[direction, step - 1, c],
            (right if direction == 0 else left, g),
        )

    def arrive(step, direction, c):
        offset = -step if direction == 0 else step
        ref = span(at(position + offset, n), c)
        remote(
            ref, ref, rs.at[direction, step - 1, c], rr.at[direction, step - 1, c],
            (left if direction == 0 else right, g),
        ).wait_recv()

    def mate_copy(k, rank, c, src=None):
        ref = span(rank, c)
        return remote(ref if src is None else src, ref, ms.at[k, c], mr.at[k, c], (p, mate))

    def mate_wait(k, rank):
        for c in range(4):
            ref = chunk(rank, mate if c < 2 else diagonal, c)
            remote(ref, ref, ms.at[k, c], mr.at[k, c], (p, mate)).wait_recv()

    def across_copy(k, rank, c=1, src=None):
        ref = span(rank, c)
        sem = k if c == 1 else n
        return remote(ref if src is None else src, ref, ys.at[sem], yr.at[sem], (p, across))

    def across_wait(k, rank, c=3):
        ref = span(rank, c)
        sem = k if c == 3 else n
        remote(ref, ref, ys.at[sem], yr.at[sem], (p, across)).wait_recv()

    def own_half(c):
        return start_ref.at[pl.ds(c * eighth, eighth)]

    if first:
        def copy_own(i, carry):
            abuf[p * pc + i] = start_ref[i].astype(BF16)
            return carry

        def group_in(group):
            lax.fori_loop(group * quarter, (group + 1) * quarter, copy_own, 0)

        group_in(g)
        for c in (0, 1):
            for d in (0, 1):
                if c in parts_of(1, d):
                    ring_copy(1, d, c).start()
        group_in(across)
        for c in range(2, parts):
            for d in (0, 1):
                if c in parts_of(1, d):
                    ring_copy(1, d, c).start()
        group_in(mate)
        group_in(diagonal)
    else:
        for c in (0, 1):
            across_copy(0, p, c, own_half(c)).start()
            for d in (0, 1):
                if c in parts_of(1, d):
                    ring_copy(1, d, c).start()
        for c in (0, 1):
            mate_copy(0, p, c, own_half(c)).start()

        def copy_own(i, carry):
            abuf[p * pc + g * quarter + i] = start_ref[i]
            return carry

        lax.fori_loop(0, quarter, copy_own, 0)
        across_wait(0, p, 2)
        for d in (0, 1):
            if 2 in parts_of(1, d):
                ring_copy(1, d, 2).start()
        mate_copy(0, p, 2).start()
        across_wait(0, p, 3)
        mate_copy(0, p, 3).start()
        mate_wait(0, p)

    settle = yield None
    acc[...] = jnp.zeros_like(acc)

    def couple(rank, k):
        if settle is not None:
            settle(k)

        def copy(i, carry):
            stage[i] = abuf[rank * pc + i]
            return carry

        lax.fori_loop(0, pc, copy, 0, unroll=4)

        def one(j, carry):
            t = g * quarter + j
            source = stage[slot_ref[t, rank]]
            x = x_ref[rank, j]
            h = jnp.dot(x, source, preferred_element_type=F32).astype(BF16)
            y = lax.dot_general(h, x, (((1,), (1,)), ((), ())), preferred_element_type=F32)
            acc[j] += fock_ref[t, rank] * y
            return carry

        lax.fori_loop(0, quarter, one, 0, unroll=4)

    couple(p, 0)

    def exchange(blocks):
        for k, rank in () if joined else blocks:
            across_wait(k, rank)
            mate_copy(k, rank, 3).start()

    def use(blocks):
        for k, rank in blocks:
            mate_wait(k, rank)
            couple(rank, k)

    landed, shared = [], []
    for step in range(1, steps + 1):
        for c in (1, 0, 2, 3)[:parts]:
            for d in (0, 1):
                rank = at(position + (-step if d == 0 else step), n)
                if c in parts_of(step, d):
                    arrive(step, d, c)
                    if step < steps and c in parts_of(step + 1, d):
                        ring_copy(step + 1, d, c).start()
                    k = 2 * step - 1 + (d if step < steps else 0)
                    if c == 1 and not joined:
                        across_copy(k, rank).start()
                    mate_copy(k, rank, c).start()
        exchange(landed)
        use(shared)
        shared = landed
        landed = [
            (2 * step - 1 + d, at(position + (-step if d == 0 else step), n))
            for d in ((0, 1) if step < steps else (0,))
        ]
    exchange(landed)
    use(shared)
    use(landed)

    def scaled(j):
        t = g * quarter + j
        row = jnp.broadcast_to(e_ref[pl.ds(t, 1), :], (width, width))
        return (-(k_ref[t] + acc[j]) / (row.T + row + fock_ref[t, n])).astype(BF16)

    if first:
        def result(j, carry):
            out_ref[j] = scaled(j)
            return carry

        lax.fori_loop(0, quarter, result, 0, unroll=2)
    else:
        def block(ref, group):
            return ref.at[pl.ds(group * quarter, quarter)]

        def result(j, carry):
            value = scaled(j)
            mine[j] = value
            out_ref[g * quarter + j] = value
            return carry

        lax.fori_loop(0, quarter, result, 0, unroll=2)
        over = remote(mine, block(out_ref, g), fs.at[0], fr.at[0], (p, across))
        beside = remote(mine, block(out_ref, g), fs.at[1], fr.at[1], (p, mate))
        corner = remote(
            block(out_ref, across), block(out_ref, across), fs.at[2], fr.at[2], (p, mate)
        )
        over.start()
        beside.start()
        remote(mine, block(out_ref, across), fs.at[0], fr.at[0], (p, across)).wait_recv()
        corner.start()
        remote(mine, block(out_ref, mate), fs.at[1], fr.at[1], (p, mate)).wait_recv()
        remote(mine, block(out_ref, diagonal), fs.at[2], fr.at[2], (p, mate)).wait_recv()
        over.wait_send()
        beside.wait_send()
        corner.wait_send()
        across_copy(0, p, 0, own_half(0)).wait_send()
        across_copy(0, p, 1, own_half(1)).wait_send()
        for c in range(4):
            mate_copy(0, p, c).wait_send()
    for k in range(1, n):
        if not joined:
            across_copy(k, p).wait_send()
        for c in range(4):
            mate_copy(k, p, c).wait_send()
    for step in range(1, steps + 1):
        for d in (0, 1):
            for c in parts_of(step, d):
                ring_copy(step, d, c).wait_send()


def intersections_alone(*args):
    steps = intersections(*args)
    next(steps)
    settle = next(steps)
    for k in range(args[0]):
        settle(k)
    next(steps, None)


def iteration_alone(n, first, *args):
    steps = iteration(n, first, False, True, *args)
    next(steps)
    try:
        steps.send(None)
    except StopIteration:
        pass


def opening(
    n, made, slot_ref, fock_ref, c_ref, dom_ref, start_ref, k_ref, e_ref, out_ref,
    x_ref, amp_ref, *scratch
):
    used = made + (len(scratch) - made) // 2
    blocks = intersections(n, slot_ref, c_ref, dom_ref, x_ref, *scratch[:made])
    next(blocks)
    amps = iteration(
        n, True, True, False, slot_ref, fock_ref, start_ref, x_ref, k_ref, e_ref, amp_ref,
        *scratch[made:used],
    )
    next(amps)
    settle = next(blocks)
    try:
        amps.send(settle)
    except StopIteration:
        pass
    amps = iteration(
        n, False, False, False, slot_ref, fock_ref, amp_ref, x_ref, k_ref, e_ref, out_ref,
        *scratch[used:],
    )
    next(amps)
    try:
        amps.send(None)
    except StopIteration:
        pass
    next(blocks, None)


class Wires:
    def __init__(self, send, recv, here):
        self.send, self.recv, self.here = send, recv, here
        self.sends, self.recvs = {}, {}

    def link(self, key, src, dst, peer, out):
        at_send = self.sends.setdefault(out, len(self.sends))
        at_recv = self.recvs.setdefault(key, len(self.recvs))
        return remote(src, dst, self.send.at[at_send], self.recv.at[at_recv], peer)

    def start_in(self, when, key, src, dst, peer, out):
        self.link(key, src, dst, peer, out).start()

    def start(self, key, src, dst, peer, out, when=None):
        def run():
            self.start_in(when, key, src, dst, peer, out)

        if when is None:
            run()
        else:
            pl.when(when)(run)

    def wait(self, key, dst, when=None):
        at_recv = self.recvs.setdefault(key, len(self.recvs))
        copy = remote(dst, dst, self.send.at[0], self.recv.at[at_recv], self.here)
        if when is None:
            copy.wait_recv()
        else:
            pl.when(when)(copy.wait_recv)

    def drain(self, out, whole, when=None):
        at_send = self.sends[out]
        copy = remote(whole, whole, self.send.at[at_send], self.recv.at[0], self.here)
        if when is None:
            copy.wait_send()
        else:
            pl.when(when)(copy.wait_send)


def note(*what):
    return None


def quadrants(
    n, owner_hbm, slot_hbm, fock_hbm, shift_hbm, c_hbm, dom_hbm, start_ref, k_ref, e_hbm, out_ref,
    owner_ref, slot_ref, fock_ref, shift_ref, c_ref, dom_ref, e_ref, src, dom, blocks, bdom, bslot, bfock, wide, turned, x, start, k_own, amps_a, amps_b, amps_c, amps_d,
    acc, yout, yx, ysum, yin, mine, send, recv, local,
):
    p, g = lax.axis_index("pairs"), lax.axis_index("grp")
    pc, rows, width = c_ref.shape
    quarter = pc // 4
    half_quarter = quarter // 2
    layers = n // 2
    layer, column = p // 2, p % 2
    inner = (layer % 2 + layer // 2) % 2
    mid, end = inner == 1, inner == 0
    partner = (layer + 1 - 2 * (layer % 2)) * 2 + column
    cross = (layers - 1 - layer) * 2 + column
    far = ((layer + layers // 2) % layers) * 2 + column
    beside = layer * 2 + 1 - column
    groups = (g, g + 1 - 2 * (g % 2), (g + 2) % 4, 3 - g)
    _, mate, across, diagonal = groups
    to_mate, to_across = (p, mate), (p, across)
    to_partner, to_cross, to_beside, to_far = (partner, g), (cross, g), (beside, g), (far, g)
    wires = Wires(send, recv, to_mate)
    amps = ((amps_a, amps_b), (amps_c, amps_d))
    wires.mid = mid

    barrier = pltpu.get_barrier_semaphore()

    def hello(peer):
        pl.semaphore_signal(barrier, inc=1, device_id=peer, device_id_type=MESH)

    for peer in (to_partner, to_beside, to_across, to_mate):
        hello(peer)
    pl.when(mid)(lambda: hello(to_cross))

    pairs = (
        (c_hbm, c_ref), (dom_hbm, dom_ref), (owner_hbm, owner_ref), (slot_hbm, slot_ref),
        (fock_hbm, fock_ref), (shift_hbm, shift_ref), (e_hbm, e_ref), (start_ref, start),
        (k_ref.at[pl.ds(g * quarter, quarter)], k_own),
    )
    loads = [pltpu.make_async_copy(*pair, local.at[i]) for i, pair in enumerate(pairs)]
    for load in loads:
        load.start()
    load_c, load_dom, load_owner, load_slot, load_fock, load_shift, load_e, load_start, load_k = loads
    load_c.wait()
    load_dom.wait()

    def four(group):
        return pl.ds(group * quarter, quarter)

    def two(group, h):
        return pl.ds(group * quarter + h * half_quarter, half_quarter)

    def both_quarters(ref):
        return ref.at[pl.ds(0, 2 * quarter)]

    def three_quarters(ref):
        return ref.at[pl.ds(0, 3 * quarter)]

    def source(b, rel):
        return c_ref if (b, rel) == (0, 0) else src.at[4 * b + rel]

    def turn(rel, b=0):
        for t in range(quarter):
            blocks[b, rel, t] = source(b, rel)[g * quarter + t].T

    for s in range(pc):
        dom[0, s] = dom_ref[pl.ds(s, 1), :]
    turn(0)

    def table(t, carry):
        at_pair = g * quarter + t
        ways = owner_ref.shape[0]
        named = [owner_ref[k, at_pair] for k in range(ways)]
        slots = [slot_ref[k, at_pair] for k in range(ways)]
        focks = [fock_ref[k, at_pair] for k in range(ways)]
        for owner in range(n):
            place, weight = 0, 0.0
            for k in range(ways):
                hit = named[k] == owner
                place = jnp.where(hit, slots[k], place)
                weight = jnp.where(hit, focks[k], weight)
            bslot[0, t, owner] = place
            bfock[0, t, owner] = weight
        return carry

    small = ("slot", "fock", "dom")
    kinds = {
        "slot": lambda b: bslot.at[b],
        "fock": lambda b: bfock.at[b],
        "dom": lambda b: bdom.at[b],
    }
    for rel in range(4):
        for h in (0, 1):
            kinds[rel, h] = functools.partial(
                lambda rel, h, b: blocks.at[b, rel, pl.ds(h * half_quarter, half_quarter)], rel, h
            )
        kinds[rel] = functools.partial(lambda rel, b: blocks.at[b, rel], rel)

    def tag(kind):
        return kind if kind in small else "targets"

    def landing(kind):
        return kind if kind in small or kind in ((3, 0), (3, 1)) else 0

    def ready(kind):
        ref = kinds[kind](0)
        onward, across_cut = kinds[kind](4), kinds[kind](2)
        if kind in ("slot", "fock"):
            wires.start(("second", kind), ref, kinds[kind](1), to_partner, kind)
        wires.start(("beside", 0 if tag(kind) == "targets" else kind), ref, onward, to_beside, tag(kind), end)
        wires.start(("cross", kind), ref, across_cut, to_cross, tag(kind), mid)

    def next_ready(kind):
        ref = kinds[kind](1)
        onward, across_cut = kinds[kind](5), kinds[kind](3)
        if kind in ("slot", "fock"):
            wires.wait(("second", kind), ref)
        wires.start(("beside2", landing(kind)), ref, onward, to_beside, tag(kind), end)
        wires.start(("further", kind), ref, across_cut, to_cross, tag(kind), mid)

    def got_first(kind):
        landed, passed = kinds[kind](2), kinds[kind](4)

        def relay():
            wires.wait(("cross", kind), landed)
            key = ("beside", 0 if tag(kind) == "targets" else kind)
            wires.start_in(mid, key, landed, passed, to_beside, tag(kind))

        pl.when(mid)(relay)

    def got_further(kind):
        landed, passed = kinds[kind](3), kinds[kind](5)

        def relay():
            wires.wait(("further", kind), landed)
            wires.start_in(mid, ("beside2", landing(kind)), landed, passed, to_beside, tag(kind))

        pl.when(mid)(relay)

    def got_beside():
        for kind in small:
            wires.wait(("beside", kind), kinds[kind](4))
        wires.wait(("beside", 0), blocks.at[4])

    def got_beside2():
        for kind in small:
            wires.wait(("beside2", kind), kinds[kind](5))
        wires.wait(("beside2", 0), blocks.at[5, pl.ds(0, 3)])

    first, second = 2 * inner, 1 + 2 * inner
    places_of = (first, 4, second, 5)

    lines = lax.broadcasted_iota(jnp.int16, (NB, rows), 0)
    lines2 = lax.broadcasted_iota(jnp.int16, (2 * NB, 2 * rows), 0)

    def one_hot(numbers, row):
        hit = numbers == row.astype(jnp.int16)
        return jnp.where(hit, jnp.ones(hit.shape, BF16), jnp.zeros(hit.shape, BF16))

    def expand(b, rel, parts=(0, 1, 2, 3)):
        base = groups[rel] * NB
        block = source(b, rel)

        def one(s, carry):
            hit = one_hot(lines, dom[4 * b + rel, s] - base)
            wide[b, s, pl.ds(rel * NB, NB)] = jnp.dot(
                hit, block[s], preferred_element_type=F32
            ).astype(BF16)
            return carry

        if len(parts) == 4:
            note("expand", b, rel)
            lax.fori_loop(0, pc, one, 0, unroll=4)
            return
        for i in parts:
            note("expand4", b, rel)
            for t in range(quarter):
                one(groups[i] * quarter + t, 0)

    every = tuple(range(quarter))
    early, later = every[:half_quarter], every[half_quarter:]

    def make_turned(b, hs=(0, 1), ts=every):
        note("make_turned", b, 0, len(hs) * len(ts) / 8)
        place = places_of[b]

        def one(t, carry):
            for h in hs:
                u, v = 2 * h, 2 * h + 1
                row = jnp.concatenate(
                    [
                        bdom[place, u * quarter + t] - groups[u] * NB,
                        bdom[place, v * quarter + t] - groups[v] * NB + NB,
                    ],
                    axis=1,
                )
                hit = one_hot(lines2, row)
                both = jnp.concatenate([blocks[place, u, t], blocks[place, v, t]], axis=1)
                turned[b, t, :, pl.ds(h * 2 * NB, 2 * NB)] = lax.dot_general(
                    both, hit, (((1,), (1,)), ((), ())), preferred_element_type=F32
                ).astype(BF16)
            return carry

        if ts == every:
            lax.fori_loop(0, quarter, one, 0, unroll=2)
        else:
            for t in ts:
                one(t, 0)

    owners = (p, partner)

    def make_x(b, s, ts=every):
        note("make_x", b, s, len(ts) / 4)
        place = places_of[b]

        def one(t, carry):
            at_source = bslot[place, t, owners[s]]
            x[b, t, s] = jnp.dot(
                turned[b, t], wide[s, at_source], preferred_element_type=F32
            ).astype(BF16)
            return carry

        for t in ts:
            one(t, 0)

    def couple(b, s, it, ts=every):
        note("couple", b, s, len(ts) / 4)
        place = places_of[b]
        found = []
        for t in ts:
            at_source = bslot[place, t, owners[s]]
            xs = x[b, t, s]
            half = jnp.dot(xs, amps[it][s][at_source], preferred_element_type=F32).astype(BF16)
            found.append((t, xs, half))
        for t, xs, half in found:
            y = lax.dot_general(half, xs, (((1,), (1,)), ((), ())), preferred_element_type=F32)
            y = bfock[place, t, owners[s]] * y
            if s == 0:
                acc[b, t] = y
            elif b % 2 == 0:
                acc[b, t] += y
            else:
                yout[it, b // 2, t] = (acc[b, t] + y).astype(BF16)

    def post(it, m, ts=every):
        for t in ts:
            wires.start(("y", it, m, t), yout.at[it, m, t], yx.at[it, m, t], to_beside, "y")

    def share(t):
        at_pair = g * quarter + t
        ref = amps[1][0].at[at_pair]
        wires.start(("own", 1, t), ref, ref, to_across, "amps")
        wires.start(("own", 2), ref, ref, to_mate, "amps")

    def share_partner(t, when):
        at_pair = g * quarter + t
        wires.start(("a", 1, 0, t), amps[1][0].at[at_pair], amps[1][1].at[at_pair], to_partner, "amps", when)

    def pass_partner(t):
        ref = amps[1][1].at[g * quarter + t]
        wires.wait(("a", 1, 0, t), ref)
        wires.start(("a", 1, 1, t), ref, ref, to_across, "amps")
        wires.start(("a", 1, 2), ref, ref, to_mate, "amps")

    def pass_own(t):
        ref = amps[1][0].at[across * quarter + t]
        wires.wait(("own", 1, t), ref)
        wires.start(("own", 2), ref, ref, to_mate, "amps")

    def pass_across(t):
        ref = amps[1][1].at[across * quarter + t]
        wires.wait(("a", 1, 1, t), ref)
        wires.start(("a", 1, 2), ref, ref, to_mate, "amps")

    def share_start(j):
        part = four((g, across)[j])
        wires.start(("start", j), amps[0][0].at[part], amps[0][1].at[part], to_partner, "amps")

    def pass_start(j):
        ref = amps[0][1].at[four((g, across)[j])]
        wires.wait(("start", j), ref)
        wires.start(("a", 0, 2), ref, ref, to_mate, "amps")

    def have_partner(it):
        wires.wait(("a", it, 2), both_quarters(amps[it][1]))

    def sum_second(it):
        for t in range(quarter):
            wires.wait(("y", it, 1, t), yx.at[it, 1, t])
            ysum[it, 1, t] = (acc[2, t] + yx[it, 1, t].astype(F32)).astype(BF16)
            job = (("yfar", it, t), ysum.at[it, 1, t], yin.at[it, 0, t])
            wires.start(*job, to_partner, "yfar", end)
            wires.start(*job, to_far, "yfar", mid)

    def sum_first(it, ts=every):
        for t in ts:
            wires.wait(("y", it, 0, t), yx.at[it, 0, t])
            total = acc[0, t] + yx[it, 0, t].astype(F32)
            acc[0, t] = total
            ysum[it, 0, t] = total.astype(BF16)
            wires.start(("ynear", it, t), ysum.at[it, 0, t], yin.at[it, 1, t], to_cross, "ynear", mid)

    def coupled(it, t):
        wires.wait(("ynear", it, t), yin.at[it, 1, t], mid)
        wires.wait(("yfar", it, t), yin.at[it, 0, t])
        near = yin[it, 1, t].astype(F32)
        return yin[it, 0, t].astype(F32) + jnp.where(mid, near, acc[0, t])

    def updated(it, t):
        at_pair = g * quarter + t
        total = coupled(it, t)
        row = jnp.broadcast_to(e_ref[pl.ds(at_pair, 1), :], (width, width))
        return (-(k_own[t] + total) / (row.T + row + shift_ref[at_pair])).astype(BF16)

    swap_mate, swap_across = (1, 0, 3, 2), (2, 3, 0, 1)

    def from_mate():
        wires.wait(("own mate", 1), src.at[1, four(g)])

    def from_mate_rest():
        wires.wait(("own mate", 0), three_quarters(src.at[1]))

    def from_across(i):
        part = four(groups[i])
        wires.wait(("own across", swap_across[i]), src.at[2, part])
        wires.start(
            ("own corner", int(i == 1)), src.at[2, part], src.at[3, part], to_mate,
            "rows",
        )

    def from_corner():
        wires.wait(("own corner", 1), src.at[3, four(g)])

    def from_corner_rest():
        wires.wait(("own corner", 0), three_quarters(src.at[3]))

    def to_next(i):
        part = four(groups[i])
        wires.start(
            ("next", i), c_ref.at[part], src.at[4, part], to_partner, "rows"
        )

    def from_next(i):
        part = four(groups[i])
        ref = src.at[4, part]
        wires.wait(("next", i), ref)
        if i > 0:
            wires.start(
                ("next across", i), ref, src.at[6, part], to_across, "rows",
            )
        wires.start(
            ("next mate", int(i == 1)), ref, src.at[5, part], to_mate, "rows",
        )

    def to_wide(i):
        part = four(groups[i])
        wires.start(
            ("next wide", i), src.at[2, part], src.at[6, part], to_partner, "rows",
        )

    def corner(i):
        part = four(groups[i])
        wires.start(
            ("next corner", int(i == 1)), src.at[6, part], src.at[7, part], to_mate, "rows",
        )

    def from_next_across(i):
        wires.wait(("next across", swap_across[i]), src.at[6, four(groups[i])])
        corner(i)

    def from_wide(i):
        wires.wait(("next wide", i), src.at[6, four(groups[i])])
        corner(i)

    def from_next_mate():
        wires.wait(("next mate", 1), src.at[5, four(g)])

    def from_next_mate_rest():
        wires.wait(("next mate", 0), three_quarters(src.at[5]))

    def from_next_corner():
        wires.wait(("next corner", 1), src.at[7, four(g)])

    def from_next_corner_rest():
        wires.wait(("next corner", 0), three_quarters(src.at[7]))

    def own_across(i):
        part = four(groups[i])
        wires.start(
            ("own across", i), c_ref.at[part], src.at[2, part], to_across, "rows",
        )

    def cast(s, carry):
        amps[0][0][s] = start[s].astype(BF16)
        return carry

    pl.semaphore_wait(barrier, 4 + inner)
    wires.start(("d", 1), dom.at[0], dom.at[1], to_mate, "doms")
    wires.start(("d", 2), dom.at[0], dom.at[2], to_across, "doms")
    own_across(2)
    to_next(0)
    ready((0, 0))
    ready((0, 1))
    for i in (1, 0, 2, 3):
        part = four(groups[i])
        wires.start(
            ("own mate", int(i == 1)), c_ref.at[part], src.at[1, part], to_mate, "rows",
        )
    own_across(3)
    own_across(0)
    to_next(2)
    from_mate()
    turn(1)
    ready(1)
    wires.wait(("d", 1), dom.at[1])
    wires.wait(("d", 2), dom.at[2])
    wires.start(("d", 3), dom.at[2], dom.at[3], to_mate, "doms")
    for load in (load_owner, load_slot, load_fock):
        load.wait()
    lax.fori_loop(0, quarter, table, 0)
    ready("slot")
    ready("fock")
    wires.wait(("d", 3), dom.at[3])
    wires.start(("d", 4), dom.at[pl.ds(0, 4)], dom.at[pl.ds(4, 4)], to_partner, "doms")
    to_next(3)
    to_next(1)
    for rel in range(4):
        for t in range(quarter):
            bdom[0, rel * quarter + t] = dom[rel, g * quarter + t]
    ready("dom")
    got_first((0, 0))
    expand(0, 0)
    from_next(0)
    turn(0, 1)
    next_ready(0)
    got_first((0, 1))
    from_across(0)
    turn(2)
    ready((2, 0))
    ready((2, 1))
    from_mate_rest()
    expand(0, 1)
    expand(0, 2, (0,))
    from_next(2)
    own_across(1)
    got_first(1)
    from_across(1)
    from_corner()
    turn(3)
    ready((3, 0))
    ready((3, 1))
    load_start.wait()
    lax.fori_loop(0, pc, cast, 0, unroll=2)
    wires.wait(("d", 4), dom.at[pl.ds(4, 4)])
    expand(0, 2, (1,))
    expand(1, 0, (0, 2))
    from_across(2)
    to_wide(2)
    share_start(0)
    share_start(1)
    got_further(0)
    from_next(3)
    expand(0, 2, (2,))
    expand(1, 0, (3,))
    got_first((2, 0))
    for rel in range(4):
        for t in range(quarter):
            bdom[1, rel * quarter + t] = dom[4 + rel, g * quarter + t]
    next_ready("dom")
    next_ready("slot")
    next_ready("fock")
    from_next(1)
    from_next_across(0)
    turn(2, 1)
    next_ready((2, 0))
    next_ready((2, 1))
    got_first((2, 1))
    expand(1, 0, (1,))
    from_next_mate()
    turn(1, 1)
    next_ready((1, 0))
    next_ready((1, 1))
    got_first((3, 0))
    from_next_mate_rest()
    expand(1, 1)
    got_first((3, 1))
    from_across(3)
    for kind in small:
        got_first(kind)
    expand(1, 2, (0,))
    from_wide(2)
    got_further((2, 0))
    expand(0, 2, (3,))
    expand(1, 2, (2,))
    from_corner_rest()
    got_further((2, 1))
    expand(0, 3)
    from_next_across(1)
    from_next_corner()
    turn(3, 1)
    next_ready((3, 0))
    next_ready((3, 1))
    got_further((1, 0))
    pass_start(0)
    expand(1, 2, (1,))
    make_turned(0)
    got_further((1, 1))
    from_next_across(3)
    make_x(0, 0)
    expand(1, 2, (3,))
    pass_start(1)
    for kind in small:
        got_further(kind)
    from_next_corner_rest()
    expand(1, 3)
    got_further((3, 0))
    got_beside()
    make_turned(1)
    make_x(1, 0)
    make_x(1, 1)
    have_partner(0)
    got_further((3, 1))
    couple(1, 0, 0)
    couple(1, 1, 0)
    post(0, 0, early)
    make_turned(2)
    make_x(2, 0)
    make_x(2, 1)
    couple(2, 0, 0)
    couple(2, 1, 0)
    got_beside2()
    make_turned(3, (0,))
    for h, ts in ((0, early), (1, later)):
        wires.wait(("beside2", (3, h)), kinds[3, h](5))
        make_turned(3, (1,), ts)
        make_x(3, 0, ts)
        make_x(3, 1, ts)
        couple(3, 0, 0, ts)
        couple(3, 1, 0, ts)
        post(0, 1, ts)
    post(0, 0, later)
    make_x(0, 1)
    couple(0, 0, 0)
    couple(0, 1, 0)
    for load in (load_k, load_e, load_shift):
        load.wait()
    sum_first(0, early)
    sum_second(0)
    sum_first(0, later)

    for t in range(quarter):
        amps[1][0][g * quarter + t] = updated(0, t)
        share_partner(t, None)
        share(t)
    for t in range(quarter):
        pass_partner(t)
        pass_own(t)
    wires.wait(("own", 2), both_quarters(amps[1][0]))
    couple(3, 0, 1)
    couple(1, 0, 1)
    for t in range(half_quarter):
        pass_across(t)
    couple(2, 0, 1)
    couple(0, 0, 1)
    for t in range(half_quarter, quarter):
        pass_across(t)
    have_partner(1)
    couple(3, 1, 1)
    post(1, 1)
    couple(1, 1, 1)
    post(1, 0)
    couple(2, 1, 1)
    couple(0, 1, 1)
    sum_second(1)
    sum_first(1)

    for t in range(quarter):
        value = coupled(1, t).astype(BF16)
        mine[t] = value
        out_ref[g * quarter + t] = value
        part, dst = mine.at[t], out_ref.at[g * quarter + t]
        wires.start(("out", 1, t), part, dst, to_across, "amps")
        wires.start(("out", 2), part, dst, to_mate, "out")
    for t in range(quarter):
        ref = out_ref.at[across * quarter + t]
        wires.wait(("out", 1, t), ref)
        wires.start(("out", 2), ref, ref, to_mate, "out")
    wires.wait(("out", 2), both_quarters(out_ref))
    wires.drain("rows", src.at[pl.ds(0, 7)])
    wires.drain("doms", dom.at[pl.ds(0, 7)])
    for role, passes in ((end, 2), (mid, 4)):
        wires.drain("targets", blocks.at[pl.ds(0, passes)], role)
        wires.drain("dom", bdom.at[pl.ds(0, passes)], role)
        wires.drain("slot", bslot.at[pl.ds(0, passes + 1)], role)
        wires.drain("fock", bfock.at[pl.ds(0, passes + 1)], role)
    wires.drain("y", yout)
    wires.drain("yfar", ysum.at[0])
    wires.drain("ynear", ysum.at[0], mid)
    wires.drain("amps", src.at[pl.ds(0, 3)])
    wires.drain("out", both_quarters(out_ref))
    assert len(wires.sends) <= SENDS and len(wires.recvs) <= RECVS, (len(wires.sends), len(wires.recvs))


SENDS, RECVS = 11, 110


def quadrants_fit(n, groups, pc, rows, width):
    return n == 2 * groups and groups == 4 and pc % (2 * groups) == 0 and rows == width


def quadrants_kernel(n, *refs):
    quadrants(n, *refs)


def quadrants_call(
    n, owner, slot, fock, shift, coefficients, domain, start, integrals, energy
):
    pc, rows, width = coefficients.shape
    quarter = pc // 4
    big, ways = (width, width), owner.shape[1]
    vmem, hbm = pl.BlockSpec(memory_space=pltpu.VMEM), pl.BlockSpec(memory_space=pl.ANY)
    dma = pltpu.SemaphoreType.DMA
    total = pl.pallas_call(
        functools.partial(quadrants_kernel, n),
        out_shape=jax.ShapeDtypeStruct((pc, *big), BF16),
        in_specs=[hbm] * 9,
        out_specs=vmem,
        scratch_shapes=[
            pltpu.SMEM((ways, pc), jnp.int32), pltpu.SMEM((ways, pc), jnp.int32),
            pltpu.SMEM((ways, pc), F32), pltpu.SMEM((pc,), F32),
            pltpu.VMEM((pc, rows, width), BF16), pltpu.VMEM((pc, rows), jnp.int32),
            pltpu.VMEM((pc, width), F32),
            pltpu.VMEM((8, pc, rows, width), BF16),
            pltpu.VMEM((8, pc, 1, rows), jnp.int32),
            pltpu.VMEM((6, 4, quarter, width, rows), BF16),
            pltpu.VMEM((6, 4 * quarter, 1, rows), jnp.int32),
            pltpu.SMEM((6, quarter, n), jnp.int32),
            pltpu.SMEM((6, quarter, n), F32),
            pltpu.VMEM((2, pc, 4 * NB, width), BF16),
            pltpu.VMEM((4, quarter, width, 4 * NB), BF16),
            pltpu.VMEM((4, quarter, 2, *big), BF16),
            pltpu.VMEM((pc, *big), F32),
            pltpu.VMEM((quarter, *big), F32),
            *[pltpu.VMEM((pc, *big), BF16)] * 4,
            pltpu.VMEM((4, quarter, *big), F32),
            pltpu.VMEM((2, 2, quarter, *big), BF16),
            pltpu.VMEM((2, 2, quarter, *big), BF16),
            pltpu.VMEM((2, 2, quarter, *big), BF16),
            pltpu.VMEM((2, 2, quarter, *big), BF16),
            pltpu.VMEM((quarter, *big), BF16),
            dma((SENDS,)), dma((RECVS,)), dma((9,)),
        ],
        compiler_params=pltpu.CompilerParams(
            collective_id=0, has_side_effects=True, vmem_limit_bytes=60 * 2**20
        ),
        name="quadrants",
    )(owner.T, slot.T, fock.T, shift, coefficients, domain, start, integrals, energy)
    denominator = energy[:, :, None] + energy[:, None, :] + shift[:, None, None]
    return -(integrals + total.astype(F32)) / denominator


def on_device(
    coefficients, domain, coupling_owner, coupling_slot, coupling_fock,
    exchange_integrals, pno_energy, pair_shift, amplitudes_start,
):
    n = lax.axis_size("pairs")
    pc, rows, width = coefficients.shape
    quarter = pc // lax.axis_size("grp")
    steps = n // 2
    named = coupling_owner[:, :, None] == jnp.arange(n, dtype=jnp.int32)[None, None, :]
    slots = jnp.sum(jnp.where(named, coupling_slot[:, :, None], 0), axis=1)
    focks = jnp.sum(jnp.where(named, coupling_fock[:, :, None], 0.0), axis=1)
    focks = jnp.concatenate([focks, pair_shift[:, None]], axis=1)
    vmem, smem = pl.BlockSpec(memory_space=pltpu.VMEM), pl.BlockSpec(memory_space=pltpu.SMEM)
    dma = pltpu.SemaphoreType.DMA

    def params(collective):
        return pltpu.CompilerParams(
            collective_id=collective, has_side_effects=True, vmem_limit_bytes=60 * 2**20
        )

    if quadrants_fit(n, lax.axis_size("grp"), pc, rows, width):
        return quadrants_call(
            n, coupling_owner, coupling_slot, coupling_fock, pair_shift, coefficients, domain,
            amplitudes_start, exchange_integrals, pno_energy,
        )

    big = (width, width)
    x_shape = jax.ShapeDtypeStruct((n, quarter, *big), BF16)
    block_scratch = [
        pltpu.VMEM((n, pc, rows, width), BF16),
        pltpu.VMEM((n, pc, rows), jnp.int32),
        pltpu.VMEM((pc, width, NB), BF16),
        pltpu.VMEM((pc, NB, width), BF16),
        pltpu.VMEM((2, 2 * quarter, *big), F32),
        pltpu.VMEM((2, 2 * quarter, *big), F32),
        pltpu.VMEM((n, 2 * quarter, *big), F32),
        pltpu.VMEM((2, quarter, *big), F32),
        pltpu.VMEM((n, quarter, *big), F32),
        pltpu.VMEM((n, quarter, *big), F32),
        dma((2, steps, 3)), dma((2, steps, 3)),
        dma((n,)), dma((n,)), dma((n,)), dma((n,)),
    ]
    amp_scratch = [
        pltpu.VMEM((n * pc, *big), BF16),
        pltpu.VMEM((pc, *big), BF16),
        pltpu.VMEM((quarter, *big), F32),
        pltpu.VMEM((quarter, *big), BF16),
        dma((2, steps, 4)), dma((2, steps, 4)),
        dma((n, 4)), dma((n, 4)), dma((n + 1,)), dma((n + 1,)), dma((3,)), dma((3,)),
    ]
    half_shape = jax.ShapeDtypeStruct((quarter, *big), BF16)

    def iterate(first, start, x):
        return pl.pallas_call(
            functools.partial(iteration_alone, n, first),
            out_shape=half_shape if first else jax.ShapeDtypeStruct((pc, *big), BF16),
            in_specs=[smem, smem, vmem, vmem, vmem, vmem],
            out_specs=vmem,
            scratch_shapes=amp_scratch,
            compiler_params=params(1 if first else 2),
            name="first" if first else "second",
        )(slots, focks, start, x, exchange_integrals, pno_energy)

    held = n * width * (2 * pc * (rows + width) + 4 * width * 4 * quarter + 2 * width * quarter)
    if held < 40 * 2**20:
        return pl.pallas_call(
            functools.partial(opening, n, len(block_scratch)),
            out_shape=jax.ShapeDtypeStruct((pc, *big), BF16),
            in_specs=[smem, smem, vmem, vmem, vmem, vmem, vmem],
            out_specs=vmem,
            scratch_shapes=[
                pltpu.VMEM(x_shape.shape, BF16), pltpu.VMEM(half_shape.shape, BF16),
                *block_scratch, *amp_scratch, *amp_scratch,
            ],
            compiler_params=params(0),
            name="amplitudes",
        )(slots, focks, coefficients, domain, amplitudes_start, exchange_integrals, pno_energy).astype(F32)
    else:
        x = pl.pallas_call(
            functools.partial(intersections_alone, n),
            out_shape=x_shape,
            in_specs=[smem, vmem, vmem],
            out_specs=vmem,
            scratch_shapes=block_scratch,
            compiler_params=params(0),
            name="intersections",
        )(slots, coefficients, domain)
        amps = iterate(True, amplitudes_start, x)
    return iterate(False, amps, x).astype(F32)


def solution(mesh):
    placed = (
        P("pairs", "grp", None),
        P("pairs", "grp"),
        P("pairs", None),
        P("pairs", None),
        P("pairs", None),
        P("pairs", None, None),
        P("pairs", None),
        P("pairs"),
        P("pairs", None, None),
    )
    return jax.shard_map(
        on_device, mesh=mesh, in_specs=placed, out_specs=P("pairs", None, None), check_vma=False
    )
```

```python
import functools

import jax
import jax.numpy as jnp
from jax import lax
from jax.experimental import pallas as pl
from jax.experimental.pallas import tpu as pltpu
from jax.sharding import PartitionSpec as P

NB = 192
MESH = pl.DeviceIdType.MESH
F32, BF16 = jnp.float32, jnp.bfloat16


def ring_position(rank, n):
    odd = rank % 2
    return (1 - odd) * (rank // 2) + odd * (n - 1 - rank // 2)


def ring_rank(position, n):
    back = position // (n // 2)
    return (1 - back) * 2 * position + back * (2 * (n - 1 - position) + 1)


def places(n):
    p, g = lax.axis_index("pairs"), lax.axis_index("grp")
    position = ring_position(p, n)
    core, half = g % 2, g // 2
    mate = 2 * half + (1 - core)
    across = 2 * (1 - half) + core
    return p, g, position, mate, across


def at(position, n):
    return ring_rank((position + n) % n, n)


def greet(peers):
    barrier = pltpu.get_barrier_semaphore()
    for peer in peers:
        pl.semaphore_signal(barrier, inc=1, device_id=peer, device_id_type=MESH)
    pl.semaphore_wait(barrier, len(peers))


def remote(src, dst, send, recv, peer):
    return pltpu.make_async_remote_copy(
        src_ref=src, dst_ref=dst, send_sem=send, recv_sem=recv, device_id=peer, device_id_type=MESH
    )


def ring_parts(steps, parts):
    def of(step, direction):
        if step < steps:
            return tuple(range(parts))
        return tuple(c for c in range(parts) if c % 2 == direction)

    return of


def intersections(
    n, slot_ref, c_ref, dom_ref, out_ref,
    cbuf, dbuf, turned, wide, own, msend, mrecv, ysend, yrecv, keep,
    rs, rr, ms, mr, ys, yr,
):
    p, g, position, mate, across = places(n)
    pc = c_ref.shape[0]
    quarter = pc // 4
    rows = c_ref.shape[1]
    steps = n // 2
    right, left = at(position + 1, n), at(position - 1, n)
    ring_peer = (lambda r: (r, g))
    peers = [(right, g), (left, g), (p, mate), (p, across)]
    greet(peers)
    parts_of = ring_parts(steps, 3)
    hp = pc // 2

    def part(ref_c, ref_d, c):
        if c == 2:
            return ref_d
        return ref_c.at[pl.ds(c * hp, hp)]

    def move(step, direction, c):
        offset = -(step - 1) if direction == 0 else step - 1
        rank = at(position + offset, n)
        if step == 1:
            src = part(c_ref, dom_ref, c)
        else:
            src = part(cbuf.at[rank], dbuf.at[rank], c)
        dst = part(cbuf.at[rank], dbuf.at[rank], c)
        return remote(
            src, dst, rs.at[direction, step - 1, c], rr.at[direction, step - 1, c],
            ring_peer(right if direction == 0 else left),
        )

    def arrive(step, direction, c):
        offset = -step if direction == 0 else step
        rank = at(position + offset, n)
        dst = part(cbuf.at[rank], dbuf.at[rank], c)
        remote(
            dst, dst, rs.at[direction, step - 1, c], rr.at[direction, step - 1, c],
            ring_peer(left if direction == 0 else right),
        ).wait_recv()

    for c in (2, 0, 1):
        for d in (0, 1):
            if c in parts_of(1, d):
                move(1, d, c).start()

    base = g * NB
    lines = lax.broadcasted_iota(jnp.int32, (NB, rows), 0)
    core, half = g % 2, g // 2

    def expand(block, doms):
        def one(s, carry):
            hit = (lines == (doms[pl.ds(s, 1), :] - base)).astype(F32).astype(BF16)
            wide[s] = jnp.dot(hit, block[s], preferred_element_type=F32).astype(BF16)
            return carry

        lax.fori_loop(0, pc, one, 0, unroll=8)

    def mate_copy(k, rank):
        return remote(msend.at[k % 2], mrecv.at[rank], ms.at[k], mr.at[k], (p, mate))

    def across_copy(k, rank):
        return remote(ysend.at[k % 2], yrecv.at[rank], ys.at[k], yr.at[k], (p, across))

    ranks = []

    def product(t, rank):
        return jnp.dot(turned[t], wide[slot_ref[t, rank]], preferred_element_type=F32)

    def links(k, rank):
        if k >= 2:
            mate_copy(k - 2, ranks[k - 2]).wait_send()

        def theirs(i, carry):
            t = (2 * (i // quarter) + 1 - core) * quarter + i % quarter
            msend[k % 2, i] = product(t, rank)
            return carry

        lax.fori_loop(0, 2 * quarter, theirs, 0, unroll=8)
        mate_copy(k, rank).start()

        def ours(i, carry):
            t = (2 * (i // quarter) + core) * quarter + i % quarter
            own[k % 2, i] = product(t, rank)
            return carry

        lax.fori_loop(0, 2 * quarter, ours, 0, unroll=8)

    def finish(k):
        rank = ranks[k]
        if k >= 2:
            across_copy(k - 2, ranks[k - 2]).wait_send()
        mate_copy(k, rank).wait_recv()

        def send(j, carry):
            i = (1 - half) * quarter + j
            ysend[k % 2, j] = own[k % 2, i] + mrecv[rank, i]
            return carry

        lax.fori_loop(0, quarter, send, 0)
        across_copy(k, rank).start()

        def hold(j, carry):
            i = half * quarter + j
            keep[rank, j] = own[k % 2, i] + mrecv[rank, i]
            return carry

        lax.fori_loop(0, quarter, hold, 0)

    def process(rank):
        k = len(ranks)
        ranks.append(rank)
        links(k, rank)

    expand(c_ref, dom_ref)

    def turn(t, carry):
        turned[t] = wide[t].astype(F32).T.astype(BF16)
        return carry

    lax.fori_loop(0, pc, turn, 0, unroll=2)
    process(p)
    finish(0)
    for step in range(1, steps + 1):
        for c in (2, 0, 1):
            for d in (0, 1):
                if c in parts_of(step, d):
                    arrive(step, d, c)
                if step < steps and c in parts_of(step + 1, d):
                    move(step + 1, d, c).start()
        if step == steps - 1:
            yield None
        for d in (0, 1) if step < steps else (0,):
            rank = at(position + (-step if d == 0 else step), n)
            expand(cbuf.at[rank], dbuf.at[rank])
            process(rank)
            if d == 1:
                finish(len(ranks) - 2)
        finish(len(ranks) - 1)
    def settle(k):
        rank = ranks[k]
        across_copy(k, rank).wait_recv()

        def last(j, carry):
            out_ref[rank, j] = (keep[rank, j] + yrecv[rank, j]).astype(BF16)
            return carry

        lax.fori_loop(0, quarter, last, 0)

    yield settle
    for k in (n - 2, n - 1):
        mate_copy(k, ranks[k]).wait_send()
        across_copy(k, ranks[k]).wait_send()
    for step in range(1, steps + 1):
        for d in (0, 1):
            for c in parts_of(step, d):
                move(step, d, c).wait_send()


def iteration(
    n, first, joined, alone, slot_ref, fock_ref, start_ref, x_ref, k_ref, e_ref, out_ref,
    abuf, stage, acc, mine, rs, rr, ms, mr, ys, yr, fs, fr,
):
    p, g, position, mate, across = places(n)
    pc = k_ref.shape[0]
    width = k_ref.shape[1]
    quarter = pc // 4
    eighth = quarter // 2
    steps = n // 2
    right, left = at(position + 1, n), at(position - 1, n)
    diagonal = 3 - g
    if alone:
        greet([(right, g), (left, g), (p, mate), (p, across)])
    parts = 4 if joined else 3
    parts_of = ring_parts(steps, parts)

    def chunk(rank, group, c):
        return abuf.at[pl.ds(rank * pc + group * quarter + (c % 2) * eighth, eighth)]

    def span(rank, c):
        return chunk(rank, g if c < 2 else across, c)

    def ring_copy(step, direction, c):
        offset = -(step - 1) if direction == 0 else step - 1
        ref = span(at(position + offset, n), c)
        src = ref
        if step == 1 and c < 2 and not first:
            src = start_ref.at[pl.ds(c * eighth, eighth)]
        return remote(
            src, ref, rs.at[direction, step - 1, c], rr.at[direction, step - 1, c],
            (right if direction == 0 else left, g),
        )

    def arrive(step, direction, c):
        offset = -step if direction == 0 else step
        ref = span(at(position + offset, n), c)
        remote(
            ref, ref, rs.at[direction, step - 1, c], rr.at[direction, step - 1, c],
            (left if direction == 0 else right, g),
        ).wait_recv()

    def mate_copy(k, rank, c, src=None):
        ref = span(rank, c)
        return remote(ref if src is None else src, ref, ms.at[k, c], mr.at[k, c], (p, mate))

    def mate_wait(k, rank):
        for c in range(4):
            ref = chunk(rank, mate if c < 2 else diagonal, c)
            remote(ref, ref, ms.at[k, c], mr.at[k, c], (p, mate)).wait_recv()

    def across_copy(k, rank, c=1, src=None):
        ref = span(rank, c)
        sem = k if c == 1 else n
        return remote(ref if src is None else src, ref, ys.at[sem], yr.at[sem], (p, across))

    def across_wait(k, rank, c=3):
        ref = span(rank, c)
        sem = k if c == 3 else n
        remote(ref, ref, ys.at[sem], yr.at[sem], (p, across)).wait_recv()

    def own_half(c):
        return start_ref.at[pl.ds(c * eighth, eighth)]

    if first:
        def copy_own(i, carry):
            abuf[p * pc + i] = start_ref[i].astype(BF16)
            return carry

        def group_in(group):
            lax.fori_loop(group * quarter, (group + 1) * quarter, copy_own, 0)

        group_in(g)
        for c in (0, 1):
            for d in (0, 1):
                if c in parts_of(1, d):
                    ring_copy(1, d, c).start()
        group_in(across)
        for c in range(2, parts):
            for d in (0, 1):
                if c in parts_of(1, d):
                    ring_copy(1, d, c).start()
        group_in(mate)
        group_in(diagonal)
    else:
        for c in (0, 1):
            across_copy(0, p, c, own_half(c)).start()
            for d in (0, 1):
                if c in parts_of(1, d):
                    ring_copy(1, d, c).start()
        for c in (0, 1):
            mate_copy(0, p, c, own_half(c)).start()

        def copy_own(i, carry):
            abuf[p * pc + g * quarter + i] = start_ref[i]
            return carry

        lax.fori_loop(0, quarter, copy_own, 0)
        across_wait(0, p, 2)
        for d in (0, 1):
            if 2 in parts_of(1, d):
                ring_copy(1, d, 2).start()
        mate_copy(0, p, 2).start()
        across_wait(0, p, 3)
        mate_copy(0, p, 3).start()
        mate_wait(0, p)

    settle = yield None
    acc[...] = jnp.zeros_like(acc)

    def couple(rank, k):
        if settle is not None:
            settle(k)

        def copy(i, carry):
            stage[i] = abuf[rank * pc + i]
            return carry

        lax.fori_loop(0, pc, copy, 0, unroll=4)

        def one(j, carry):
            t = g * quarter + j
            source = stage[slot_ref[t, rank]]
            x = x_ref[rank, j]
            h = jnp.dot(x, source, preferred_element_type=F32).astype(BF16)
            y = lax.dot_general(h, x, (((1,), (1,)), ((), ())), preferred_element_type=F32)
            acc[j] += fock_ref[t, rank] * y
            return carry

        lax.fori_loop(0, quarter, one, 0, unroll=4)

    couple(p, 0)

    def exchange(blocks):
        for k, rank in () if joined else blocks:
            across_wait(k, rank)
            mate_copy(k, rank, 3).start()

    def use(blocks):
        for k, rank in blocks:
            mate_wait(k, rank)
            couple(rank, k)

    landed, shared = [], []
    for step in range(1, steps + 1):
        for c in (1, 0, 2, 3)[:parts]:
            for d in (0, 1):
                rank = at(position + (-step if d == 0 else step), n)
                if c in parts_of(step, d):
                    arrive(step, d, c)
                    if step < steps and c in parts_of(step + 1, d):
                        ring_copy(step + 1, d, c).start()
                    k = 2 * step - 1 + (d if step < steps else 0)
                    if c == 1 and not joined:
                        across_copy(k, rank).start()
                    mate_copy(k, rank, c).start()
        exchange(landed)
        use(shared)
        shared = landed
        landed = [
            (2 * step - 1 + d, at(position + (-step if d == 0 else step), n))
            for d in ((0, 1) if step < steps else (0,))
        ]
    exchange(landed)
    use(shared)
    use(landed)

    def scaled(j):
        t = g * quarter + j
        row = jnp.broadcast_to(e_ref[pl.ds(t, 1), :], (width, width))
        return (-(k_ref[t] + acc[j]) / (row.T + row + fock_ref[t, n])).astype(BF16)

    if first:
        def result(j, carry):
            out_ref[j] = scaled(j)
            return carry

        lax.fori_loop(0, quarter, result, 0, unroll=2)
    else:
        def block(ref, group):
            return ref.at[pl.ds(group * quarter, quarter)]

        def result(j, carry):
            value = scaled(j)
            mine[j] = value
            out_ref[g * quarter + j] = value
            return carry

        lax.fori_loop(0, quarter, result, 0, unroll=2)
        over = remote(mine, block(out_ref, g), fs.at[0], fr.at[0], (p, across))
        beside = remote(mine, block(out_ref, g), fs.at[1], fr.at[1], (p, mate))
        corner = remote(
            block(out_ref, across), block(out_ref, across), fs.at[2], fr.at[2], (p, mate)
        )
        over.start()
        beside.start()
        remote(mine, block(out_ref, across), fs.at[0], fr.at[0], (p, across)).wait_recv()
        corner.start()
        remote(mine, block(out_ref, mate), fs.at[1], fr.at[1], (p, mate)).wait_recv()
        remote(mine, block(out_ref, diagonal), fs.at[2], fr.at[2], (p, mate)).wait_recv()
        over.wait_send()
        beside.wait_send()
        corner.wait_send()
        across_copy(0, p, 0, own_half(0)).wait_send()
        across_copy(0, p, 1, own_half(1)).wait_send()
        for c in range(4):
            mate_copy(0, p, c).wait_send()
    for k in range(1, n):
        if not joined:
            across_copy(k, p).wait_send()
        for c in range(4):
            mate_copy(k, p, c).wait_send()
    for step in range(1, steps + 1):
        for d in (0, 1):
            for c in parts_of(step, d):
                ring_copy(step, d, c).wait_send()


def intersections_alone(*args):
    steps = intersections(*args)
    next(steps)
    settle = next(steps)
    for k in range(args[0]):
        settle(k)
    next(steps, None)


def iteration_alone(n, first, *args):
    steps = iteration(n, first, False, True, *args)
    next(steps)
    try:
        steps.send(None)
    except StopIteration:
        pass


def opening(
    n, made, slot_ref, fock_ref, c_ref, dom_ref, start_ref, k_ref, e_ref, out_ref,
    x_ref, amp_ref, *scratch
):
    used = made + (len(scratch) - made) // 2
    blocks = intersections(n, slot_ref, c_ref, dom_ref, x_ref, *scratch[:made])
    next(blocks)
    amps = iteration(
        n, True, True, False, slot_ref, fock_ref, start_ref, x_ref, k_ref, e_ref, amp_ref,
        *scratch[made:used],
    )
    next(amps)
    settle = next(blocks)
    try:
        amps.send(settle)
    except StopIteration:
        pass
    amps = iteration(
        n, False, False, False, slot_ref, fock_ref, amp_ref, x_ref, k_ref, e_ref, out_ref,
        *scratch[used:],
    )
    next(amps)
    try:
        amps.send(None)
    except StopIteration:
        pass
    next(blocks, None)


class Wires:
    def __init__(self, send, recv, here):
        self.send, self.recv, self.here = send, recv, here
        self.sends, self.recvs = {}, {}

    def link(self, key, src, dst, peer, out):
        at_send = self.sends.setdefault(out, len(self.sends))
        at_recv = self.recvs.setdefault(key, len(self.recvs))
        return remote(src, dst, self.send.at[at_send], self.recv.at[at_recv], peer)

    def start_in(self, when, key, src, dst, peer, out):
        self.link(key, src, dst, peer, out).start()

    def start(self, key, src, dst, peer, out, when=None):
        def run():
            self.start_in(when, key, src, dst, peer, out)

        if when is None:
            run()
        else:
            pl.when(when)(run)

    def wait(self, key, dst, when=None):
        at_recv = self.recvs.setdefault(key, len(self.recvs))
        copy = remote(dst, dst, self.send.at[0], self.recv.at[at_recv], self.here)
        if when is None:
            copy.wait_recv()
        else:
            pl.when(when)(copy.wait_recv)

    def drain(self, out, whole, when=None):
        at_send = self.sends[out]
        copy = remote(whole, whole, self.send.at[at_send], self.recv.at[0], self.here)
        if when is None:
            copy.wait_send()
        else:
            pl.when(when)(copy.wait_send)


def note(*what):
    return None


def quadrants(
    n, owner_hbm, slot_hbm, fock_hbm, shift_hbm, c_hbm, dom_hbm, start_ref, k_ref, e_hbm, out_ref,
    owner_ref, slot_ref, fock_ref, shift_ref, c_ref, dom_ref, e_ref, src, dom, blocks, bdom, bslot, bfock, wide, turned, x, start, k_own, amps_a, amps_b, amps_c, amps_d,
    acc, yout, yx, ysum, yin, mine, theirs, inverse, send, recv, local,
):
    p, g = lax.axis_index("pairs"), lax.axis_index("grp")
    pc, rows, width = c_ref.shape
    quarter = pc // 4
    half_quarter = quarter // 2
    layers = n // 2
    layer, column = p // 2, p % 2
    inner = (layer % 2 + layer // 2) % 2
    mid, end = inner == 1, inner == 0
    partner = (layer + 1 - 2 * (layer % 2)) * 2 + column
    cross = (layers - 1 - layer) * 2 + column
    far = ((layer + layers // 2) % layers) * 2 + column
    beside = layer * 2 + 1 - column
    groups = (g, g + 1 - 2 * (g % 2), (g + 2) % 4, 3 - g)
    _, mate, across, diagonal = groups
    to_mate, to_across = (p, mate), (p, across)
    to_partner, to_cross, to_beside, to_far = (partner, g), (cross, g), (beside, g), (far, g)
    wires = Wires(send, recv, to_mate)
    amps = ((amps_a, amps_b), (amps_c, amps_d))
    wires.mid = mid

    barrier = pltpu.get_barrier_semaphore()

    def hello(peer):
        pl.semaphore_signal(barrier, inc=1, device_id=peer, device_id_type=MESH)

    for peer in (to_partner, to_beside, to_across, to_mate):
        hello(peer)
    pl.when(mid)(lambda: hello(to_cross))

    pairs = (
        (c_hbm, c_ref), (dom_hbm, dom_ref), (owner_hbm, owner_ref), (slot_hbm, slot_ref),
        (fock_hbm, fock_ref), (shift_hbm, shift_ref), (e_hbm, e_ref), (start_ref, start),
        (k_ref.at[pl.ds(g * quarter, quarter)], k_own),
    )
    loads = [pltpu.make_async_copy(*pair, local.at[i]) for i, pair in enumerate(pairs)]
    for load in loads:
        load.start()
    load_c, load_dom, load_owner, load_slot, load_fock, load_shift, load_e, load_start, load_k = loads
    load_c.wait()
    load_dom.wait()

    def four(group):
        return pl.ds(group * quarter, quarter)

    def two(group, h):
        return pl.ds(group * quarter + h * half_quarter, half_quarter)

    def both_quarters(ref):
        return ref.at[pl.ds(0, 2 * quarter)]

    def three_quarters(ref):
        return ref.at[pl.ds(0, 3 * quarter)]

    def source(b, rel):
        return c_ref if (b, rel) == (0, 0) else src.at[4 * b + rel]

    def turn(rel, b=0):
        for t in range(quarter):
            blocks[b, rel, t] = source(b, rel)[g * quarter + t].T

    for s in range(pc):
        dom[0, s] = dom_ref[pl.ds(s, 1), :]
    turn(0)

    def table(t, carry):
        at_pair = g * quarter + t
        ways = owner_ref.shape[0]
        named = [owner_ref[k, at_pair] for k in range(ways)]
        slots = [slot_ref[k, at_pair] for k in range(ways)]
        focks = [fock_ref[k, at_pair] for k in range(ways)]
        for owner in range(n):
            place, weight = 0, 0.0
            for k in range(ways):
                hit = named[k] == owner
                place = jnp.where(hit, slots[k], place)
                weight = jnp.where(hit, focks[k], weight)
            bslot[0, t, owner] = place
            bfock[0, t, owner] = weight
        return carry

    small = ("slot", "fock", "dom")
    kinds = {
        "slot": lambda b: bslot.at[b],
        "fock": lambda b: bfock.at[b],
        "dom": lambda b: bdom.at[b],
    }
    for rel in range(4):
        for h in (0, 1):
            kinds[rel, h] = functools.partial(
                lambda rel, h, b: blocks.at[b, rel, pl.ds(h * half_quarter, half_quarter)], rel, h
            )
        kinds[rel] = functools.partial(lambda rel, b: blocks.at[b, rel], rel)

    def tag(kind):
        return kind if kind in small else "targets"

    def landing(kind):
        return kind if kind in small or kind in ((3, 0), (3, 1)) else 0

    def ready(kind):
        ref = kinds[kind](0)
        onward, across_cut = kinds[kind](4), kinds[kind](2)
        if kind in ("slot", "fock"):
            wires.start(("second", kind), ref, kinds[kind](1), to_partner, kind)
        wires.start(("beside", 0 if tag(kind) == "targets" else kind), ref, onward, to_beside, tag(kind), end)
        wires.start(("cross", kind), ref, across_cut, to_cross, tag(kind), mid)

    def next_ready(kind):
        ref = kinds[kind](1)
        onward, across_cut = kinds[kind](5), kinds[kind](3)
        if kind in ("slot", "fock"):
            wires.wait(("second", kind), ref)
        wires.start(("beside2", landing(kind)), ref, onward, to_beside, tag(kind), end)
        wires.start(("further", kind), ref, across_cut, to_cross, tag(kind), mid)

    def got_first(kind):
        landed, passed = kinds[kind](2), kinds[kind](4)

        def relay():
            wires.wait(("cross", kind), landed)
            key = ("beside", 0 if tag(kind) == "targets" else kind)
            wires.start_in(mid, key, landed, passed, to_beside, tag(kind))

        pl.when(mid)(relay)

    def got_further(kind):
        landed, passed = kinds[kind](3), kinds[kind](5)

        def relay():
            wires.wait(("further", kind), landed)
            wires.start_in(mid, ("beside2", landing(kind)), landed, passed, to_beside, tag(kind))

        pl.when(mid)(relay)

    def got_beside():
        for kind in small:
            wires.wait(("beside", kind), kinds[kind](4))
        wires.wait(("beside", 0), blocks.at[4])

    def got_beside2():
        for kind in small:
            wires.wait(("beside2", kind), kinds[kind](5))
        wires.wait(("beside2", 0), blocks.at[5, pl.ds(0, 3)])

    first, second = 2 * inner, 1 + 2 * inner
    places_of = (first, 4, second, 5)

    lines = lax.broadcasted_iota(jnp.int16, (NB, rows), 0)
    lines2 = lax.broadcasted_iota(jnp.int16, (2 * NB, 2 * rows), 0)

    def one_hot(numbers, row):
        hit = numbers == row.astype(jnp.int16)
        return jnp.where(hit, jnp.ones(hit.shape, BF16), jnp.zeros(hit.shape, BF16))

    def expand(b, rel, parts=(0, 1, 2, 3)):
        base = groups[rel] * NB
        block = source(b, rel)

        def one(s, carry):
            hit = one_hot(lines, dom[4 * b + rel, s] - base)
            wide[b, s, pl.ds(rel * NB, NB)] = jnp.dot(
                hit, block[s], preferred_element_type=F32
            ).astype(BF16)
            return carry

        if len(parts) == 4:
            note("expand", b, rel)
            lax.fori_loop(0, pc, one, 0, unroll=4)
            return
        for i in parts:
            note("expand4", b, rel)
            for t in range(quarter):
                one(groups[i] * quarter + t, 0)

    every = tuple(range(quarter))
    early, later = every[:half_quarter], every[half_quarter:]

    def make_turned(b, hs=(0, 1), ts=every):
        note("make_turned", b, 0, len(hs) * len(ts) / 8)
        place = places_of[b]

        def one(t, carry):
            for h in hs:
                u, v = 2 * h, 2 * h + 1
                row = jnp.concatenate(
                    [
                        bdom[place, u * quarter + t] - groups[u] * NB,
                        bdom[place, v * quarter + t] - groups[v] * NB + NB,
                    ],
                    axis=1,
                )
                hit = one_hot(lines2, row)
                both = jnp.concatenate([blocks[place, u, t], blocks[place, v, t]], axis=1)
                turned[b, t, :, pl.ds(h * 2 * NB, 2 * NB)] = lax.dot_general(
                    both, hit, (((1,), (1,)), ((), ())), preferred_element_type=F32
                ).astype(BF16)
            return carry

        if ts == every:
            lax.fori_loop(0, quarter, one, 0, unroll=2)
        else:
            for t in ts:
                one(t, 0)

    owners = (p, partner)

    def make_x(b, s, ts=every):
        note("make_x", b, s, len(ts) / 4)
        place = places_of[b]

        def one(t, carry):
            at_source = bslot[place, t, owners[s]]
            x[b, t, s] = jnp.dot(
                turned[b, t], wide[s, at_source], preferred_element_type=F32
            ).astype(BF16)
            return carry

        for t in ts:
            one(t, 0)

    def couple(b, s, it, ts=every):
        note("couple", b, s, len(ts) / 4)
        place = places_of[b]
        found = []
        for t in ts:
            at_source = bslot[place, t, owners[s]]
            xs = x[b, t, s]
            half = jnp.dot(xs, amps[it][s][at_source], preferred_element_type=F32).astype(BF16)
            found.append((t, xs, half))
        for t, xs, half in found:
            y = lax.dot_general(half, xs, (((1,), (1,)), ((), ())), preferred_element_type=F32)
            y = bfock[place, t, owners[s]] * y
            if s == 0:
                acc[b, t] = y
            elif b % 2 == 0:
                acc[b, t] += y
            else:
                yout[it, b // 2, t] = (acc[b, t] + y).astype(BF16)

    def post(it, m, ts=every):
        for t in ts:
            wires.start(("y", it, m, t), yout.at[it, m, t], yx.at[it, m, t], to_beside, "y")

    def share(t):
        at_pair = g * quarter + t
        ref = amps[1][0].at[at_pair]
        wires.start(("own", 1, t), ref, ref, to_across, "amps")
        wires.start(("own", 2), ref, ref, to_mate, "amps")

    def share_partner(t, when):
        at_pair = g * quarter + t
        wires.start(("a", 1, 0, t), amps[1][0].at[at_pair], amps[1][1].at[at_pair], to_partner, "amps", when)

    def pass_partner(t):
        ref = amps[1][1].at[g * quarter + t]
        wires.wait(("a", 1, 0, t), ref)
        wires.start(("a", 1, 1, t), ref, ref, to_across, "amps")
        wires.start(("a", 1, 2), ref, ref, to_mate, "amps")

    def pass_own(t):
        ref = amps[1][0].at[across * quarter + t]
        wires.wait(("own", 1, t), ref)
        wires.start(("own", 2), ref, ref, to_mate, "amps")

    def pass_across(t):
        ref = amps[1][1].at[across * quarter + t]
        wires.wait(("a", 1, 1, t), ref)
        wires.start(("a", 1, 2), ref, ref, to_mate, "amps")

    def share_start(j):
        part = four((g, across)[j])
        wires.start(("start", j), amps[0][0].at[part], amps[0][1].at[part], to_partner, "amps")

    def pass_start(j):
        ref = amps[0][1].at[four((g, across)[j])]
        wires.wait(("start", j), ref)
        wires.start(("a", 0, 2), ref, ref, to_mate, "amps")

    def have_partner(it):
        wires.wait(("a", it, 2), both_quarters(amps[it][1]))

    def sum_second(it):
        for t in range(quarter):
            wires.wait(("y", it, 1, t), yx.at[it, 1, t])
            ysum[it, 1, t] = (acc[2, t] + yx[it, 1, t].astype(F32)).astype(BF16)
            job = (("yfar", it, t), ysum.at[it, 1, t], yin.at[it, 0, t])
            wires.start(*job, to_partner, "yfar", end)
            wires.start(*job, to_far, "yfar", mid)

    def sum_first(it, ts=every):
        for t in ts:
            wires.wait(("y", it, 0, t), yx.at[it, 0, t])
            total = acc[0, t] + yx[it, 0, t].astype(F32)
            acc[0, t] = total
            ysum[it, 0, t] = total.astype(BF16)
            wires.start(("ynear", it, t), ysum.at[it, 0, t], yin.at[it, 1, t], to_cross, "ynear", mid)

    def coupled(it, t):
        wires.wait(("ynear", it, t), yin.at[it, 1, t], mid)
        wires.wait(("yfar", it, t), yin.at[it, 0, t])
        near = yin[it, 1, t].astype(F32)
        return yin[it, 0, t].astype(F32) + jnp.where(mid, near, acc[0, t])

    def invert(t, carry):
        at_pair = g * quarter + t
        row = jnp.broadcast_to(e_ref[pl.ds(at_pair, 1), :], (width, width))
        over = 1.0 / (row.T + row + shift_ref[at_pair])
        inverse[t] = over
        k_own[t] = k_own[t] * over
        return carry

    def updated(it, t):
        return (-(k_own[t] + coupled(it, t) * inverse[t])).astype(BF16)

    swap_mate, swap_across = (1, 0, 3, 2), (2, 3, 0, 1)

    def from_mate():
        wires.wait(("own mate", 1), src.at[1, four(g)])

    def from_mate_rest():
        wires.wait(("own mate", 0), three_quarters(src.at[1]))

    def from_across(i):
        part = four(groups[i])
        wires.wait(("own across", swap_across[i]), src.at[2, part])
        wires.start(
            ("own corner", int(i == 1)), src.at[2, part], src.at[3, part], to_mate,
            "rows",
        )

    def from_corner():
        wires.wait(("own corner", 1), src.at[3, four(g)])

    def from_corner_rest():
        wires.wait(("own corner", 0), three_quarters(src.at[3]))

    def to_next(i):
        part = four(groups[i])
        wires.start(
            ("next", i), c_ref.at[part], src.at[4, part], to_partner, "rows"
        )

    def from_next(i):
        part = four(groups[i])
        ref = src.at[4, part]
        wires.wait(("next", i), ref)
        if i > 0:
            wires.start(
                ("next across", i), ref, src.at[6, part], to_across, "rows",
            )
        wires.start(
            ("next mate", int(i == 1)), ref, src.at[5, part], to_mate, "rows",
        )

    def to_wide(i):
        part = four(groups[i])
        wires.start(
            ("next wide", i), src.at[2, part], src.at[6, part], to_partner, "rows",
        )

    def corner(i):
        part = four(groups[i])
        wires.start(
            ("next corner", int(i == 1)), src.at[6, part], src.at[7, part], to_mate, "rows",
        )

    def from_next_across(i):
        wires.wait(("next across", swap_across[i]), src.at[6, four(groups[i])])
        corner(i)

    def from_wide(i):
        wires.wait(("next wide", i), src.at[6, four(groups[i])])
        corner(i)

    def from_next_mate():
        wires.wait(("next mate", 1), src.at[5, four(g)])

    def from_next_mate_rest():
        wires.wait(("next mate", 0), three_quarters(src.at[5]))

    def from_next_corner():
        wires.wait(("next corner", 1), src.at[7, four(g)])

    def from_next_corner_rest():
        wires.wait(("next corner", 0), three_quarters(src.at[7]))

    def own_across(i):
        part = four(groups[i])
        wires.start(
            ("own across", i), c_ref.at[part], src.at[2, part], to_across, "rows",
        )

    def cast(s, carry):
        amps[0][0][s] = start[s].astype(BF16)
        return carry

    pl.semaphore_wait(barrier, 4 + inner)
    wires.start(("d", 1), dom.at[0], dom.at[1], to_mate, "doms")
    wires.start(("d", 2), dom.at[0], dom.at[2], to_across, "doms")
    own_across(2)
    to_next(0)
    ready((0, 0))
    ready((0, 1))
    for i in (1, 0, 2, 3):
        part = four(groups[i])
        wires.start(
            ("own mate", int(i == 1)), c_ref.at[part], src.at[1, part], to_mate, "rows",
        )
    own_across(3)
    own_across(0)
    to_next(2)
    from_mate()
    turn(1)
    ready((1, 0))
    ready((1, 1))
    wires.wait(("d", 1), dom.at[1])
    wires.wait(("d", 2), dom.at[2])
    wires.start(("d", 3), dom.at[2], dom.at[3], to_mate, "doms")
    for load in (load_owner, load_slot, load_fock):
        load.wait()
    lax.fori_loop(0, quarter, table, 0)
    ready("slot")
    ready("fock")
    wires.wait(("d", 3), dom.at[3])
    wires.start(("d", 4), dom.at[pl.ds(0, 4)], dom.at[pl.ds(4, 4)], to_partner, "doms")
    to_next(3)
    to_next(1)
    for rel in range(4):
        for t in range(quarter):
            bdom[0, rel * quarter + t] = dom[rel, g * quarter + t]
    ready("dom")
    got_first((0, 0))
    expand(0, 0)
    from_next(0)
    turn(0, 1)
    next_ready((0, 0))
    next_ready((0, 1))
    got_first((0, 1))
    from_across(0)
    turn(2)
    ready((2, 0))
    ready((2, 1))
    from_mate_rest()
    got_first((1, 0))
    expand(0, 1)
    from_next(2)
    got_first((1, 1))
    expand(0, 2, (0,))
    from_across(1)
    got_further((0, 0))
    from_corner()
    turn(3)
    ready((3, 0))
    ready((3, 1))
    load_start.wait()
    lax.fori_loop(0, pc, cast, 0, unroll=2)
    for load in (load_k, load_e, load_shift):
        load.wait()
    wires.wait(("d", 4), dom.at[pl.ds(4, 4)])
    expand(0, 2, (1,))
    from_across(2)
    to_wide(2)
    share_start(0)
    share_start(1)
    got_further((0, 1))
    expand(1, 0, (0, 2))
    from_next(3)
    own_across(1)
    expand(0, 2, (2,))
    got_first((2, 0))
    expand(1, 0, (3,))
    for rel in range(4):
        for t in range(quarter):
            bdom[1, rel * quarter + t] = dom[4 + rel, g * quarter + t]
    next_ready("dom")
    next_ready("slot")
    next_ready("fock")
    from_next_across(0)
    turn(2, 1)
    next_ready((2, 0))
    next_ready((2, 1))
    got_first((2, 1))
    from_next(1)
    expand(1, 0, (1,))
    got_first((3, 0))
    from_next_mate()
    turn(1, 1)
    next_ready((1, 0))
    next_ready((1, 1))
    from_next_mate_rest()
    expand(1, 1, (0, 1))
    from_next_across(1)
    got_first((3, 1))
    expand(1, 1, (2, 3))
    from_next_corner()
    turn(3, 1)
    next_ready((3, 0))
    next_ready((3, 1))
    for kind in small:
        got_first(kind)
    from_wide(2)
    got_further((2, 0))
    lax.fori_loop(0, half_quarter, invert, 0)
    expand(1, 2, (0, 1))
    from_across(3)
    got_further((2, 1))
    expand(1, 2, (2,))
    expand(0, 2, (3,))
    from_corner_rest()
    expand(0, 3, (0, 1))
    got_further((1, 0))
    expand(0, 3, (2, 3))
    make_turned(0)
    pass_start(0)
    got_further((1, 1))
    lax.fori_loop(half_quarter, quarter, invert, 0)
    from_next_across(3)
    make_x(0, 0)
    expand(1, 2, (3,))
    pass_start(1)
    for kind in small:
        got_further(kind)
    from_next_corner_rest()
    expand(1, 3)
    got_further((3, 0))
    got_beside()
    make_turned(1)
    make_x(1, 0)
    make_x(1, 1)
    have_partner(0)
    got_further((3, 1))
    couple(1, 0, 0)
    couple(1, 1, 0)
    post(0, 0, early)
    make_turned(2)
    make_x(2, 0)
    make_x(2, 1)
    couple(2, 0, 0)
    couple(2, 1, 0)
    got_beside2()
    make_turned(3, (0,))
    for h, ts in ((0, early), (1, later)):
        wires.wait(("beside2", (3, h)), kinds[3, h](5))
        make_turned(3, (1,), ts)
        make_x(3, 0, ts)
        make_x(3, 1, ts)
        couple(3, 0, 0, ts)
        couple(3, 1, 0, ts)
        post(0, 1, ts)
    post(0, 0, later)
    make_x(0, 1)
    couple(0, 0, 0)
    couple(0, 1, 0)
    sum_first(0, early)
    sum_second(0)
    sum_first(0, later)

    for t in range(quarter):
        amps[1][0][g * quarter + t] = updated(0, t)
        share_partner(t, None)
        share(t)
    for t in range(quarter):
        pass_partner(t)
        pass_own(t)
    wires.wait(("own", 2), both_quarters(amps[1][0]))
    couple(3, 0, 1)
    couple(1, 0, 1)
    for t in range(half_quarter):
        pass_across(t)
    couple(2, 0, 1)
    couple(0, 0, 1)
    for t in range(half_quarter, quarter):
        pass_across(t)
    have_partner(1)
    for b in (3, 1):
        for ts in (early, later):
            couple(b, 1, 1, ts)
            post(1, b // 2, ts)
    couple(2, 1, 1)
    couple(0, 1, 1)
    sum_second(1)
    sum_first(1)

    for t in range(quarter):
        mine[t] = coupled(1, t).astype(BF16)
        part = mine.at[t]
        wires.start(("out", 1, t), part, theirs.at[t], to_across, "amps")
        wires.start(("out", 2), part, out_ref.at[g * quarter + t], to_mate, "out")
    keep_mine = pltpu.make_async_copy(mine, out_ref.at[four(g)], local.at[9])
    keep_mine.start()
    for t in range(quarter):
        ref = theirs.at[t]
        wires.wait(("out", 1, t), ref)
        wires.start(("out", 2), ref, out_ref.at[across * quarter + t], to_mate, "out")
    keep_theirs = pltpu.make_async_copy(theirs, out_ref.at[four(across)], local.at[10])
    keep_theirs.start()
    wires.drain("rows", src.at[pl.ds(0, 7)])
    wires.drain("doms", dom.at[pl.ds(0, 7)])
    for role, passes in ((end, 2), (mid, 4)):
        wires.drain("targets", blocks.at[pl.ds(0, passes)], role)
        wires.drain("dom", bdom.at[pl.ds(0, passes)], role)
        wires.drain("slot", bslot.at[pl.ds(0, passes + 1)], role)
        wires.drain("fock", bfock.at[pl.ds(0, passes + 1)], role)
    wires.drain("y", yout)
    wires.drain("yfar", ysum.at[0])
    wires.drain("ynear", ysum.at[0], mid)
    wires.drain("amps", src.at[pl.ds(0, 3)])
    wires.drain("out", both_quarters(amps[1][0]))
    wires.wait(("out", 2), both_quarters(out_ref))
    keep_mine.wait()
    keep_theirs.wait()
    assert len(wires.sends) <= SENDS and len(wires.recvs) <= RECVS, (len(wires.sends), len(wires.recvs))


SENDS, RECVS = 11, 112


def quadrants_fit(n, groups, pc, rows, width):
    return n == 2 * groups and groups == 4 and pc % (2 * groups) == 0 and rows == width


def quadrants_kernel(n, *refs):
    quadrants(n, *refs)


def quadrants_call(
    n, owner, slot, fock, shift, coefficients, domain, start, integrals, energy
):
    pc, rows, width = coefficients.shape
    quarter = pc // 4
    big, ways = (width, width), owner.shape[1]
    hbm = pl.BlockSpec(memory_space=pl.ANY)
    dma = pltpu.SemaphoreType.DMA
    total = pl.pallas_call(
        functools.partial(quadrants_kernel, n),
        out_shape=jax.ShapeDtypeStruct((pc, *big), BF16),
        in_specs=[hbm] * 9,
        out_specs=hbm,
        scratch_shapes=[
            pltpu.SMEM((ways, pc), jnp.int32), pltpu.SMEM((ways, pc), jnp.int32),
            pltpu.SMEM((ways, pc), F32), pltpu.SMEM((pc,), F32),
            pltpu.VMEM((pc, rows, width), BF16), pltpu.VMEM((pc, rows), jnp.int32),
            pltpu.VMEM((pc, width), F32),
            pltpu.VMEM((8, pc, rows, width), BF16),
            pltpu.VMEM((8, pc, 1, rows), jnp.int32),
            pltpu.VMEM((6, 4, quarter, width, rows), BF16),
            pltpu.VMEM((6, 4 * quarter, 1, rows), jnp.int32),
            pltpu.SMEM((6, quarter, n), jnp.int32),
            pltpu.SMEM((6, quarter, n), F32),
            pltpu.VMEM((2, pc, 4 * NB, width), BF16),
            pltpu.VMEM((4, quarter, width, 4 * NB), BF16),
            pltpu.VMEM((4, quarter, 2, *big), BF16),
            pltpu.VMEM((pc, *big), F32),
            pltpu.VMEM((quarter, *big), F32),
            *[pltpu.VMEM((pc, *big), BF16)] * 4,
            pltpu.VMEM((4, quarter, *big), F32),
            pltpu.VMEM((2, 2, quarter, *big), BF16),
            pltpu.VMEM((2, 2, quarter, *big), BF16),
            pltpu.VMEM((2, 2, quarter, *big), BF16),
            pltpu.VMEM((2, 2, quarter, *big), BF16),
            pltpu.VMEM((quarter, *big), BF16), pltpu.VMEM((quarter, *big), BF16),
            pltpu.VMEM((quarter, *big), F32),
            dma((SENDS,)), dma((RECVS,)), dma((11,)),
        ],
        compiler_params=pltpu.CompilerParams(
            collective_id=0, has_side_effects=True, vmem_limit_bytes=60 * 2**20
        ),
        name="quadrants",
    )(owner.T, slot.T, fock.T, shift, coefficients, domain, start, integrals, energy)
    denominator = energy[:, :, None] + energy[:, None, :] + shift[:, None, None]
    return -(integrals + total.astype(F32)) / denominator


def on_device(
    coefficients, domain, coupling_owner, coupling_slot, coupling_fock,
    exchange_integrals, pno_energy, pair_shift, amplitudes_start,
):
    n = lax.axis_size("pairs")
    pc, rows, width = coefficients.shape
    quarter = pc // lax.axis_size("grp")
    steps = n // 2
    named = coupling_owner[:, :, None] == jnp.arange(n, dtype=jnp.int32)[None, None, :]
    slots = jnp.sum(jnp.where(named, coupling_slot[:, :, None], 0), axis=1)
    focks = jnp.sum(jnp.where(named, coupling_fock[:, :, None], 0.0), axis=1)
    focks = jnp.concatenate([focks, pair_shift[:, None]], axis=1)
    vmem, smem = pl.BlockSpec(memory_space=pltpu.VMEM), pl.BlockSpec(memory_space=pltpu.SMEM)
    dma = pltpu.SemaphoreType.DMA

    def params(collective):
        return pltpu.CompilerParams(
            collective_id=collective, has_side_effects=True, vmem_limit_bytes=60 * 2**20
        )

    if quadrants_fit(n, lax.axis_size("grp"), pc, rows, width):
        return quadrants_call(
            n, coupling_owner, coupling_slot, coupling_fock, pair_shift, coefficients, domain,
            amplitudes_start, exchange_integrals, pno_energy,
        )

    big = (width, width)
    x_shape = jax.ShapeDtypeStruct((n, quarter, *big), BF16)
    block_scratch = [
        pltpu.VMEM((n, pc, rows, width), BF16),
        pltpu.VMEM((n, pc, rows), jnp.int32),
        pltpu.VMEM((pc, width, NB), BF16),
        pltpu.VMEM((pc, NB, width), BF16),
        pltpu.VMEM((2, 2 * quarter, *big), F32),
        pltpu.VMEM((2, 2 * quarter, *big), F32),
        pltpu.VMEM((n, 2 * quarter, *big), F32),
        pltpu.VMEM((2, quarter, *big), F32),
        pltpu.VMEM((n, quarter, *big), F32),
        pltpu.VMEM((n, quarter, *big), F32),
        dma((2, steps, 3)), dma((2, steps, 3)),
        dma((n,)), dma((n,)), dma((n,)), dma((n,)),
    ]
    amp_scratch = [
        pltpu.VMEM((n * pc, *big), BF16),
        pltpu.VMEM((pc, *big), BF16),
        pltpu.VMEM((quarter, *big), F32),
        pltpu.VMEM((quarter, *big), BF16),
        dma((2, steps, 4)), dma((2, steps, 4)),
        dma((n, 4)), dma((n, 4)), dma((n + 1,)), dma((n + 1,)), dma((3,)), dma((3,)),
    ]
    half_shape = jax.ShapeDtypeStruct((quarter, *big), BF16)

    def iterate(first, start, x):
        return pl.pallas_call(
            functools.partial(iteration_alone, n, first),
            out_shape=half_shape if first else jax.ShapeDtypeStruct((pc, *big), BF16),
            in_specs=[smem, smem, vmem, vmem, vmem, vmem],
            out_specs=vmem,
            scratch_shapes=amp_scratch,
            compiler_params=params(1 if first else 2),
            name="first" if first else "second",
        )(slots, focks, start, x, exchange_integrals, pno_energy)

    held = n * width * (2 * pc * (rows + width) + 4 * width * 4 * quarter + 2 * width * quarter)
    if held < 40 * 2**20:
        return pl.pallas_call(
            functools.partial(opening, n, len(block_scratch)),
            out_shape=jax.ShapeDtypeStruct((pc, *big), BF16),
            in_specs=[smem, smem, vmem, vmem, vmem, vmem, vmem],
            out_specs=vmem,
            scratch_shapes=[
                pltpu.VMEM(x_shape.shape, BF16), pltpu.VMEM(half_shape.shape, BF16),
                *block_scratch, *amp_scratch, *amp_scratch,
            ],
            compiler_params=params(0),
            name="amplitudes",
        )(slots, focks, coefficients, domain, amplitudes_start, exchange_integrals, pno_energy).astype(F32)
    else:
        x = pl.pallas_call(
            functools.partial(intersections_alone, n),
            out_shape=x_shape,
            in_specs=[smem, vmem, vmem],
            out_specs=vmem,
            scratch_shapes=block_scratch,
            compiler_params=params(0),
            name="intersections",
        )(slots, coefficients, domain)
        amps = iterate(True, amplitudes_start, x)
    return iterate(False, amps, x).astype(F32)


def solution(mesh):
    placed = (
        P("pairs", "grp", None),
        P("pairs", "grp"),
        P("pairs", None),
        P("pairs", None),
        P("pairs", None),
        P("pairs", None, None),
        P("pairs", None),
        P("pairs"),
        P("pairs", None, None),
    )
    return jax.shard_map(
        on_device, mesh=mesh, in_specs=placed, out_specs=P("pairs", None, None), check_vma=False
    )
```

```python
import functools

import jax
import jax.numpy as jnp
from jax import lax
from jax.experimental import pallas as pl
from jax.experimental.pallas import tpu as pltpu
from jax.sharding import PartitionSpec as P

NB = 192
MESH = pl.DeviceIdType.MESH
F32, BF16 = jnp.float32, jnp.bfloat16


def ring_position(rank, n):
    odd = rank % 2
    return (1 - odd) * (rank // 2) + odd * (n - 1 - rank // 2)


def ring_rank(position, n):
    back = position // (n // 2)
    return (1 - back) * 2 * position + back * (2 * (n - 1 - position) + 1)


def places(n):
    p, g = lax.axis_index("pairs"), lax.axis_index("grp")
    position = ring_position(p, n)
    core, half = g % 2, g // 2
    mate = 2 * half + (1 - core)
    across = 2 * (1 - half) + core
    return p, g, position, mate, across


def at(position, n):
    return ring_rank((position + n) % n, n)


def greet(peers):
    barrier = pltpu.get_barrier_semaphore()
    for peer in peers:
        pl.semaphore_signal(barrier, inc=1, device_id=peer, device_id_type=MESH)
    pl.semaphore_wait(barrier, len(peers))


def remote(src, dst, send, recv, peer):
    return pltpu.make_async_remote_copy(
        src_ref=src, dst_ref=dst, send_sem=send, recv_sem=recv, device_id=peer, device_id_type=MESH
    )


def ring_parts(steps, parts):
    def of(step, direction):
        if step < steps:
            return tuple(range(parts))
        return tuple(c for c in range(parts) if c % 2 == direction)

    return of


def intersections(
    n, slot_ref, c_ref, dom_ref, out_ref,
    cbuf, dbuf, turned, wide, own, msend, mrecv, ysend, yrecv, keep,
    rs, rr, ms, mr, ys, yr,
):
    p, g, position, mate, across = places(n)
    pc = c_ref.shape[0]
    quarter = pc // 4
    rows = c_ref.shape[1]
    steps = n // 2
    right, left = at(position + 1, n), at(position - 1, n)
    ring_peer = (lambda r: (r, g))
    peers = [(right, g), (left, g), (p, mate), (p, across)]
    greet(peers)
    parts_of = ring_parts(steps, 3)
    hp = pc // 2

    def part(ref_c, ref_d, c):
        if c == 2:
            return ref_d
        return ref_c.at[pl.ds(c * hp, hp)]

    def move(step, direction, c):
        offset = -(step - 1) if direction == 0 else step - 1
        rank = at(position + offset, n)
        if step == 1:
            src = part(c_ref, dom_ref, c)
        else:
            src = part(cbuf.at[rank], dbuf.at[rank], c)
        dst = part(cbuf.at[rank], dbuf.at[rank], c)
        return remote(
            src, dst, rs.at[direction, step - 1, c], rr.at[direction, step - 1, c],
            ring_peer(right if direction == 0 else left),
        )

    def arrive(step, direction, c):
        offset = -step if direction == 0 else step
        rank = at(position + offset, n)
        dst = part(cbuf.at[rank], dbuf.at[rank], c)
        remote(
            dst, dst, rs.at[direction, step - 1, c], rr.at[direction, step - 1, c],
            ring_peer(left if direction == 0 else right),
        ).wait_recv()

    for c in (2, 0, 1):
        for d in (0, 1):
            if c in parts_of(1, d):
                move(1, d, c).start()

    base = g * NB
    lines = lax.broadcasted_iota(jnp.int32, (NB, rows), 0)
    core, half = g % 2, g // 2

    def expand(block, doms):
        def one(s, carry):
            hit = (lines == (doms[pl.ds(s, 1), :] - base)).astype(F32).astype(BF16)
            wide[s] = jnp.dot(hit, block[s], preferred_element_type=F32).astype(BF16)
            return carry

        lax.fori_loop(0, pc, one, 0, unroll=8)

    def mate_copy(k, rank):
        return remote(msend.at[k % 2], mrecv.at[rank], ms.at[k], mr.at[k], (p, mate))

    def across_copy(k, rank):
        return remote(ysend.at[k % 2], yrecv.at[rank], ys.at[k], yr.at[k], (p, across))

    ranks = []

    def product(t, rank):
        return jnp.dot(turned[t], wide[slot_ref[t, rank]], preferred_element_type=F32)

    def links(k, rank):
        if k >= 2:
            mate_copy(k - 2, ranks[k - 2]).wait_send()

        def theirs(i, carry):
            t = (2 * (i // quarter) + 1 - core) * quarter + i % quarter
            msend[k % 2, i] = product(t, rank)
            return carry

        lax.fori_loop(0, 2 * quarter, theirs, 0, unroll=8)
        mate_copy(k, rank).start()

        def ours(i, carry):
            t = (2 * (i // quarter) + core) * quarter + i % quarter
            own[k % 2, i] = product(t, rank)
            return carry

        lax.fori_loop(0, 2 * quarter, ours, 0, unroll=8)

    def finish(k):
        rank = ranks[k]
        if k >= 2:
            across_copy(k - 2, ranks[k - 2]).wait_send()
        mate_copy(k, rank).wait_recv()

        def send(j, carry):
            i = (1 - half) * quarter + j
            ysend[k % 2, j] = own[k % 2, i] + mrecv[rank, i]
            return carry

        lax.fori_loop(0, quarter, send, 0)
        across_copy(k, rank).start()

        def hold(j, carry):
            i = half * quarter + j
            keep[rank, j] = own[k % 2, i] + mrecv[rank, i]
            return carry

        lax.fori_loop(0, quarter, hold, 0)

    def process(rank):
        k = len(ranks)
        ranks.append(rank)
        links(k, rank)

    expand(c_ref, dom_ref)

    def turn(t, carry):
        turned[t] = wide[t].astype(F32).T.astype(BF16)
        return carry

    lax.fori_loop(0, pc, turn, 0, unroll=2)
    process(p)
    finish(0)
    for step in range(1, steps + 1):
        for c in (2, 0, 1):
            for d in (0, 1):
                if c in parts_of(step, d):
                    arrive(step, d, c)
                if step < steps and c in parts_of(step + 1, d):
                    move(step + 1, d, c).start()
        if step == steps - 1:
            yield None
        for d in (0, 1) if step < steps else (0,):
            rank = at(position + (-step if d == 0 else step), n)
            expand(cbuf.at[rank], dbuf.at[rank])
            process(rank)
            if d == 1:
                finish(len(ranks) - 2)
        finish(len(ranks) - 1)
    def settle(k):
        rank = ranks[k]
        across_copy(k, rank).wait_recv()

        def last(j, carry):
            out_ref[rank, j] = (keep[rank, j] + yrecv[rank, j]).astype(BF16)
            return carry

        lax.fori_loop(0, quarter, last, 0)

    yield settle
    for k in (n - 2, n - 1):
        mate_copy(k, ranks[k]).wait_send()
        across_copy(k, ranks[k]).wait_send()
    for step in range(1, steps + 1):
        for d in (0, 1):
            for c in parts_of(step, d):
                move(step, d, c).wait_send()


def iteration(
    n, first, joined, alone, slot_ref, fock_ref, start_ref, x_ref, k_ref, e_ref, out_ref,
    abuf, stage, acc, mine, rs, rr, ms, mr, ys, yr, fs, fr,
):
    p, g, position, mate, across = places(n)
    pc = k_ref.shape[0]
    width = k_ref.shape[1]
    quarter = pc // 4
    eighth = quarter // 2
    steps = n // 2
    right, left = at(position + 1, n), at(position - 1, n)
    diagonal = 3 - g
    if alone:
        greet([(right, g), (left, g), (p, mate), (p, across)])
    parts = 4 if joined else 3
    parts_of = ring_parts(steps, parts)

    def chunk(rank, group, c):
        return abuf.at[pl.ds(rank * pc + group * quarter + (c % 2) * eighth, eighth)]

    def span(rank, c):
        return chunk(rank, g if c < 2 else across, c)

    def ring_copy(step, direction, c):
        offset = -(step - 1) if direction == 0 else step - 1
        ref = span(at(position + offset, n), c)
        src = ref
        if step == 1 and c < 2 and not first:
            src = start_ref.at[pl.ds(c * eighth, eighth)]
        return remote(
            src, ref, rs.at[direction, step - 1, c], rr.at[direction, step - 1, c],
            (right if direction == 0 else left, g),
        )

    def arrive(step, direction, c):
        offset = -step if direction == 0 else step
        ref = span(at(position + offset, n), c)
        remote(
            ref, ref, rs.at[direction, step - 1, c], rr.at[direction, step - 1, c],
            (left if direction == 0 else right, g),
        ).wait_recv()

    def mate_copy(k, rank, c, src=None):
        ref = span(rank, c)
        return remote(ref if src is None else src, ref, ms.at[k, c], mr.at[k, c], (p, mate))

    def mate_wait(k, rank):
        for c in range(4):
            ref = chunk(rank, mate if c < 2 else diagonal, c)
            remote(ref, ref, ms.at[k, c], mr.at[k, c], (p, mate)).wait_recv()

    def across_copy(k, rank, c=1, src=None):
        ref = span(rank, c)
        sem = k if c == 1 else n
        return remote(ref if src is None else src, ref, ys.at[sem], yr.at[sem], (p, across))

    def across_wait(k, rank, c=3):
        ref = span(rank, c)
        sem = k if c == 3 else n
        remote(ref, ref, ys.at[sem], yr.at[sem], (p, across)).wait_recv()

    def own_half(c):
        return start_ref.at[pl.ds(c * eighth, eighth)]

    if first:
        def copy_own(i, carry):
            abuf[p * pc + i] = start_ref[i].astype(BF16)
            return carry

        def group_in(group):
            lax.fori_loop(group * quarter, (group + 1) * quarter, copy_own, 0)

        group_in(g)
        for c in (0, 1):
            for d in (0, 1):
                if c in parts_of(1, d):
                    ring_copy(1, d, c).start()
        group_in(across)
        for c in range(2, parts):
            for d in (0, 1):
                if c in parts_of(1, d):
                    ring_copy(1, d, c).start()
        group_in(mate)
        group_in(diagonal)
    else:
        for c in (0, 1):
            across_copy(0, p, c, own_half(c)).start()
            for d in (0, 1):
                if c in parts_of(1, d):
                    ring_copy(1, d, c).start()
        for c in (0, 1):
            mate_copy(0, p, c, own_half(c)).start()

        def copy_own(i, carry):
            abuf[p * pc + g * quarter + i] = start_ref[i]
            return carry

        lax.fori_loop(0, quarter, copy_own, 0)
        across_wait(0, p, 2)
        for d in (0, 1):
            if 2 in parts_of(1, d):
                ring_copy(1, d, 2).start()
        mate_copy(0, p, 2).start()
        across_wait(0, p, 3)
        mate_copy(0, p, 3).start()
        mate_wait(0, p)

    settle = yield None
    acc[...] = jnp.zeros_like(acc)

    def couple(rank, k):
        if settle is not None:
            settle(k)

        def copy(i, carry):
            stage[i] = abuf[rank * pc + i]
            return carry

        lax.fori_loop(0, pc, copy, 0, unroll=4)

        def one(j, carry):
            t = g * quarter + j
            source = stage[slot_ref[t, rank]]
            x = x_ref[rank, j]
            h = jnp.dot(x, source, preferred_element_type=F32).astype(BF16)
            y = lax.dot_general(h, x, (((1,), (1,)), ((), ())), preferred_element_type=F32)
            acc[j] += fock_ref[t, rank] * y
            return carry

        lax.fori_loop(0, quarter, one, 0, unroll=4)

    couple(p, 0)

    def exchange(blocks):
        for k, rank in () if joined else blocks:
            across_wait(k, rank)
            mate_copy(k, rank, 3).start()

    def use(blocks):
        for k, rank in blocks:
            mate_wait(k, rank)
            couple(rank, k)

    landed, shared = [], []
    for step in range(1, steps + 1):
        for c in (1, 0, 2, 3)[:parts]:
            for d in (0, 1):
                rank = at(position + (-step if d == 0 else step), n)
                if c in parts_of(step, d):
                    arrive(step, d, c)
                    if step < steps and c in parts_of(step + 1, d):
                        ring_copy(step + 1, d, c).start()
                    k = 2 * step - 1 + (d if step < steps else 0)
                    if c == 1 and not joined:
                        across_copy(k, rank).start()
                    mate_copy(k, rank, c).start()
        exchange(landed)
        use(shared)
        shared = landed
        landed = [
            (2 * step - 1 + d, at(position + (-step if d == 0 else step), n))
            for d in ((0, 1) if step < steps else (0,))
        ]
    exchange(landed)
    use(shared)
    use(landed)

    def scaled(j):
        t = g * quarter + j
        row = jnp.broadcast_to(e_ref[pl.ds(t, 1), :], (width, width))
        return (-(k_ref[t] + acc[j]) / (row.T + row + fock_ref[t, n])).astype(BF16)

    if first:
        def result(j, carry):
            out_ref[j] = scaled(j)
            return carry

        lax.fori_loop(0, quarter, result, 0, unroll=2)
    else:
        def block(ref, group):
            return ref.at[pl.ds(group * quarter, quarter)]

        def result(j, carry):
            value = scaled(j)
            mine[j] = value
            out_ref[g * quarter + j] = value
            return carry

        lax.fori_loop(0, quarter, result, 0, unroll=2)
        over = remote(mine, block(out_ref, g), fs.at[0], fr.at[0], (p, across))
        beside = remote(mine, block(out_ref, g), fs.at[1], fr.at[1], (p, mate))
        corner = remote(
            block(out_ref, across), block(out_ref, across), fs.at[2], fr.at[2], (p, mate)
        )
        over.start()
        beside.start()
        remote(mine, block(out_ref, across), fs.at[0], fr.at[0], (p, across)).wait_recv()
        corner.start()
        remote(mine, block(out_ref, mate), fs.at[1], fr.at[1], (p, mate)).wait_recv()
        remote(mine, block(out_ref, diagonal), fs.at[2], fr.at[2], (p, mate)).wait_recv()
        over.wait_send()
        beside.wait_send()
        corner.wait_send()
        across_copy(0, p, 0, own_half(0)).wait_send()
        across_copy(0, p, 1, own_half(1)).wait_send()
        for c in range(4):
            mate_copy(0, p, c).wait_send()
    for k in range(1, n):
        if not joined:
            across_copy(k, p).wait_send()
        for c in range(4):
            mate_copy(k, p, c).wait_send()
    for step in range(1, steps + 1):
        for d in (0, 1):
            for c in parts_of(step, d):
                ring_copy(step, d, c).wait_send()


def intersections_alone(*args):
    steps = intersections(*args)
    next(steps)
    settle = next(steps)
    for k in range(args[0]):
        settle(k)
    next(steps, None)


def iteration_alone(n, first, *args):
    steps = iteration(n, first, False, True, *args)
    next(steps)
    try:
        steps.send(None)
    except StopIteration:
        pass


def opening(
    n, made, slot_ref, fock_ref, c_ref, dom_ref, start_ref, k_ref, e_ref, out_ref,
    x_ref, amp_ref, *scratch
):
    used = made + (len(scratch) - made) // 2
    blocks = intersections(n, slot_ref, c_ref, dom_ref, x_ref, *scratch[:made])
    next(blocks)
    amps = iteration(
        n, True, True, False, slot_ref, fock_ref, start_ref, x_ref, k_ref, e_ref, amp_ref,
        *scratch[made:used],
    )
    next(amps)
    settle = next(blocks)
    try:
        amps.send(settle)
    except StopIteration:
        pass
    amps = iteration(
        n, False, False, False, slot_ref, fock_ref, amp_ref, x_ref, k_ref, e_ref, out_ref,
        *scratch[used:],
    )
    next(amps)
    try:
        amps.send(None)
    except StopIteration:
        pass
    next(blocks, None)


class Wires:
    def __init__(self, send, recv, here):
        self.send, self.recv, self.here = send, recv, here
        self.sends, self.recvs = {}, {}

    def link(self, key, src, dst, peer, out):
        at_send = self.sends.setdefault(out, len(self.sends))
        at_recv = self.recvs.setdefault(key, len(self.recvs))
        return remote(src, dst, self.send.at[at_send], self.recv.at[at_recv], peer)

    def start_in(self, when, key, src, dst, peer, out):
        self.link(key, src, dst, peer, out).start()

    def start(self, key, src, dst, peer, out, when=None):
        def run():
            self.start_in(when, key, src, dst, peer, out)

        if when is None:
            run()
        else:
            pl.when(when)(run)

    def wait(self, key, dst, when=None):
        at_recv = self.recvs.setdefault(key, len(self.recvs))
        copy = remote(dst, dst, self.send.at[0], self.recv.at[at_recv], self.here)
        if when is None:
            copy.wait_recv()
        else:
            pl.when(when)(copy.wait_recv)

    def drain(self, out, whole, when=None):
        at_send = self.sends[out]
        copy = remote(whole, whole, self.send.at[at_send], self.recv.at[0], self.here)
        if when is None:
            copy.wait_send()
        else:
            pl.when(when)(copy.wait_send)


def note(*what):
    return None


def quadrants(
    n, owner_hbm, slot_hbm, fock_hbm, shift_hbm, c_hbm, dom_hbm, start_ref, k_ref, e_hbm, out_ref,
    owner_ref, slot_ref, fock_ref, shift_ref, c_ref, dom_ref, e_ref, src, dom, blocks, bdom, bslot, bfock, wide, turned, x, start, k_own, amps_a, amps_b, amps_c, amps_d,
    acc, yout, yx, ysum, yin, mine, theirs, inverse, send, recv, local,
):
    p, g = lax.axis_index("pairs"), lax.axis_index("grp")
    pc, rows, width = c_ref.shape
    quarter = pc // 4
    half_quarter = quarter // 2
    layers = n // 2
    layer, column = p // 2, p % 2
    inner = (layer % 2 + layer // 2) % 2
    mid, end = inner == 1, inner == 0
    partner = (layer + 1 - 2 * (layer % 2)) * 2 + column
    cross = (layers - 1 - layer) * 2 + column
    far = ((layer + layers // 2) % layers) * 2 + column
    beside = layer * 2 + 1 - column
    groups = (g, g + 1 - 2 * (g % 2), (g + 2) % 4, 3 - g)
    _, mate, across, diagonal = groups
    to_mate, to_across = (p, mate), (p, across)
    to_partner, to_cross, to_beside, to_far = (partner, g), (cross, g), (beside, g), (far, g)
    wires = Wires(send, recv, to_mate)
    amps = ((amps_a, amps_b), (amps_c, amps_d))
    wires.mid = mid

    barrier = pltpu.get_barrier_semaphore()

    def hello(peer):
        pl.semaphore_signal(barrier, inc=1, device_id=peer, device_id_type=MESH)

    for peer in (to_partner, to_beside, to_across, to_mate):
        hello(peer)
    pl.when(mid)(lambda: hello(to_cross))

    pairs = (
        (c_hbm, c_ref), (dom_hbm, dom_ref), (owner_hbm, owner_ref), (slot_hbm, slot_ref),
        (fock_hbm, fock_ref), (shift_hbm, shift_ref), (e_hbm, e_ref), (start_ref, start),
        (k_ref.at[pl.ds(g * quarter, quarter)], k_own),
    )
    loads = [pltpu.make_async_copy(*pair, local.at[i]) for i, pair in enumerate(pairs)]
    for load in loads:
        load.start()
    load_c, load_dom, load_owner, load_slot, load_fock, load_shift, load_e, load_start, load_k = loads
    load_c.wait()
    load_dom.wait()

    def four(group):
        return pl.ds(group * quarter, quarter)

    def two(group, h):
        return pl.ds(group * quarter + h * half_quarter, half_quarter)

    def both_quarters(ref):
        return ref.at[pl.ds(0, 2 * quarter)]

    def three_quarters(ref):
        return ref.at[pl.ds(0, 3 * quarter)]

    def source(b, rel):
        return c_ref if (b, rel) == (0, 0) else src.at[4 * b + rel]

    def turn(rel, b=0):
        for t in range(quarter):
            blocks[b, rel, t] = source(b, rel)[g * quarter + t].T

    for s in range(pc):
        dom[0, s] = dom_ref[pl.ds(s, 1), :]
    turn(0)

    def table(t, carry):
        at_pair = g * quarter + t
        ways = owner_ref.shape[0]
        named = [owner_ref[k, at_pair] for k in range(ways)]
        slots = [slot_ref[k, at_pair] for k in range(ways)]
        focks = [fock_ref[k, at_pair] for k in range(ways)]
        for owner in range(n):
            place, weight = 0, 0.0
            for k in range(ways):
                hit = named[k] == owner
                place = jnp.where(hit, slots[k], place)
                weight = jnp.where(hit, focks[k], weight)
            bslot[0, t, owner] = place
            bfock[0, t, owner] = weight
        return carry

    small = ("slot", "fock", "dom")
    kinds = {
        "slot": lambda b: bslot.at[b],
        "fock": lambda b: bfock.at[b],
        "dom": lambda b: bdom.at[b],
    }
    for rel in range(4):
        for h in (0, 1):
            kinds[rel, h] = functools.partial(
                lambda rel, h, b: blocks.at[b, rel, pl.ds(h * half_quarter, half_quarter)], rel, h
            )
        kinds[rel] = functools.partial(lambda rel, b: blocks.at[b, rel], rel)

    def tag(kind):
        return kind if kind in small else "targets"

    def landing(kind):
        return kind if kind in small or kind in ((3, 0), (3, 1)) else 0

    def ready(kind):
        ref = kinds[kind](0)
        onward, across_cut = kinds[kind](4), kinds[kind](2)
        if kind in ("slot", "fock"):
            wires.start(("second", kind), ref, kinds[kind](1), to_partner, kind)
        wires.start(("beside", 0 if tag(kind) == "targets" else kind), ref, onward, to_beside, tag(kind), end)
        wires.start(("cross", kind), ref, across_cut, to_cross, tag(kind), mid)

    def next_ready(kind):
        ref = kinds[kind](1)
        onward, across_cut = kinds[kind](5), kinds[kind](3)
        if kind in ("slot", "fock"):
            wires.wait(("second", kind), ref)
        wires.start(("beside2", landing(kind)), ref, onward, to_beside, tag(kind), end)
        wires.start(("further", kind), ref, across_cut, to_cross, tag(kind), mid)

    def got_first(kind):
        landed, passed = kinds[kind](2), kinds[kind](4)

        def relay():
            wires.wait(("cross", kind), landed)
            key = ("beside", 0 if tag(kind) == "targets" else kind)
            wires.start_in(mid, key, landed, passed, to_beside, tag(kind))

        pl.when(mid)(relay)

    def got_further(kind):
        landed, passed = kinds[kind](3), kinds[kind](5)

        def relay():
            wires.wait(("further", kind), landed)
            wires.start_in(mid, ("beside2", landing(kind)), landed, passed, to_beside, tag(kind))

        pl.when(mid)(relay)

    def got_beside():
        for kind in small:
            wires.wait(("beside", kind), kinds[kind](4))
        wires.wait(("beside", 0), blocks.at[4])

    def got_beside2():
        for kind in small:
            wires.wait(("beside2", kind), kinds[kind](5))
        wires.wait(("beside2", 0), blocks.at[5, pl.ds(0, 3)])

    first, second = 2 * inner, 1 + 2 * inner
    places_of = (first, 4, second, 5)

    lines = lax.broadcasted_iota(jnp.int16, (NB, rows), 0)
    lines2 = lax.broadcasted_iota(jnp.int16, (2 * NB, 2 * rows), 0)

    def one_hot(numbers, row):
        hit = numbers == row.astype(jnp.int16)
        return jnp.where(hit, jnp.ones(hit.shape, BF16), jnp.zeros(hit.shape, BF16))

    def expand(b, rel, parts=(0, 1, 2, 3)):
        base = groups[rel] * NB
        block = source(b, rel)

        def one(s, carry):
            hit = one_hot(lines, dom[4 * b + rel, s] - base)
            wide[b, s, pl.ds(rel * NB, NB)] = jnp.dot(
                hit, block[s], preferred_element_type=F32
            ).astype(BF16)
            return carry

        if len(parts) == 4:
            note("expand", b, rel)
            lax.fori_loop(0, pc, one, 0, unroll=4)
            return
        for i in parts:
            note("expand4", b, rel)
            for t in range(quarter):
                one(groups[i] * quarter + t, 0)

    every = tuple(range(quarter))
    early, later = every[:half_quarter], every[half_quarter:]

    def make_turned(b, hs=(0, 1), ts=every):
        note("make_turned", b, 0, len(hs) * len(ts) / 8)
        place = places_of[b]

        def one(t, carry):
            for h in hs:
                u, v = 2 * h, 2 * h + 1
                row = jnp.concatenate(
                    [
                        bdom[place, u * quarter + t] - groups[u] * NB,
                        bdom[place, v * quarter + t] - groups[v] * NB + NB,
                    ],
                    axis=1,
                )
                hit = one_hot(lines2, row)
                both = jnp.concatenate([blocks[place, u, t], blocks[place, v, t]], axis=1)
                turned[b, t, :, pl.ds(h * 2 * NB, 2 * NB)] = lax.dot_general(
                    both, hit, (((1,), (1,)), ((), ())), preferred_element_type=F32
                ).astype(BF16)
            return carry

        if ts == every:
            lax.fori_loop(0, quarter, one, 0, unroll=2)
        else:
            for t in ts:
                one(t, 0)

    owners = (p, partner)

    def make_x(b, s, ts=every):
        note("make_x", b, s, len(ts) / 4)
        place = places_of[b]

        def one(t, carry):
            at_source = bslot[place, t, owners[s]]
            x[b, t, s] = jnp.dot(
                turned[b, t], wide[s, at_source], preferred_element_type=F32
            ).astype(BF16)
            return carry

        for t in ts:
            one(t, 0)

    def couple(b, s, it, ts=every):
        note("couple", b, s, len(ts) / 4)
        place = places_of[b]
        found = []
        for t in ts:
            at_source = bslot[place, t, owners[s]]
            xs = x[b, t, s]
            half = jnp.dot(xs, amps[it][s][at_source], preferred_element_type=F32).astype(BF16)
            found.append((t, xs, half))
        for t, xs, half in found:
            y = lax.dot_general(half, xs, (((1,), (1,)), ((), ())), preferred_element_type=F32)
            y = bfock[place, t, owners[s]] * y
            if s == 0:
                acc[b, t] = y
            elif b % 2 == 0:
                acc[b, t] += y
            else:
                yout[it, b // 2, t] = (acc[b, t] + y).astype(BF16)

    def post(it, m, ts=every):
        for t in ts:
            wires.start(("y", it, m, t), yout.at[it, m, t], yx.at[it, m, t], to_beside, "y")

    def share(t):
        at_pair = g * quarter + t
        ref = amps[1][0].at[at_pair]
        wires.start(("own", 1, t), ref, ref, to_across, "amps")
        wires.start(("own", 2), ref, ref, to_mate, "amps")

    def share_partner(t, when):
        at_pair = g * quarter + t
        wires.start(("a", 1, 0, t), amps[1][0].at[at_pair], amps[1][1].at[at_pair], to_partner, "amps", when)

    def pass_partner(t):
        ref = amps[1][1].at[g * quarter + t]
        wires.wait(("a", 1, 0, t), ref)
        wires.start(("a", 1, 1, t), ref, ref, to_across, "amps")
        wires.start(("a", 1, 2), ref, ref, to_mate, "amps")

    def pass_own(t):
        ref = amps[1][0].at[across * quarter + t]
        wires.wait(("own", 1, t), ref)
        wires.start(("own", 2), ref, ref, to_mate, "amps")

    def pass_across(t):
        ref = amps[1][1].at[across * quarter + t]
        wires.wait(("a", 1, 1, t), ref)
        wires.start(("a", 1, 2), ref, ref, to_mate, "amps")

    def share_start(j):
        part = four((g, across)[j])
        wires.start(("start", j), amps[0][0].at[part], amps[0][1].at[part], to_partner, "amps")

    def pass_start(j):
        ref = amps[0][1].at[four((g, across)[j])]
        wires.wait(("start", j), ref)
        wires.start(("a", 0, 2), ref, ref, to_mate, "amps")

    def have_partner(it):
        wires.wait(("a", it, 2), both_quarters(amps[it][1]))

    def sum_second(it, ts=every):
        for t in ts:
            wires.wait(("y", it, 1, t), yx.at[it, 1, t])
            ysum[it, 1, t] = (acc[2, t] + yx[it, 1, t].astype(F32)).astype(BF16)
            job = (("yfar", it, t), ysum.at[it, 1, t], yin.at[it, 0, t])
            wires.start(*job, to_partner, "yfar", end)
            wires.start(*job, to_far, "yfar", mid)

    def sum_first(it, ts=every):
        for t in ts:
            wires.wait(("y", it, 0, t), yx.at[it, 0, t])
            total = acc[0, t] + yx[it, 0, t].astype(F32)
            acc[0, t] = total
            ysum[it, 0, t] = total.astype(BF16)
            wires.start(("ynear", it, t), ysum.at[it, 0, t], yin.at[it, 1, t], to_cross, "ynear", mid)

    def coupled(it, t):
        wires.wait(("ynear", it, t), yin.at[it, 1, t], mid)
        wires.wait(("yfar", it, t), yin.at[it, 0, t])
        near = yin[it, 1, t].astype(F32)
        return yin[it, 0, t].astype(F32) + jnp.where(mid, near, acc[0, t])

    def invert(t, carry):
        at_pair = g * quarter + t
        row = jnp.broadcast_to(e_ref[pl.ds(at_pair, 1), :], (width, width))
        over = 1.0 / (row.T + row + shift_ref[at_pair])
        inverse[t] = over
        k_own[t] = k_own[t] * over
        return carry

    def updated(it, t):
        return (-(k_own[t] + coupled(it, t) * inverse[t])).astype(BF16)

    swap_mate, swap_across = (1, 0, 3, 2), (2, 3, 0, 1)

    def from_mate():
        wires.wait(("own mate", 1), src.at[1, four(g)])

    def from_mate_rest():
        wires.wait(("own mate", 0), three_quarters(src.at[1]))

    def from_across(i):
        part = four(groups[i])
        wires.wait(("own across", swap_across[i]), src.at[2, part])
        wires.start(
            ("own corner", int(i == 1)), src.at[2, part], src.at[3, part], to_mate,
            "rows",
        )

    def from_corner():
        wires.wait(("own corner", 1), src.at[3, four(g)])

    def from_corner_rest():
        wires.wait(("own corner", 0), three_quarters(src.at[3]))

    def to_next(i):
        part = four(groups[i])
        wires.start(
            ("next", i), c_ref.at[part], src.at[4, part], to_partner, "rows"
        )

    def from_next(i):
        part = four(groups[i])
        ref = src.at[4, part]
        wires.wait(("next", i), ref)
        if i > 0:
            wires.start(
                ("next across", i), ref, src.at[6, part], to_across, "rows",
            )
        wires.start(
            ("next mate", int(i == 1)), ref, src.at[5, part], to_mate, "rows",
        )

    def to_wide(i):
        part = four(groups[i])
        wires.start(
            ("next wide", i), src.at[2, part], src.at[6, part], to_partner, "rows",
        )

    def corner(i):
        part = four(groups[i])
        wires.start(
            ("next corner", int(i == 1)), src.at[6, part], src.at[7, part], to_mate, "rows",
        )

    def from_next_across(i):
        wires.wait(("next across", swap_across[i]), src.at[6, four(groups[i])])
        corner(i)

    def from_wide(i):
        wires.wait(("next wide", i), src.at[6, four(groups[i])])
        corner(i)

    def from_next_mate():
        wires.wait(("next mate", 1), src.at[5, four(g)])

    def from_next_mate_rest():
        wires.wait(("next mate", 0), three_quarters(src.at[5]))

    def from_next_corner():
        wires.wait(("next corner", 1), src.at[7, four(g)])

    def from_next_corner_rest():
        wires.wait(("next corner", 0), three_quarters(src.at[7]))

    def own_across(i):
        part = four(groups[i])
        wires.start(
            ("own across", i), c_ref.at[part], src.at[2, part], to_across, "rows",
        )

    def cast(s, carry):
        amps[0][0][s] = start[s].astype(BF16)
        return carry

    pl.semaphore_wait(barrier, 4 + inner)
    wires.start(("d", 1), dom.at[0], dom.at[1], to_mate, "doms")
    wires.start(("d", 2), dom.at[0], dom.at[2], to_across, "doms")
    own_across(2)
    to_next(0)
    ready((0, 0))
    ready((0, 1))
    for i in (1, 0, 2, 3):
        part = four(groups[i])
        wires.start(
            ("own mate", int(i == 1)), c_ref.at[part], src.at[1, part], to_mate, "rows",
        )
    own_across(3)
    own_across(0)
    to_next(2)
    from_mate()
    turn(1)
    ready((1, 0))
    ready((1, 1))
    wires.wait(("d", 1), dom.at[1])
    wires.wait(("d", 2), dom.at[2])
    wires.start(("d", 3), dom.at[2], dom.at[3], to_mate, "doms")
    for load in (load_owner, load_slot, load_fock):
        load.wait()
    lax.fori_loop(0, quarter, table, 0)
    ready("slot")
    ready("fock")
    wires.wait(("d", 3), dom.at[3])
    wires.start(("d", 4), dom.at[pl.ds(0, 4)], dom.at[pl.ds(4, 4)], to_partner, "doms")
    to_next(3)
    to_next(1)
    for rel in range(4):
        for t in range(quarter):
            bdom[0, rel * quarter + t] = dom[rel, g * quarter + t]
    ready("dom")
    got_first((0, 0))
    expand(0, 0)
    from_next(0)
    turn(0, 1)
    next_ready((0, 0))
    next_ready((0, 1))
    got_first((0, 1))
    from_across(0)
    turn(2)
    ready((2, 0))
    ready((2, 1))
    from_mate_rest()
    got_first((1, 0))
    expand(0, 1)
    from_next(2)
    got_first((1, 1))
    expand(0, 2, (0,))
    from_across(1)
    got_further((0, 0))
    from_corner()
    turn(3)
    ready((3, 0))
    ready((3, 1))
    load_start.wait()
    lax.fori_loop(0, pc, cast, 0, unroll=2)
    for load in (load_k, load_e, load_shift):
        load.wait()
    wires.wait(("d", 4), dom.at[pl.ds(4, 4)])
    expand(0, 2, (1,))
    from_across(2)
    to_wide(2)
    share_start(0)
    share_start(1)
    got_further((0, 1))
    expand(1, 0, (0, 2))
    from_next(3)
    own_across(1)
    expand(0, 2, (2,))
    got_first((2, 0))
    expand(1, 0, (3,))
    for rel in range(4):
        for t in range(quarter):
            bdom[1, rel * quarter + t] = dom[4 + rel, g * quarter + t]
    next_ready("dom")
    next_ready("slot")
    next_ready("fock")
    from_next_across(0)
    turn(2, 1)
    next_ready((2, 0))
    next_ready((2, 1))
    got_first((2, 1))
    from_next(1)
    expand(1, 0, (1,))
    got_first((3, 0))
    from_next_mate()
    turn(1, 1)
    next_ready((1, 0))
    next_ready((1, 1))
    from_next_mate_rest()
    expand(1, 1, (0, 1))
    from_next_across(1)
    got_first((3, 1))
    expand(1, 1, (2, 3))
    from_next_corner()
    turn(3, 1)
    next_ready((3, 0))
    next_ready((3, 1))
    for kind in small:
        got_first(kind)
    from_wide(2)
    got_further((2, 0))
    lax.fori_loop(0, half_quarter, invert, 0)
    expand(1, 2, (0, 1))
    from_across(3)
    got_further((2, 1))
    expand(1, 2, (2,))
    expand(0, 2, (3,))
    from_corner_rest()
    expand(0, 3, (0, 1))
    got_further((1, 0))
    expand(0, 3, (2, 3))
    make_turned(0)
    pass_start(0)
    got_further((1, 1))
    lax.fori_loop(half_quarter, quarter, invert, 0)
    from_next_across(3)
    make_x(0, 0)
    expand(1, 2, (3,))
    pass_start(1)
    for kind in small:
        got_further(kind)
    from_next_corner_rest()
    expand(1, 3)
    got_further((3, 0))
    got_beside()
    make_turned(1)
    make_x(1, 0)
    make_x(1, 1)
    have_partner(0)
    got_further((3, 1))
    couple(1, 0, 0)
    couple(1, 1, 0)
    post(0, 0, early)
    make_turned(2)
    make_x(2, 0)
    make_x(2, 1)
    couple(2, 0, 0)
    couple(2, 1, 0)
    got_beside2()
    make_turned(3, (0,))
    for h, ts in ((0, early), (1, later)):
        wires.wait(("beside2", (3, h)), kinds[3, h](5))
        make_turned(3, (1,), ts)
        make_x(3, 0, ts)
        make_x(3, 1, ts)
        couple(3, 0, 0, ts)
        couple(3, 1, 0, ts)
        post(0, 1, ts)
    post(0, 0, later)
    make_x(0, 1)
    couple(0, 0, 0)
    couple(0, 1, 0)
    sum_first(0, early)
    sum_second(0)
    sum_first(0, later)

    for t in range(quarter):
        amps[1][0][g * quarter + t] = updated(0, t)
        share_partner(t, None)
        share(t)
    for t in range(quarter):
        pass_partner(t)
        pass_own(t)
    wires.wait(("own", 2), both_quarters(amps[1][0]))
    couple(3, 0, 1)
    couple(1, 0, 1)
    for t in range(half_quarter):
        pass_across(t)
    couple(2, 0, 1)
    couple(0, 0, 1)
    for t in range(half_quarter, quarter):
        pass_across(t)
    have_partner(1)
    for ts in (early, later):
        for b in (3, 1):
            couple(b, 1, 1, ts)
            post(1, b // 2, ts)
    couple(2, 1, 1)
    couple(0, 1, 1)
    sum_second(1, early)
    sum_first(1, early)
    sum_second(1, later)
    sum_first(1, later)

    for t in range(quarter):
        mine[t] = coupled(1, t).astype(BF16)
        part = mine.at[t]
        wires.start(("out", 1, t), part, theirs.at[t], to_across, "amps")
        wires.start(("out", 2), part, out_ref.at[g * quarter + t], to_mate, "out")
    keep_mine = pltpu.make_async_copy(mine, out_ref.at[four(g)], local.at[9])
    keep_mine.start()
    for t in range(quarter):
        ref = theirs.at[t]
        wires.wait(("out", 1, t), ref)
        wires.start(("out", 2), ref, out_ref.at[across * quarter + t], to_mate, "out")
    keep_theirs = pltpu.make_async_copy(theirs, out_ref.at[four(across)], local.at[10])
    keep_theirs.start()
    wires.drain("rows", src.at[pl.ds(0, 7)])
    wires.drain("doms", dom.at[pl.ds(0, 7)])
    for role, passes in ((end, 2), (mid, 4)):
        wires.drain("targets", blocks.at[pl.ds(0, passes)], role)
        wires.drain("dom", bdom.at[pl.ds(0, passes)], role)
        wires.drain("slot", bslot.at[pl.ds(0, passes + 1)], role)
        wires.drain("fock", bfock.at[pl.ds(0, passes + 1)], role)
    wires.drain("y", yout)
    wires.drain("yfar", ysum.at[0])
    wires.drain("ynear", ysum.at[0], mid)
    wires.drain("amps", src.at[pl.ds(0, 3)])
    wires.drain("out", both_quarters(amps[1][0]))
    wires.wait(("out", 2), both_quarters(out_ref))
    keep_mine.wait()
    keep_theirs.wait()
    assert len(wires.sends) <= SENDS and len(wires.recvs) <= RECVS, (len(wires.sends), len(wires.recvs))


SENDS, RECVS = 11, 112


def quadrants_fit(n, groups, pc, rows, width):
    return n == 2 * groups and groups == 4 and pc % (2 * groups) == 0 and rows == width


def quadrants_kernel(n, *refs):
    quadrants(n, *refs)


def quadrants_call(
    n, owner, slot, fock, shift, coefficients, domain, start, integrals, energy
):
    pc, rows, width = coefficients.shape
    quarter = pc // 4
    big, ways = (width, width), owner.shape[1]
    hbm = pl.BlockSpec(memory_space=pl.ANY)
    dma = pltpu.SemaphoreType.DMA
    total = pl.pallas_call(
        functools.partial(quadrants_kernel, n),
        out_shape=jax.ShapeDtypeStruct((pc, *big), BF16),
        in_specs=[hbm] * 9,
        out_specs=hbm,
        scratch_shapes=[
            pltpu.SMEM((ways, pc), jnp.int32), pltpu.SMEM((ways, pc), jnp.int32),
            pltpu.SMEM((ways, pc), F32), pltpu.SMEM((pc,), F32),
            pltpu.VMEM((pc, rows, width), BF16), pltpu.VMEM((pc, rows), jnp.int32),
            pltpu.VMEM((pc, width), F32),
            pltpu.VMEM((8, pc, rows, width), BF16),
            pltpu.VMEM((8, pc, 1, rows), jnp.int32),
            pltpu.VMEM((6, 4, quarter, width, rows), BF16),
            pltpu.VMEM((6, 4 * quarter, 1, rows), jnp.int32),
            pltpu.SMEM((6, quarter, n), jnp.int32),
            pltpu.SMEM((6, quarter, n), F32),
            pltpu.VMEM((2, pc, 4 * NB, width), BF16),
            pltpu.VMEM((4, quarter, width, 4 * NB), BF16),
            pltpu.VMEM((4, quarter, 2, *big), BF16),
            pltpu.VMEM((pc, *big), F32),
            pltpu.VMEM((quarter, *big), F32),
            *[pltpu.VMEM((pc, *big), BF16)] * 4,
            pltpu.VMEM((4, quarter, *big), F32),
            pltpu.VMEM((2, 2, quarter, *big), BF16),
            pltpu.VMEM((2, 2, quarter, *big), BF16),
            pltpu.VMEM((2, 2, quarter, *big), BF16),
            pltpu.VMEM((2, 2, quarter, *big), BF16),
            pltpu.VMEM((quarter, *big), BF16), pltpu.VMEM((quarter, *big), BF16),
            pltpu.VMEM((quarter, *big), F32),
            dma((SENDS,)), dma((RECVS,)), dma((11,)),
        ],
        compiler_params=pltpu.CompilerParams(
            collective_id=0, has_side_effects=True, vmem_limit_bytes=60 * 2**20
        ),
        name="quadrants",
    )(owner.T, slot.T, fock.T, shift, coefficients, domain, start, integrals, energy)
    denominator = energy[:, :, None] + energy[:, None, :] + shift[:, None, None]
    return -(integrals + total.astype(F32)) / denominator


def on_device(
    coefficients, domain, coupling_owner, coupling_slot, coupling_fock,
    exchange_integrals, pno_energy, pair_shift, amplitudes_start,
):
    n = lax.axis_size("pairs")
    pc, rows, width = coefficients.shape
    quarter = pc // lax.axis_size("grp")
    steps = n // 2
    named = coupling_owner[:, :, None] == jnp.arange(n, dtype=jnp.int32)[None, None, :]
    slots = jnp.sum(jnp.where(named, coupling_slot[:, :, None], 0), axis=1)
    focks = jnp.sum(jnp.where(named, coupling_fock[:, :, None], 0.0), axis=1)
    focks = jnp.concatenate([focks, pair_shift[:, None]], axis=1)
    vmem, smem = pl.BlockSpec(memory_space=pltpu.VMEM), pl.BlockSpec(memory_space=pltpu.SMEM)
    dma = pltpu.SemaphoreType.DMA

    def params(collective):
        return pltpu.CompilerParams(
            collective_id=collective, has_side_effects=True, vmem_limit_bytes=60 * 2**20
        )

    if quadrants_fit(n, lax.axis_size("grp"), pc, rows, width):
        return quadrants_call(
            n, coupling_owner, coupling_slot, coupling_fock, pair_shift, coefficients, domain,
            amplitudes_start, exchange_integrals, pno_energy,
        )

    big = (width, width)
    x_shape = jax.ShapeDtypeStruct((n, quarter, *big), BF16)
    block_scratch = [
        pltpu.VMEM((n, pc, rows, width), BF16),
        pltpu.VMEM((n, pc, rows), jnp.int32),
        pltpu.VMEM((pc, width, NB), BF16),
        pltpu.VMEM((pc, NB, width), BF16),
        pltpu.VMEM((2, 2 * quarter, *big), F32),
        pltpu.VMEM((2, 2 * quarter, *big), F32),
        pltpu.VMEM((n, 2 * quarter, *big), F32),
        pltpu.VMEM((2, quarter, *big), F32),
        pltpu.VMEM((n, quarter, *big), F32),
        pltpu.VMEM((n, quarter, *big), F32),
        dma((2, steps, 3)), dma((2, steps, 3)),
        dma((n,)), dma((n,)), dma((n,)), dma((n,)),
    ]
    amp_scratch = [
        pltpu.VMEM((n * pc, *big), BF16),
        pltpu.VMEM((pc, *big), BF16),
        pltpu.VMEM((quarter, *big), F32),
        pltpu.VMEM((quarter, *big), BF16),
        dma((2, steps, 4)), dma((2, steps, 4)),
        dma((n, 4)), dma((n, 4)), dma((n + 1,)), dma((n + 1,)), dma((3,)), dma((3,)),
    ]
    half_shape = jax.ShapeDtypeStruct((quarter, *big), BF16)

    def iterate(first, start, x):
        return pl.pallas_call(
            functools.partial(iteration_alone, n, first),
            out_shape=half_shape if first else jax.ShapeDtypeStruct((pc, *big), BF16),
            in_specs=[smem, smem, vmem, vmem, vmem, vmem],
            out_specs=vmem,
            scratch_shapes=amp_scratch,
            compiler_params=params(1 if first else 2),
            name="first" if first else "second",
        )(slots, focks, start, x, exchange_integrals, pno_energy)

    held = n * width * (2 * pc * (rows + width) + 4 * width * 4 * quarter + 2 * width * quarter)
    if held < 40 * 2**20:
        return pl.pallas_call(
            functools.partial(opening, n, len(block_scratch)),
            out_shape=jax.ShapeDtypeStruct((pc, *big), BF16),
            in_specs=[smem, smem, vmem, vmem, vmem, vmem, vmem],
            out_specs=vmem,
            scratch_shapes=[
                pltpu.VMEM(x_shape.shape, BF16), pltpu.VMEM(half_shape.shape, BF16),
                *block_scratch, *amp_scratch, *amp_scratch,
            ],
            compiler_params=params(0),
            name="amplitudes",
        )(slots, focks, coefficients, domain, amplitudes_start, exchange_integrals, pno_energy).astype(F32)
    else:
        x = pl.pallas_call(
            functools.partial(intersections_alone, n),
            out_shape=x_shape,
            in_specs=[smem, vmem, vmem],
            out_specs=vmem,
            scratch_shapes=block_scratch,
            compiler_params=params(0),
            name="intersections",
        )(slots, coefficients, domain)
        amps = iterate(True, amplitudes_start, x)
    return iterate(False, amps, x).astype(F32)


def solution(mesh):
    placed = (
        P("pairs", "grp", None),
        P("pairs", "grp"),
        P("pairs", None),
        P("pairs", None),
        P("pairs", None),
        P("pairs", None, None),
        P("pairs", None),
        P("pairs"),
        P("pairs", None, None),
    )
    return jax.shard_map(
        on_device, mesh=mesh, in_specs=placed, out_specs=P("pairs", None, None), check_vma=False
    )
```

```python
import functools

import jax
import jax.numpy as jnp
from jax import lax
from jax.experimental import pallas as pl
from jax.experimental.pallas import tpu as pltpu
from jax.sharding import PartitionSpec as P

NB = 192
MESH = pl.DeviceIdType.MESH
F32, BF16 = jnp.float32, jnp.bfloat16


def ring_position(rank, n):
    odd = rank % 2
    return (1 - odd) * (rank // 2) + odd * (n - 1 - rank // 2)


def ring_rank(position, n):
    back = position // (n // 2)
    return (1 - back) * 2 * position + back * (2 * (n - 1 - position) + 1)


def places(n):
    p, g = lax.axis_index("pairs"), lax.axis_index("grp")
    position = ring_position(p, n)
    core, half = g % 2, g // 2
    mate = 2 * half + (1 - core)
    across = 2 * (1 - half) + core
    return p, g, position, mate, across


def at(position, n):
    return ring_rank((position + n) % n, n)


def greet(peers):
    barrier = pltpu.get_barrier_semaphore()
    for peer in peers:
        pl.semaphore_signal(barrier, inc=1, device_id=peer, device_id_type=MESH)
    pl.semaphore_wait(barrier, len(peers))


def remote(src, dst, send, recv, peer):
    return pltpu.make_async_remote_copy(
        src_ref=src, dst_ref=dst, send_sem=send, recv_sem=recv, device_id=peer, device_id_type=MESH
    )


def ring_parts(steps, parts):
    def of(step, direction):
        if step < steps:
            return tuple(range(parts))
        return tuple(c for c in range(parts) if c % 2 == direction)

    return of


def intersections(
    n, slot_ref, c_ref, dom_ref, out_ref,
    cbuf, dbuf, turned, wide, own, msend, mrecv, ysend, yrecv, keep,
    rs, rr, ms, mr, ys, yr,
):
    p, g, position, mate, across = places(n)
    pc = c_ref.shape[0]
    quarter = pc // 4
    rows = c_ref.shape[1]
    steps = n // 2
    right, left = at(position + 1, n), at(position - 1, n)
    ring_peer = (lambda r: (r, g))
    peers = [(right, g), (left, g), (p, mate), (p, across)]
    greet(peers)
    parts_of = ring_parts(steps, 3)
    hp = pc // 2

    def part(ref_c, ref_d, c):
        if c == 2:
            return ref_d
        return ref_c.at[pl.ds(c * hp, hp)]

    def move(step, direction, c):
        offset = -(step - 1) if direction == 0 else step - 1
        rank = at(position + offset, n)
        if step == 1:
            src = part(c_ref, dom_ref, c)
        else:
            src = part(cbuf.at[rank], dbuf.at[rank], c)
        dst = part(cbuf.at[rank], dbuf.at[rank], c)
        return remote(
            src, dst, rs.at[direction, step - 1, c], rr.at[direction, step - 1, c],
            ring_peer(right if direction == 0 else left),
        )

    def arrive(step, direction, c):
        offset = -step if direction == 0 else step
        rank = at(position + offset, n)
        dst = part(cbuf.at[rank], dbuf.at[rank], c)
        remote(
            dst, dst, rs.at[direction, step - 1, c], rr.at[direction, step - 1, c],
            ring_peer(left if direction == 0 else right),
        ).wait_recv()

    for c in (2, 0, 1):
        for d in (0, 1):
            if c in parts_of(1, d):
                move(1, d, c).start()

    base = g * NB
    lines = lax.broadcasted_iota(jnp.int32, (NB, rows), 0)
    core, half = g % 2, g // 2

    def expand(block, doms):
        def one(s, carry):
            hit = (lines == (doms[pl.ds(s, 1), :] - base)).astype(F32).astype(BF16)
            wide[s] = jnp.dot(hit, block[s], preferred_element_type=F32).astype(BF16)
            return carry

        lax.fori_loop(0, pc, one, 0, unroll=8)

    def mate_copy(k, rank):
        return remote(msend.at[k % 2], mrecv.at[rank], ms.at[k], mr.at[k], (p, mate))

    def across_copy(k, rank):
        return remote(ysend.at[k % 2], yrecv.at[rank], ys.at[k], yr.at[k], (p, across))

    ranks = []

    def product(t, rank):
        return jnp.dot(turned[t], wide[slot_ref[t, rank]], preferred_element_type=F32)

    def links(k, rank):
        if k >= 2:
            mate_copy(k - 2, ranks[k - 2]).wait_send()

        def theirs(i, carry):
            t = (2 * (i // quarter) + 1 - core) * quarter + i % quarter
            msend[k % 2, i] = product(t, rank)
            return carry

        lax.fori_loop(0, 2 * quarter, theirs, 0, unroll=8)
        mate_copy(k, rank).start()

        def ours(i, carry):
            t = (2 * (i // quarter) + core) * quarter + i % quarter
            own[k % 2, i] = product(t, rank)
            return carry

        lax.fori_loop(0, 2 * quarter, ours, 0, unroll=8)

    def finish(k):
        rank = ranks[k]
        if k >= 2:
            across_copy(k - 2, ranks[k - 2]).wait_send()
        mate_copy(k, rank).wait_recv()

        def send(j, carry):
            i = (1 - half) * quarter + j
            ysend[k % 2, j] = own[k % 2, i] + mrecv[rank, i]
            return carry

        lax.fori_loop(0, quarter, send, 0)
        across_copy(k, rank).start()

        def hold(j, carry):
            i = half * quarter + j
            keep[rank, j] = own[k % 2, i] + mrecv[rank, i]
            return carry

        lax.fori_loop(0, quarter, hold, 0)

    def process(rank):
        k = len(ranks)
        ranks.append(rank)
        links(k, rank)

    expand(c_ref, dom_ref)

    def turn(t, carry):
        turned[t] = wide[t].astype(F32).T.astype(BF16)
        return carry

    lax.fori_loop(0, pc, turn, 0, unroll=2)
    process(p)
    finish(0)
    for step in range(1, steps + 1):
        for c in (2, 0, 1):
            for d in (0, 1):
                if c in parts_of(step, d):
                    arrive(step, d, c)
                if step < steps and c in parts_of(step + 1, d):
                    move(step + 1, d, c).start()
        if step == steps - 1:
            yield None
        for d in (0, 1) if step < steps else (0,):
            rank = at(position + (-step if d == 0 else step), n)
            expand(cbuf.at[rank], dbuf.at[rank])
            process(rank)
            if d == 1:
                finish(len(ranks) - 2)
        finish(len(ranks) - 1)
    def settle(k):
        rank = ranks[k]
        across_copy(k, rank).wait_recv()

        def last(j, carry):
            out_ref[rank, j] = (keep[rank, j] + yrecv[rank, j]).astype(BF16)
            return carry

        lax.fori_loop(0, quarter, last, 0)

    yield settle
    for k in (n - 2, n - 1):
        mate_copy(k, ranks[k]).wait_send()
        across_copy(k, ranks[k]).wait_send()
    for step in range(1, steps + 1):
        for d in (0, 1):
            for c in parts_of(step, d):
                move(step, d, c).wait_send()


def iteration(
    n, first, joined, alone, slot_ref, fock_ref, start_ref, x_ref, k_ref, e_ref, out_ref,
    abuf, stage, acc, mine, rs, rr, ms, mr, ys, yr, fs, fr,
):
    p, g, position, mate, across = places(n)
    pc = k_ref.shape[0]
    width = k_ref.shape[1]
    quarter = pc // 4
    eighth = quarter // 2
    steps = n // 2
    right, left = at(position + 1, n), at(position - 1, n)
    diagonal = 3 - g
    if alone:
        greet([(right, g), (left, g), (p, mate), (p, across)])
    parts = 4 if joined else 3
    parts_of = ring_parts(steps, parts)

    def chunk(rank, group, c):
        return abuf.at[pl.ds(rank * pc + group * quarter + (c % 2) * eighth, eighth)]

    def span(rank, c):
        return chunk(rank, g if c < 2 else across, c)

    def ring_copy(step, direction, c):
        offset = -(step - 1) if direction == 0 else step - 1
        ref = span(at(position + offset, n), c)
        src = ref
        if step == 1 and c < 2 and not first:
            src = start_ref.at[pl.ds(c * eighth, eighth)]
        return remote(
            src, ref, rs.at[direction, step - 1, c], rr.at[direction, step - 1, c],
            (right if direction == 0 else left, g),
        )

    def arrive(step, direction, c):
        offset = -step if direction == 0 else step
        ref = span(at(position + offset, n), c)
        remote(
            ref, ref, rs.at[direction, step - 1, c], rr.at[direction, step - 1, c],
            (left if direction == 0 else right, g),
        ).wait_recv()

    def mate_copy(k, rank, c, src=None):
        ref = span(rank, c)
        return remote(ref if src is None else src, ref, ms.at[k, c], mr.at[k, c], (p, mate))

    def mate_wait(k, rank):
        for c in range(4):
            ref = chunk(rank, mate if c < 2 else diagonal, c)
            remote(ref, ref, ms.at[k, c], mr.at[k, c], (p, mate)).wait_recv()

    def across_copy(k, rank, c=1, src=None):
        ref = span(rank, c)
        sem = k if c == 1 else n
        return remote(ref if src is None else src, ref, ys.at[sem], yr.at[sem], (p, across))

    def across_wait(k, rank, c=3):
        ref = span(rank, c)
        sem = k if c == 3 else n
        remote(ref, ref, ys.at[sem], yr.at[sem], (p, across)).wait_recv()

    def own_half(c):
        return start_ref.at[pl.ds(c * eighth, eighth)]

    if first:
        def copy_own(i, carry):
            abuf[p * pc + i] = start_ref[i].astype(BF16)
            return carry

        def group_in(group):
            lax.fori_loop(group * quarter, (group + 1) * quarter, copy_own, 0)

        group_in(g)
        for c in (0, 1):
            for d in (0, 1):
                if c in parts_of(1, d):
                    ring_copy(1, d, c).start()
        group_in(across)
        for c in range(2, parts):
            for d in (0, 1):
                if c in parts_of(1, d):
                    ring_copy(1, d, c).start()
        group_in(mate)
        group_in(diagonal)
    else:
        for c in (0, 1):
            across_copy(0, p, c, own_half(c)).start()
            for d in (0, 1):
                if c in parts_of(1, d):
                    ring_copy(1, d, c).start()
        for c in (0, 1):
            mate_copy(0, p, c, own_half(c)).start()

        def copy_own(i, carry):
            abuf[p * pc + g * quarter + i] = start_ref[i]
            return carry

        lax.fori_loop(0, quarter, copy_own, 0)
        across_wait(0, p, 2)
        for d in (0, 1):
            if 2 in parts_of(1, d):
                ring_copy(1, d, 2).start()
        mate_copy(0, p, 2).start()
        across_wait(0, p, 3)
        mate_copy(0, p, 3).start()
        mate_wait(0, p)

    settle = yield None
    acc[...] = jnp.zeros_like(acc)

    def couple(rank, k):
        if settle is not None:
            settle(k)

        def copy(i, carry):
            stage[i] = abuf[rank * pc + i]
            return carry

        lax.fori_loop(0, pc, copy, 0, unroll=4)

        def one(j, carry):
            t = g * quarter + j
            source = stage[slot_ref[t, rank]]
            x = x_ref[rank, j]
            h = jnp.dot(x, source, preferred_element_type=F32).astype(BF16)
            y = lax.dot_general(h, x, (((1,), (1,)), ((), ())), preferred_element_type=F32)
            acc[j] += fock_ref[t, rank] * y
            return carry

        lax.fori_loop(0, quarter, one, 0, unroll=4)

    couple(p, 0)

    def exchange(blocks):
        for k, rank in () if joined else blocks:
            across_wait(k, rank)
            mate_copy(k, rank, 3).start()

    def use(blocks):
        for k, rank in blocks:
            mate_wait(k, rank)
            couple(rank, k)

    landed, shared = [], []
    for step in range(1, steps + 1):
        for c in (1, 0, 2, 3)[:parts]:
            for d in (0, 1):
                rank = at(position + (-step if d == 0 else step), n)
                if c in parts_of(step, d):
                    arrive(step, d, c)
                    if step < steps and c in parts_of(step + 1, d):
                        ring_copy(step + 1, d, c).start()
                    k = 2 * step - 1 + (d if step < steps else 0)
                    if c == 1 and not joined:
                        across_copy(k, rank).start()
                    mate_copy(k, rank, c).start()
        exchange(landed)
        use(shared)
        shared = landed
        landed = [
            (2 * step - 1 + d, at(position + (-step if d == 0 else step), n))
            for d in ((0, 1) if step < steps else (0,))
        ]
    exchange(landed)
    use(shared)
    use(landed)

    def scaled(j):
        t = g * quarter + j
        row = jnp.broadcast_to(e_ref[pl.ds(t, 1), :], (width, width))
        return (-(k_ref[t] + acc[j]) / (row.T + row + fock_ref[t, n])).astype(BF16)

    if first:
        def result(j, carry):
            out_ref[j] = scaled(j)
            return carry

        lax.fori_loop(0, quarter, result, 0, unroll=2)
    else:
        def block(ref, group):
            return ref.at[pl.ds(group * quarter, quarter)]

        def result(j, carry):
            value = scaled(j)
            mine[j] = value
            out_ref[g * quarter + j] = value
            return carry

        lax.fori_loop(0, quarter, result, 0, unroll=2)
        over = remote(mine, block(out_ref, g), fs.at[0], fr.at[0], (p, across))
        beside = remote(mine, block(out_ref, g), fs.at[1], fr.at[1], (p, mate))
        corner = remote(
            block(out_ref, across), block(out_ref, across), fs.at[2], fr.at[2], (p, mate)
        )
        over.start()
        beside.start()
        remote(mine, block(out_ref, across), fs.at[0], fr.at[0], (p, across)).wait_recv()
        corner.start()
        remote(mine, block(out_ref, mate), fs.at[1], fr.at[1], (p, mate)).wait_recv()
        remote(mine, block(out_ref, diagonal), fs.at[2], fr.at[2], (p, mate)).wait_recv()
        over.wait_send()
        beside.wait_send()
        corner.wait_send()
        across_copy(0, p, 0, own_half(0)).wait_send()
        across_copy(0, p, 1, own_half(1)).wait_send()
        for c in range(4):
            mate_copy(0, p, c).wait_send()
    for k in range(1, n):
        if not joined:
            across_copy(k, p).wait_send()
        for c in range(4):
            mate_copy(k, p, c).wait_send()
    for step in range(1, steps + 1):
        for d in (0, 1):
            for c in parts_of(step, d):
                ring_copy(step, d, c).wait_send()


def intersections_alone(*args):
    steps = intersections(*args)
    next(steps)
    settle = next(steps)
    for k in range(args[0]):
        settle(k)
    next(steps, None)


def iteration_alone(n, first, *args):
    steps = iteration(n, first, False, True, *args)
    next(steps)
    try:
        steps.send(None)
    except StopIteration:
        pass


def opening(
    n, made, slot_ref, fock_ref, c_ref, dom_ref, start_ref, k_ref, e_ref, out_ref,
    x_ref, amp_ref, *scratch
):
    used = made + (len(scratch) - made) // 2
    blocks = intersections(n, slot_ref, c_ref, dom_ref, x_ref, *scratch[:made])
    next(blocks)
    amps = iteration(
        n, True, True, False, slot_ref, fock_ref, start_ref, x_ref, k_ref, e_ref, amp_ref,
        *scratch[made:used],
    )
    next(amps)
    settle = next(blocks)
    try:
        amps.send(settle)
    except StopIteration:
        pass
    amps = iteration(
        n, False, False, False, slot_ref, fock_ref, amp_ref, x_ref, k_ref, e_ref, out_ref,
        *scratch[used:],
    )
    next(amps)
    try:
        amps.send(None)
    except StopIteration:
        pass
    next(blocks, None)


class Wires:
    def __init__(self, send, recv, here):
        self.send, self.recv, self.here = send, recv, here
        self.sends, self.recvs = {}, {}

    def link(self, key, src, dst, peer, out):
        at_send = self.sends.setdefault(out, len(self.sends))
        at_recv = self.recvs.setdefault(key, len(self.recvs))
        return remote(src, dst, self.send.at[at_send], self.recv.at[at_recv], peer)

    def start_in(self, when, key, src, dst, peer, out):
        self.link(key, src, dst, peer, out).start()

    def start(self, key, src, dst, peer, out, when=None):
        def run():
            self.start_in(when, key, src, dst, peer, out)

        if when is None:
            run()
        else:
            pl.when(when)(run)

    def wait(self, key, dst, when=None):
        at_recv = self.recvs.setdefault(key, len(self.recvs))
        copy = remote(dst, dst, self.send.at[0], self.recv.at[at_recv], self.here)
        if when is None:
            copy.wait_recv()
        else:
            pl.when(when)(copy.wait_recv)

    def drain(self, out, whole, when=None):
        at_send = self.sends[out]
        copy = remote(whole, whole, self.send.at[at_send], self.recv.at[0], self.here)
        if when is None:
            copy.wait_send()
        else:
            pl.when(when)(copy.wait_send)


def note(*what):
    return None


def quadrants(
    n, owner_hbm, slot_hbm, fock_hbm, shift_hbm, c_hbm, dom_hbm, start_ref, k_ref, e_hbm, out_ref,
    owner_ref, slot_ref, fock_ref, shift_ref, c_ref, dom_ref, e_ref, src, dom, blocks, bdom, bslot, bfock, wide, turned, x, start, k_own, amps_a, amps_b, amps_c, amps_d,
    acc, yout, yx, ysum, yin, mine, theirs, inverse, send, recv, local,
):
    p, g = lax.axis_index("pairs"), lax.axis_index("grp")
    pc, rows, width = c_ref.shape
    quarter = pc // 4
    half_quarter = quarter // 2
    layers = n // 2
    layer, column = p // 2, p % 2
    inner = (layer % 2 + layer // 2) % 2
    mid, end = inner == 1, inner == 0
    partner = (layer + 1 - 2 * (layer % 2)) * 2 + column
    cross = (layers - 1 - layer) * 2 + column
    far = ((layer + layers // 2) % layers) * 2 + column
    beside = layer * 2 + 1 - column
    groups = (g, g + 1 - 2 * (g % 2), (g + 2) % 4, 3 - g)
    _, mate, across, diagonal = groups
    to_mate, to_across = (p, mate), (p, across)
    to_partner, to_cross, to_beside, to_far = (partner, g), (cross, g), (beside, g), (far, g)
    wires = Wires(send, recv, to_mate)
    amps = ((amps_a, amps_b), (amps_c, amps_d))
    wires.mid = mid

    barrier = pltpu.get_barrier_semaphore()

    def hello(peer):
        pl.semaphore_signal(barrier, inc=1, device_id=peer, device_id_type=MESH)

    for peer in (to_partner, to_beside, to_across, to_mate):
        hello(peer)
    pl.when(mid)(lambda: hello(to_cross))

    pairs = (
        (c_hbm, c_ref), (dom_hbm, dom_ref), (owner_hbm, owner_ref), (slot_hbm, slot_ref),
        (fock_hbm, fock_ref), (shift_hbm, shift_ref), (e_hbm, e_ref), (start_ref, start),
        (k_ref.at[pl.ds(g * quarter, quarter)], k_own),
    )
    loads = [pltpu.make_async_copy(*pair, local.at[i]) for i, pair in enumerate(pairs)]
    for load in loads:
        load.start()
    load_c, load_dom, load_owner, load_slot, load_fock, load_shift, load_e, load_start, load_k = loads
    load_c.wait()
    load_dom.wait()

    def four(group):
        return pl.ds(group * quarter, quarter)

    def two(group, h):
        return pl.ds(group * quarter + h * half_quarter, half_quarter)

    def both_quarters(ref):
        return ref.at[pl.ds(0, 2 * quarter)]

    def three_quarters(ref):
        return ref.at[pl.ds(0, 3 * quarter)]

    def source(b, rel):
        return c_ref if (b, rel) == (0, 0) else src.at[4 * b + rel]

    def turn(rel, b=0):
        for t in range(quarter):
            blocks[b, rel, t] = source(b, rel)[g * quarter + t].T

    for s in range(pc):
        dom[0, s] = dom_ref[pl.ds(s, 1), :]
    turn(0)

    def table(t, carry):
        at_pair = g * quarter + t
        ways = owner_ref.shape[0]
        named = [owner_ref[k, at_pair] for k in range(ways)]
        slots = [slot_ref[k, at_pair] for k in range(ways)]
        focks = [fock_ref[k, at_pair] for k in range(ways)]
        for owner in range(n):
            place, weight = 0, 0.0
            for k in range(ways):
                hit = named[k] == owner
                place = jnp.where(hit, slots[k], place)
                weight = jnp.where(hit, focks[k], weight)
            bslot[0, t, owner] = place
            bfock[0, t, owner] = weight
        return carry

    small = ("slot", "fock", "dom")
    kinds = {
        "slot": lambda b: bslot.at[b],
        "fock": lambda b: bfock.at[b],
        "dom": lambda b: bdom.at[b],
    }
    for rel in range(4):
        for h in (0, 1):
            kinds[rel, h] = functools.partial(
                lambda rel, h, b: blocks.at[b, rel, pl.ds(h * half_quarter, half_quarter)], rel, h
            )
        kinds[rel] = functools.partial(lambda rel, b: blocks.at[b, rel], rel)

    def tag(kind):
        return kind if kind in small else "targets"

    def landing(kind):
        return kind if kind in small or kind in ((3, 0), (3, 1)) else 0

    def ready(kind):
        ref = kinds[kind](0)
        onward, across_cut = kinds[kind](4), kinds[kind](2)
        if kind in ("slot", "fock"):
            wires.start(("second", kind), ref, kinds[kind](1), to_partner, kind)
        wires.start(("beside", 0 if tag(kind) == "targets" else kind), ref, onward, to_beside, tag(kind), end)
        wires.start(("cross", kind), ref, across_cut, to_cross, tag(kind), mid)

    def next_ready(kind):
        ref = kinds[kind](1)
        onward, across_cut = kinds[kind](5), kinds[kind](3)
        if kind in ("slot", "fock"):
            wires.wait(("second", kind), ref)
        wires.start(("beside2", landing(kind)), ref, onward, to_beside, tag(kind), end)
        wires.start(("further", kind), ref, across_cut, to_cross, tag(kind), mid)

    def got_first(kind):
        landed, passed = kinds[kind](2), kinds[kind](4)

        def relay():
            wires.wait(("cross", kind), landed)
            key = ("beside", 0 if tag(kind) == "targets" else kind)
            wires.start_in(mid, key, landed, passed, to_beside, tag(kind))

        pl.when(mid)(relay)

    def got_further(kind):
        landed, passed = kinds[kind](3), kinds[kind](5)

        def relay():
            wires.wait(("further", kind), landed)
            wires.start_in(mid, ("beside2", landing(kind)), landed, passed, to_beside, tag(kind))

        pl.when(mid)(relay)

    def got_beside():
        for kind in small:
            wires.wait(("beside", kind), kinds[kind](4))
        wires.wait(("beside", 0), blocks.at[4])

    def got_beside2():
        for kind in small:
            wires.wait(("beside2", kind), kinds[kind](5))
        wires.wait(("beside2", 0), blocks.at[5, pl.ds(0, 3)])

    first, second = 2 * inner, 1 + 2 * inner
    places_of = (first, 4, second, 5)

    lines = lax.broadcasted_iota(jnp.int16, (NB, rows), 0)
    lines2 = lax.broadcasted_iota(jnp.int16, (2 * NB, 2 * rows), 0)

    def one_hot(numbers, row):
        hit = numbers == row.astype(jnp.int16)
        return jnp.where(hit, jnp.ones(hit.shape, BF16), jnp.zeros(hit.shape, BF16))

    def expand(b, rel, parts=(0, 1, 2, 3)):
        base = groups[rel] * NB
        block = source(b, rel)

        def one(s, carry):
            hit = one_hot(lines, dom[4 * b + rel, s] - base)
            wide[b, s, pl.ds(rel * NB, NB)] = jnp.dot(
                hit, block[s], preferred_element_type=F32
            ).astype(BF16)
            return carry

        if len(parts) == 4:
            note("expand", b, rel)
            lax.fori_loop(0, pc, one, 0, unroll=8)
            return
        for i in parts:
            note("expand4", b, rel)
            for t in range(quarter):
                one(groups[i] * quarter + t, 0)

    every = tuple(range(quarter))
    early, later = every[:half_quarter], every[half_quarter:]

    def make_turned(b, hs=(0, 1), ts=every):
        note("make_turned", b, 0, len(hs) * len(ts) / 8)
        place = places_of[b]

        def one(t, carry):
            for h in hs:
                u, v = 2 * h, 2 * h + 1
                row = jnp.concatenate(
                    [
                        bdom[place, u * quarter + t] - groups[u] * NB,
                        bdom[place, v * quarter + t] - groups[v] * NB + NB,
                    ],
                    axis=1,
                )
                hit = one_hot(lines2, row)
                both = jnp.concatenate([blocks[place, u, t], blocks[place, v, t]], axis=1)
                turned[b, t, :, pl.ds(h * 2 * NB, 2 * NB)] = lax.dot_general(
                    both, hit, (((1,), (1,)), ((), ())), preferred_element_type=F32
                ).astype(BF16)
            return carry

        if ts == every:
            lax.fori_loop(0, quarter, one, 0, unroll=2)
        else:
            for t in ts:
                one(t, 0)

    owners = (p, partner)

    def make_x(b, s, ts=every):
        note("make_x", b, s, len(ts) / 4)
        place = places_of[b]

        def one(t, carry):
            at_source = bslot[place, t, owners[s]]
            x[b, t, s] = jnp.dot(
                turned[b, t], wide[s, at_source], preferred_element_type=F32
            ).astype(BF16)
            return carry

        for t in ts:
            one(t, 0)

    def couple(b, s, it, ts=every):
        note("couple", b, s, len(ts) / 4)
        place = places_of[b]
        found = []
        for t in ts:
            at_source = bslot[place, t, owners[s]]
            xs = x[b, t, s]
            half = jnp.dot(xs, amps[it][s][at_source], preferred_element_type=F32).astype(BF16)
            found.append((t, xs, half))
        for t, xs, half in found:
            y = lax.dot_general(half, xs, (((1,), (1,)), ((), ())), preferred_element_type=F32)
            y = bfock[place, t, owners[s]] * y
            if s == 0:
                acc[b, t] = y
            elif b % 2 == 0:
                acc[b, t] += y
            else:
                yout[it, b // 2, t] = (acc[b, t] + y).astype(BF16)

    def post(it, m, ts=every):
        for t in ts:
            wires.start(("y", it, m, t), yout.at[it, m, t], yx.at[it, m, t], to_beside, "y")

    def share(t):
        at_pair = g * quarter + t
        ref = amps[1][0].at[at_pair]
        wires.start(("own", 1, t), ref, ref, to_across, "amps")
        wires.start(("own", 2), ref, ref, to_mate, "amps")

    def share_partner(t, when):
        at_pair = g * quarter + t
        wires.start(("a", 1, 0, t), amps[1][0].at[at_pair], amps[1][1].at[at_pair], to_partner, "amps", when)

    def pass_partner(t):
        ref = amps[1][1].at[g * quarter + t]
        wires.wait(("a", 1, 0, t), ref)
        wires.start(("a", 1, 1, t), ref, ref, to_across, "amps")
        wires.start(("a", 1, 2), ref, ref, to_mate, "amps")

    def pass_own(t):
        ref = amps[1][0].at[across * quarter + t]
        wires.wait(("own", 1, t), ref)
        wires.start(("own", 2), ref, ref, to_mate, "amps")

    def pass_across(t):
        ref = amps[1][1].at[across * quarter + t]
        wires.wait(("a", 1, 1, t), ref)
        wires.start(("a", 1, 2), ref, ref, to_mate, "amps")

    def share_start(j):
        part = four((g, across)[j])
        wires.start(("start", j), amps[0][0].at[part], amps[0][1].at[part], to_partner, "amps")

    def pass_start(j):
        ref = amps[0][1].at[four((g, across)[j])]
        wires.wait(("start", j), ref)
        wires.start(("a", 0, 2), ref, ref, to_mate, "amps")

    def have_partner(it):
        wires.wait(("a", it, 2), both_quarters(amps[it][1]))

    def sum_second(it, ts=every):
        for t in ts:
            wires.wait(("y", it, 1, t), yx.at[it, 1, t])
            ysum[it, 1, t] = (acc[2, t] + yx[it, 1, t].astype(F32)).astype(BF16)
            job = (("yfar", it, t), ysum.at[it, 1, t], yin.at[it, 0, t])
            wires.start(*job, to_partner, "yfar", end)
            wires.start(*job, to_far, "yfar", mid)

    def sum_first(it, ts=every):
        for t in ts:
            wires.wait(("y", it, 0, t), yx.at[it, 0, t])
            total = acc[0, t] + yx[it, 0, t].astype(F32)
            acc[0, t] = total
            ysum[it, 0, t] = total.astype(BF16)
            wires.start(("ynear", it, t), ysum.at[it, 0, t], yin.at[it, 1, t], to_cross, "ynear", mid)

    def coupled(it, t):
        wires.wait(("ynear", it, t), yin.at[it, 1, t], mid)
        wires.wait(("yfar", it, t), yin.at[it, 0, t])
        near = yin[it, 1, t].astype(F32)
        return yin[it, 0, t].astype(F32) + jnp.where(mid, near, acc[0, t])

    def invert(t, carry):
        at_pair = g * quarter + t
        row = jnp.broadcast_to(e_ref[pl.ds(at_pair, 1), :], (width, width))
        over = 1.0 / (row.T + row + shift_ref[at_pair])
        inverse[t] = over
        k_own[t] = k_own[t] * over
        return carry

    def updated(it, t):
        return (-(k_own[t] + coupled(it, t) * inverse[t])).astype(BF16)

    swap_mate, swap_across = (1, 0, 3, 2), (2, 3, 0, 1)

    def from_mate():
        wires.wait(("own mate", 1), src.at[1, four(g)])

    def from_mate_rest():
        wires.wait(("own mate", 0), three_quarters(src.at[1]))

    def from_across(i):
        part = four(groups[i])
        wires.wait(("own across", swap_across[i]), src.at[2, part])
        wires.start(
            ("own corner", int(i == 1)), src.at[2, part], src.at[3, part], to_mate,
            "rows",
        )

    def from_corner():
        wires.wait(("own corner", 1), src.at[3, four(g)])

    def from_corner_rest():
        wires.wait(("own corner", 0), three_quarters(src.at[3]))

    def to_next(i):
        part = four(groups[i])
        wires.start(
            ("next", i), c_ref.at[part], src.at[4, part], to_partner, "rows"
        )

    def from_next(i):
        part = four(groups[i])
        ref = src.at[4, part]
        wires.wait(("next", i), ref)
        if i > 0:
            wires.start(
                ("next across", i), ref, src.at[6, part], to_across, "rows",
            )
        wires.start(
            ("next mate", int(i == 1)), ref, src.at[5, part], to_mate, "rows",
        )

    def to_wide(i):
        part = four(groups[i])
        wires.start(
            ("next wide", i), src.at[2, part], src.at[6, part], to_partner, "rows",
        )

    def corner(i):
        part = four(groups[i])
        wires.start(
            ("next corner", int(i == 1)), src.at[6, part], src.at[7, part], to_mate, "rows",
        )

    def from_next_across(i):
        wires.wait(("next across", swap_across[i]), src.at[6, four(groups[i])])
        corner(i)

    def from_wide(i):
        wires.wait(("next wide", i), src.at[6, four(groups[i])])
        corner(i)

    def from_next_mate():
        wires.wait(("next mate", 1), src.at[5, four(g)])

    def from_next_mate_rest():
        wires.wait(("next mate", 0), three_quarters(src.at[5]))

    def from_next_corner():
        wires.wait(("next corner", 1), src.at[7, four(g)])

    def from_next_corner_rest():
        wires.wait(("next corner", 0), three_quarters(src.at[7]))

    def own_across(i):
        part = four(groups[i])
        wires.start(
            ("own across", i), c_ref.at[part], src.at[2, part], to_across, "rows",
        )

    def cast(s, carry):
        amps[0][0][s] = start[s].astype(BF16)
        return carry

    pl.semaphore_wait(barrier, 4 + inner)
    wires.start(("d", 1), dom.at[0], dom.at[1], to_mate, "doms")
    wires.start(("d", 2), dom.at[0], dom.at[2], to_across, "doms")
    own_across(2)
    to_next(0)
    ready((0, 0))
    ready((0, 1))
    for i in (1, 0, 2, 3):
        part = four(groups[i])
        wires.start(
            ("own mate", int(i == 1)), c_ref.at[part], src.at[1, part], to_mate, "rows",
        )
    own_across(3)
    own_across(0)
    to_next(2)
    from_mate()
    turn(1)
    ready((1, 0))
    ready((1, 1))
    wires.wait(("d", 1), dom.at[1])
    wires.wait(("d", 2), dom.at[2])
    wires.start(("d", 3), dom.at[2], dom.at[3], to_mate, "doms")
    for load in (load_owner, load_slot, load_fock):
        load.wait()
    lax.fori_loop(0, quarter, table, 0)
    ready("slot")
    ready("fock")
    wires.wait(("d", 3), dom.at[3])
    wires.start(("d", 4), dom.at[pl.ds(0, 4)], dom.at[pl.ds(4, 4)], to_partner, "doms")
    to_next(3)
    to_next(1)
    for rel in range(4):
        for t in range(quarter):
            bdom[0, rel * quarter + t] = dom[rel, g * quarter + t]
    ready("dom")
    got_first((0, 0))
    expand(0, 0)
    from_next(0)
    turn(0, 1)
    next_ready((0, 0))
    next_ready((0, 1))
    got_first((0, 1))
    from_across(0)
    turn(2)
    ready((2, 0))
    ready((2, 1))
    from_mate_rest()
    got_first((1, 0))
    expand(0, 1)
    from_next(2)
    got_first((1, 1))
    expand(0, 2, (0,))
    from_across(1)
    got_further((0, 0))
    from_corner()
    turn(3)
    ready((3, 0))
    ready((3, 1))
    load_start.wait()
    lax.fori_loop(0, pc, cast, 0, unroll=2)
    for load in (load_k, load_e, load_shift):
        load.wait()
    wires.wait(("d", 4), dom.at[pl.ds(4, 4)])
    expand(0, 2, (1,))
    from_across(2)
    to_wide(2)
    share_start(0)
    share_start(1)
    got_further((0, 1))
    expand(1, 0, (0, 2))
    from_next(3)
    own_across(1)
    expand(0, 2, (2,))
    got_first((2, 0))
    expand(1, 0, (3,))
    for rel in range(4):
        for t in range(quarter):
            bdom[1, rel * quarter + t] = dom[4 + rel, g * quarter + t]
    next_ready("dom")
    next_ready("slot")
    next_ready("fock")
    from_next_across(0)
    turn(2, 1)
    next_ready((2, 0))
    next_ready((2, 1))
    got_first((2, 1))
    from_next(1)
    expand(1, 0, (1,))
    got_first((3, 0))
    from_next_mate()
    turn(1, 1)
    next_ready((1, 0))
    next_ready((1, 1))
    from_next_mate_rest()
    expand(1, 1, (0, 1))
    from_next_across(1)
    got_first((3, 1))
    expand(1, 1, (2, 3))
    from_next_corner()
    turn(3, 1)
    next_ready((3, 0))
    next_ready((3, 1))
    for kind in small:
        got_first(kind)
    from_wide(2)
    got_further((2, 0))
    lax.fori_loop(0, half_quarter, invert, 0)
    expand(1, 2, (0, 1))
    from_across(3)
    got_further((2, 1))
    expand(1, 2, (2,))
    expand(0, 2, (3,))
    from_corner_rest()
    expand(0, 3, (0, 1))
    got_further((1, 0))
    expand(0, 3, (2, 3))
    make_turned(0)
    pass_start(0)
    got_further((1, 1))
    lax.fori_loop(half_quarter, quarter, invert, 0)
    from_next_across(3)
    make_x(0, 0)
    expand(1, 2, (3,))
    pass_start(1)
    for kind in small:
        got_further(kind)
    from_next_corner_rest()
    expand(1, 3)
    got_further((3, 0))
    got_beside()
    make_turned(1)
    make_x(1, 0)
    make_x(1, 1)
    have_partner(0)
    got_further((3, 1))
    couple(1, 0, 0)
    couple(1, 1, 0)
    post(0, 0, early)
    make_turned(2)
    make_x(2, 0)
    make_x(2, 1)
    couple(2, 0, 0)
    couple(2, 1, 0)
    got_beside2()
    make_turned(3, (0,))
    for h, ts in ((0, early), (1, later)):
        wires.wait(("beside2", (3, h)), kinds[3, h](5))
        make_turned(3, (1,), ts)
        make_x(3, 0, ts)
        make_x(3, 1, ts)
        couple(3, 0, 0, ts)
        couple(3, 1, 0, ts)
        post(0, 1, ts)
    post(0, 0, later)
    make_x(0, 1)
    couple(0, 0, 0)
    couple(0, 1, 0)
    sum_first(0, early)
    sum_second(0)
    sum_first(0, later)

    for t in range(quarter):
        amps[1][0][g * quarter + t] = updated(0, t)
        share_partner(t, None)
        share(t)
    for t in range(quarter):
        pass_partner(t)
        pass_own(t)
    wires.wait(("own", 2), both_quarters(amps[1][0]))
    couple(3, 0, 1)
    couple(1, 0, 1)
    for t in range(half_quarter):
        pass_across(t)
    couple(2, 0, 1)
    couple(0, 0, 1)
    for t in range(half_quarter, quarter):
        pass_across(t)
    have_partner(1)
    for ts in (early, later):
        for b in (3, 1):
            couple(b, 1, 1, ts)
            post(1, b // 2, ts)
    couple(2, 1, 1)
    couple(0, 1, 1)
    sum_second(1, early)
    sum_first(1, early)
    sum_second(1, later)
    sum_first(1, later)

    for t in range(quarter):
        mine[t] = coupled(1, t).astype(BF16)
        part = mine.at[t]
        wires.start(("out", 1, t), part, theirs.at[t], to_across, "amps")
        wires.start(("out", 2), part, out_ref.at[g * quarter + t], to_mate, "out")
    keep_mine = pltpu.make_async_copy(mine, out_ref.at[four(g)], local.at[9])
    keep_mine.start()
    for t in range(quarter):
        ref = theirs.at[t]
        wires.wait(("out", 1, t), ref)
        wires.start(("out", 2), ref, out_ref.at[across * quarter + t], to_mate, "out")
    keep_theirs = pltpu.make_async_copy(theirs, out_ref.at[four(across)], local.at[10])
    keep_theirs.start()
    wires.drain("rows", src.at[pl.ds(0, 7)])
    wires.drain("doms", dom.at[pl.ds(0, 7)])
    for role, passes in ((end, 2), (mid, 4)):
        wires.drain("targets", blocks.at[pl.ds(0, passes)], role)
        wires.drain("dom", bdom.at[pl.ds(0, passes)], role)
        wires.drain("slot", bslot.at[pl.ds(0, passes + 1)], role)
        wires.drain("fock", bfock.at[pl.ds(0, passes + 1)], role)
    wires.drain("y", yout)
    wires.drain("yfar", ysum.at[0])
    wires.drain("ynear", ysum.at[0], mid)
    wires.drain("amps", src.at[pl.ds(0, 3)])
    wires.drain("out", both_quarters(amps[1][0]))
    wires.wait(("out", 2), both_quarters(out_ref))
    keep_mine.wait()
    keep_theirs.wait()
    assert len(wires.sends) <= SENDS and len(wires.recvs) <= RECVS, (len(wires.sends), len(wires.recvs))


SENDS, RECVS = 11, 112


def quadrants_fit(n, groups, pc, rows, width):
    return n == 2 * groups and groups == 4 and pc % (2 * groups) == 0 and rows == width


def quadrants_kernel(n, *refs):
    quadrants(n, *refs)


def quadrants_call(
    n, owner, slot, fock, shift, coefficients, domain, start, integrals, energy
):
    pc, rows, width = coefficients.shape
    quarter = pc // 4
    big, ways = (width, width), owner.shape[1]
    hbm = pl.BlockSpec(memory_space=pl.ANY)
    dma = pltpu.SemaphoreType.DMA
    total = pl.pallas_call(
        functools.partial(quadrants_kernel, n),
        out_shape=jax.ShapeDtypeStruct((pc, *big), BF16),
        in_specs=[hbm] * 9,
        out_specs=hbm,
        scratch_shapes=[
            pltpu.SMEM((ways, pc), jnp.int32), pltpu.SMEM((ways, pc), jnp.int32),
            pltpu.SMEM((ways, pc), F32), pltpu.SMEM((pc,), F32),
            pltpu.VMEM((pc, rows, width), BF16), pltpu.VMEM((pc, rows), jnp.int32),
            pltpu.VMEM((pc, width), F32),
            pltpu.VMEM((8, pc, rows, width), BF16),
            pltpu.VMEM((8, pc, 1, rows), jnp.int32),
            pltpu.VMEM((6, 4, quarter, width, rows), BF16),
            pltpu.VMEM((6, 4 * quarter, 1, rows), jnp.int32),
            pltpu.SMEM((6, quarter, n), jnp.int32),
            pltpu.SMEM((6, quarter, n), F32),
            pltpu.VMEM((2, pc, 4 * NB, width), BF16),
            pltpu.VMEM((4, quarter, width, 4 * NB), BF16),
            pltpu.VMEM((4, quarter, 2, *big), BF16),
            pltpu.VMEM((pc, *big), F32),
            pltpu.VMEM((quarter, *big), F32),
            *[pltpu.VMEM((pc, *big), BF16)] * 4,
            pltpu.VMEM((4, quarter, *big), F32),
            pltpu.VMEM((2, 2, quarter, *big), BF16),
            pltpu.VMEM((2, 2, quarter, *big), BF16),
            pltpu.VMEM((2, 2, quarter, *big), BF16),
            pltpu.VMEM((2, 2, quarter, *big), BF16),
            pltpu.VMEM((quarter, *big), BF16), pltpu.VMEM((quarter, *big), BF16),
            pltpu.VMEM((quarter, *big), F32),
            dma((SENDS,)), dma((RECVS,)), dma((11,)),
        ],
        compiler_params=pltpu.CompilerParams(
            collective_id=0, has_side_effects=True, vmem_limit_bytes=60 * 2**20
        ),
        name="quadrants",
    )(owner.T, slot.T, fock.T, shift, coefficients, domain, start, integrals, energy)
    denominator = energy[:, :, None] + energy[:, None, :] + shift[:, None, None]
    return -(integrals + total.astype(F32)) / denominator


def on_device(
    coefficients, domain, coupling_owner, coupling_slot, coupling_fock,
    exchange_integrals, pno_energy, pair_shift, amplitudes_start,
):
    n = lax.axis_size("pairs")
    pc, rows, width = coefficients.shape
    quarter = pc // lax.axis_size("grp")
    steps = n // 2
    named = coupling_owner[:, :, None] == jnp.arange(n, dtype=jnp.int32)[None, None, :]
    slots = jnp.sum(jnp.where(named, coupling_slot[:, :, None], 0), axis=1)
    focks = jnp.sum(jnp.where(named, coupling_fock[:, :, None], 0.0), axis=1)
    focks = jnp.concatenate([focks, pair_shift[:, None]], axis=1)
    vmem, smem = pl.BlockSpec(memory_space=pltpu.VMEM), pl.BlockSpec(memory_space=pltpu.SMEM)
    dma = pltpu.SemaphoreType.DMA

    def params(collective):
        return pltpu.CompilerParams(
            collective_id=collective, has_side_effects=True, vmem_limit_bytes=60 * 2**20
        )

    if quadrants_fit(n, lax.axis_size("grp"), pc, rows, width):
        return quadrants_call(
            n, coupling_owner, coupling_slot, coupling_fock, pair_shift, coefficients, domain,
            amplitudes_start, exchange_integrals, pno_energy,
        )

    big = (width, width)
    x_shape = jax.ShapeDtypeStruct((n, quarter, *big), BF16)
    block_scratch = [
        pltpu.VMEM((n, pc, rows, width), BF16),
        pltpu.VMEM((n, pc, rows), jnp.int32),
        pltpu.VMEM((pc, width, NB), BF16),
        pltpu.VMEM((pc, NB, width), BF16),
        pltpu.VMEM((2, 2 * quarter, *big), F32),
        pltpu.VMEM((2, 2 * quarter, *big), F32),
        pltpu.VMEM((n, 2 * quarter, *big), F32),
        pltpu.VMEM((2, quarter, *big), F32),
        pltpu.VMEM((n, quarter, *big), F32),
        pltpu.VMEM((n, quarter, *big), F32),
        dma((2, steps, 3)), dma((2, steps, 3)),
        dma((n,)), dma((n,)), dma((n,)), dma((n,)),
    ]
    amp_scratch = [
        pltpu.VMEM((n * pc, *big), BF16),
        pltpu.VMEM((pc, *big), BF16),
        pltpu.VMEM((quarter, *big), F32),
        pltpu.VMEM((quarter, *big), BF16),
        dma((2, steps, 4)), dma((2, steps, 4)),
        dma((n, 4)), dma((n, 4)), dma((n + 1,)), dma((n + 1,)), dma((3,)), dma((3,)),
    ]
    half_shape = jax.ShapeDtypeStruct((quarter, *big), BF16)

    def iterate(first, start, x):
        return pl.pallas_call(
            functools.partial(iteration_alone, n, first),
            out_shape=half_shape if first else jax.ShapeDtypeStruct((pc, *big), BF16),
            in_specs=[smem, smem, vmem, vmem, vmem, vmem],
            out_specs=vmem,
            scratch_shapes=amp_scratch,
            compiler_params=params(1 if first else 2),
            name="first" if first else "second",
        )(slots, focks, start, x, exchange_integrals, pno_energy)

    held = n * width * (2 * pc * (rows + width) + 4 * width * 4 * quarter + 2 * width * quarter)
    if held < 40 * 2**20:
        return pl.pallas_call(
            functools.partial(opening, n, len(block_scratch)),
            out_shape=jax.ShapeDtypeStruct((pc, *big), BF16),
            in_specs=[smem, smem, vmem, vmem, vmem, vmem, vmem],
            out_specs=vmem,
            scratch_shapes=[
                pltpu.VMEM(x_shape.shape, BF16), pltpu.VMEM(half_shape.shape, BF16),
                *block_scratch, *amp_scratch, *amp_scratch,
            ],
            compiler_params=params(0),
            name="amplitudes",
        )(slots, focks, coefficients, domain, amplitudes_start, exchange_integrals, pno_energy).astype(F32)
    else:
        x = pl.pallas_call(
            functools.partial(intersections_alone, n),
            out_shape=x_shape,
            in_specs=[smem, vmem, vmem],
            out_specs=vmem,
            scratch_shapes=block_scratch,
            compiler_params=params(0),
            name="intersections",
        )(slots, coefficients, domain)
        amps = iterate(True, amplitudes_start, x)
    return iterate(False, amps, x).astype(F32)


def solution(mesh):
    placed = (
        P("pairs", "grp", None),
        P("pairs", "grp"),
        P("pairs", None),
        P("pairs", None),
        P("pairs", None),
        P("pairs", None, None),
        P("pairs", None),
        P("pairs"),
        P("pairs", None, None),
    )
    return jax.shard_map(
        on_device, mesh=mesh, in_specs=placed, out_specs=P("pairs", None, None), check_vma=False
    )
```
